256 devices in a mesh: rows: 64 (over z, y, core), grp: 4 (over x).
Axes of the slice: x: 4, y: 4, z: 8, core: 2. Of those that a mesh axis runs over, the one named last changes fastest.
Arguments:
- a_diag: bfloat16 [512, 12, 128, 128], P('rows', 'grp'), may hold values from -1.25 to 1.25
- diag_cols: int32 [512, 12], P('rows', 'grp'), may hold values from 0 to 7
- a_offd: bfloat16 [512, 12, 128, 128], P('rows', 'grp'), may hold values from -1.25 to 1.25
- offd_cols: int32 [512, 12], P('rows', 'grp'), may hold values from 0 to 255, as said below
- prolong: bfloat16 [512, 2, 128, 128], P('rows'), may hold values from -0.5 to 0.5
- aggregate: int32 [512, 2], P('rows'), may hold values from 0 to 1, as said below
- send_rows: int32 [64, 64, 4], P('rows'), may hold values from 0 to 8, as said below
- ghost_agg: int32 [64, 64, 4, 2], P('rows'), may hold values from 0 to 1, as said below
- coarse_map: int32 [64, 98], P('rows'), may hold values from 0 to 127, as said below
Outputs:
- coarse: bfloat16 [128, 98, 128, 128], P('rows', None, 'grp')
The draws below stay inside these ranges and needn't reach their ends.
Inputs may be any that keep to these rules, and one draw needn't show every extreme that they name: `send_rows`: for owner s and receiving node n, the block rows of s (0 to 7 within s) in the 4 slots of n; 8 marks an empty slot. A node receives from exactly 48 other nodes and never from itself; from each of them 4 - 1 to 4 distinct rows in the first slots, and 4 rows from at least one of them. `ghost_agg`: the aggregate entry of the sender's block row for each received tile; 0 in empty slots. `coarse_map`: distinct for each node, and holding every coarse id that a right factor of that node's products has. `aggregate`: distinct within a block row. `offd_cols`: always a filled slot of the node's received rows.
All inputs are finite; a program needn't handle non-finite values.
Results may differ from the reference program's by a relative error of at most 0.0049.
Values may be sent and summed in bfloat16 or wider, within the bound.
A program may use at most 128 MiB of HBM per device.

```python
import jax
import jax.numpy as jnp
from jax import lax

TILE = 128
BR = 8
CR1 = 2
KP = 2
CAP = 4
NODES = 64
NPEER = 48
KD = 12
KO = 12
NB = 512
NC = 128
KC = 98


def build_pattern(key):
    key_list = jax.random.split(jax.random.fold_in(key, 11), 7)
    node_ids = jnp.arange(NODES, dtype=jnp.int32)
    offsets = jax.vmap(lambda subkey: jax.random.permutation(subkey, NODES - 1))(jax.random.split(key_list[0], NODES))[:, :NPEER] + 1
    peer_nodes = ((node_ids[:, None] + offsets) % NODES).astype(jnp.int32)
    counts = jax.random.randint(key_list[1], (NODES, NPEER), CAP - 1, CAP + 1).at[:, 0].set(CAP)
    picked = jax.vmap(lambda subkey: jax.random.permutation(subkey, BR)[:CAP])(jax.random.split(key_list[2], NODES * NPEER)).reshape(NODES, NPEER, CAP)
    slot_ids = jnp.arange(CAP, dtype=jnp.int32)
    filled = slot_ids[None, None, :] < counts[:, :, None]
    dest_idx = jnp.broadcast_to(node_ids[:, None, None], (NODES, NPEER, CAP))
    src_idx = jnp.broadcast_to(peer_nodes[:, :, None], (NODES, NPEER, CAP))
    cap_idx = jnp.broadcast_to(slot_ids[None, None, :], (NODES, NPEER, CAP))
    received = jnp.full((NODES, NODES, CAP), BR, jnp.int32)
    received = received.at[dest_idx, src_idx, cap_idx].set(jnp.where(filled, picked, BR).astype(jnp.int32))
    aggregate = jax.vmap(lambda subkey: jax.random.permutation(subkey, CR1)[:KP])(jax.random.split(key_list[3], NB)).astype(jnp.int32)
    safe_rows = jnp.minimum(received, BR - 1)
    owner_rows = node_ids[None, :, None] * BR + safe_rows
    ghost_agg = jnp.where((received < BR)[..., None], aggregate[owner_rows], 0).astype(jnp.int32)
    local_ids = node_ids[:, None] * CR1 + jnp.arange(CR1, dtype=jnp.int32)[None, :]
    peer_ids = (peer_nodes[:, :, None] * CR1 + jnp.arange(CR1, dtype=jnp.int32)[None, None, :]).reshape(NODES, NPEER * CR1)
    listed = jnp.concatenate([local_ids, peer_ids], axis=1)
    slot_order = jax.vmap(lambda subkey: jax.random.permutation(subkey, KC))(jax.random.split(key_list[4], NODES))
    coarse_map = jnp.take_along_axis(listed, slot_order, axis=1).astype(jnp.int32)
    diag_cols = jax.random.randint(key_list[5], (NB, KD), 0, BR).astype(jnp.int32)
    is_filled = (received < BR).reshape(NODES, NODES * CAP).astype(jnp.int32)
    running = jnp.cumsum(is_filled, axis=1)
    used_count = running[:, -1]
    sampled = jax.random.randint(key_list[6], (NODES, BR * KO), 0, used_count[:, None])
    offd_flat = jnp.sum((running[:, None, :] <= sampled[:, :, None]).astype(jnp.int32), axis=2)
    offd_cols = offd_flat.reshape(NB, KO).astype(jnp.int32)
    return (received, aggregate, ghost_agg, coarse_map, diag_cols, offd_cols)


def draw_send_rows(key, part):
    return jnp.transpose(build_pattern(key)[0], (1, 0, 2))


def draw_aggregate(key, part):
    return build_pattern(key)[1]


def draw_ghost_agg(key, part):
    return build_pattern(key)[2]


def draw_coarse_map(key, part):
    return build_pattern(key)[3]


def draw_diag_cols(key, part):
    return build_pattern(key)[4]


def draw_offd_cols(key, part):
    return build_pattern(key)[5]


def steps_of(key, shape, pieces, smallest, top_value):
    level, own = 1.0, jax.random.fold_in(key, 6)
    for axis_at, parts in pieces:
        heights = jnp.exp(jax.random.uniform(jax.random.fold_in(own, axis_at), (parts,), jnp.float32, smallest / len(pieces), top_value / len(pieces)))
        level = level * jnp.repeat(heights, shape[axis_at] // parts).reshape([-1 if axis == axis_at else 1 for axis in range(len(shape))])
    return level


def centred(stream_key, shape, scale, limit, pieces=(), held_as=jnp.bfloat16):
    gain = steps_of(stream_key, shape, pieces, -0.22, 0.18) if pieces else 1.0
    array = jax.random.normal(stream_key, shape, jnp.float32) * scale * gain
    return jnp.minimum(jnp.maximum(array, -limit), limit).astype(held_as)


def setup_inputs(seed: int = 0) -> dict:
    arg_keys = jax.random.split(jax.random.key(seed), 10)
    a_diag = centred(arg_keys[0], (NB, KD, TILE, TILE), (KD + KO) ** -0.5, 1.25, ((0, 64), (1, 4)))
    diag_cols = draw_diag_cols(jax.random.fold_in(arg_keys[9], 71), 0)
    a_offd = centred(arg_keys[2], (NB, KO, TILE, TILE), (KD + KO) ** -0.5, 1.25, ((0, 64), (1, 4)))
    offd_cols = draw_offd_cols(jax.random.fold_in(arg_keys[9], 71), 0)
    prolong = centred(arg_keys[4], (NB, KP, TILE, TILE), TILE ** -0.5, 0.5, ((0, 64),))
    aggregate = draw_aggregate(jax.random.fold_in(arg_keys[9], 71), 0)
    send_rows = draw_send_rows(jax.random.fold_in(arg_keys[9], 71), 0)
    ghost_agg = draw_ghost_agg(jax.random.fold_in(arg_keys[9], 71), 0)
    coarse_map = draw_coarse_map(jax.random.fold_in(arg_keys[9], 71), 0)
    return {"a_diag": a_diag, "diag_cols": diag_cols, "a_offd": a_offd, "offd_cols": offd_cols, "prolong": prolong, "aggregate": aggregate, "send_rows": send_rows, "ghost_agg": ghost_agg, "coarse_map": coarse_map}


def slot_of(global_ids, col_map):
    positions = jnp.arange(col_map.shape[0], dtype=jnp.int32)
    return jnp.sum(jnp.where(global_ids[..., None] == col_map, positions, 0), axis=-1).astype(jnp.int32)


def galerkin_terms(running, a_tiles, right_tiles, slot_ids, left_tiles, targets):
    top_precision = lax.Precision.HIGHEST
    products_ab = jnp.einsum("rkab,rkjbc->rkjac", a_tiles.astype(jnp.float32), right_tiles.astype(jnp.float32), precision=top_precision).astype(jnp.bfloat16)
    galerkin_part = jnp.einsum("riaq,rkjac->rkijqc", left_tiles.astype(jnp.float32), products_ab.astype(jnp.float32), precision=top_precision)
    index_shape = galerkin_part.shape[:4]
    rows_idx = jnp.broadcast_to(targets[:, None, :, None], index_shape)
    cols_idx = jnp.broadcast_to(slot_ids[:, :, None, :], index_shape)
    return running.at[rows_idx, cols_idx].add(galerkin_part)


def reference(a_diag, diag_cols, a_offd, offd_cols, prolong, aggregate, send_rows, ghost_agg, coarse_map):
    tile_size = prolong.shape[2]
    padded = jnp.concatenate([prolong.reshape(NODES, BR, KP, tile_size, tile_size), jnp.zeros((NODES, 1, KP, tile_size, tile_size), prolong.dtype)], axis=1)
    sender_ids = jnp.arange(NODES, dtype=jnp.int32)

    def one_node(node_index):
        start = (node_index * BR).astype(jnp.int32)
        own_rows = lax.dynamic_slice_in_dim(prolong, start, BR, 0)
        own_agg = lax.dynamic_slice_in_dim(aggregate, start, BR, 0)
        diag_tiles = lax.dynamic_slice_in_dim(a_diag, start, BR, 0)
        diag_here = lax.dynamic_slice_in_dim(diag_cols, start, BR, 0)
        offd_tiles = lax.dynamic_slice_in_dim(a_offd, start, BR, 0)
        offd_here = lax.dynamic_slice_in_dim(offd_cols, start, BR, 0)
        rows_from = send_rows[:, node_index, :]
        ghosts = padded[sender_ids[:, None], rows_from].reshape(NODES * CAP, KP, tile_size, tile_size)
        col_map = coarse_map[node_index]
        ghost_ids = sender_ids[:, None, None] * CR1 + ghost_agg[node_index]
        ghost_slots = slot_of(ghost_ids, col_map).reshape(NODES * CAP, KP)
        own_slots = slot_of(node_index * CR1 + own_agg, col_map)
        running = jnp.zeros((CR1, KC, tile_size, tile_size), jnp.float32)
        running = galerkin_terms(running, diag_tiles, own_rows[diag_here], own_slots[diag_here], own_rows, own_agg)
        running = galerkin_terms(running, offd_tiles, ghosts[offd_here], ghost_slots[offd_here], own_rows, own_agg)
        return running.astype(jnp.bfloat16)

    stacked = lax.map(one_node, sender_ids)
    return stacked.reshape(NC, KC, tile_size, tile_size)
```

```python
import functools

import jax
import jax.numpy as jnp
from jax import lax
from jax.experimental import pallas as pl
from jax.experimental.pallas import tpu as pltpu
from jax.sharding import PartitionSpec as P

CR1 = 2
T = 128
H = T // 2


def ordered_tiles(prolong, aggregate):
    first = (aggregate[:, 0] == 0)[:, None, None]
    zero = jnp.where(first, prolong[:, 0], prolong[:, 1])
    one = jnp.where(first, prolong[:, 1], prolong[:, 0])
    return jnp.concatenate([zero, one], axis=-1)


def left_kernel(a_ref, p_ref, l_ref):
    left = p_ref[0].T
    groups, _, per, _, _ = a_ref.shape
    for g in range(groups):
        for k in range(per):
            l_ref[0, g * per + k] = jnp.dot(
                left, a_ref[g, 0, k], preferred_element_type=jnp.float32
            ).astype(l_ref.dtype)


def left_factors(a_all, ordered):
    groups, rows, per, _, _ = a_all.shape
    count = groups * per
    return pl.pallas_call(
        left_kernel,
        grid=(rows,),
        in_specs=[
            pl.BlockSpec((groups, 1, per, T, T), lambda i: (0, i, 0, 0, 0)),
            pl.BlockSpec((1, T, 2 * T), lambda i: (i, 0, 0)),
        ],
        out_specs=pl.BlockSpec((1, count, 2 * T, T), lambda i: (i, 0, 0, 0)),
        out_shape=jax.ShapeDtypeStruct((rows, count, 2 * T, T), jnp.bfloat16),
        cost_estimate=pl.CostEstimate(
            flops=rows * count * 4 * T**3, bytes_accessed=rows * count * 6 * T * T, transcendentals=0
        ),
        name="left_factors",
    )(a_all, ordered)


def diag_kernel(cols_ref, a_ref, p_ref, d_ref):
    rows, per, _, _ = a_ref.shape

    def row(i, _):
        left = p_ref[i].T
        for k in range(per):
            part = jnp.dot(left, a_ref[i, k], preferred_element_type=jnp.float32)
            d_ref[...] += jnp.dot(
                part.astype(jnp.bfloat16), p_ref[cols_ref[i, k]], preferred_element_type=jnp.float32
            )
        return 0

    d_ref[...] = jnp.zeros_like(d_ref)
    lax.fori_loop(0, rows, row, 0)


def diag_terms(a_diag, diag_cols, ordered):
    rows, per, _, _ = a_diag.shape
    return pl.pallas_call(
        diag_kernel,
        in_specs=[
            pl.BlockSpec(memory_space=pltpu.SMEM),
            pl.BlockSpec(memory_space=pltpu.VMEM),
            pl.BlockSpec(memory_space=pltpu.VMEM),
        ],
        out_specs=pl.BlockSpec(memory_space=pltpu.VMEM),
        out_shape=jax.ShapeDtypeStruct((2 * T, 2 * T), jnp.float32),
        cost_estimate=pl.CostEstimate(
            flops=rows * per * 12 * T**3, bytes_accessed=rows * per * 2 * T * T, transcendentals=0
        ),
        name="diag_terms",
    )(diag_cols, a_diag, ordered)


def offd_kernel(node_ref, pair_ref, odd_ref, l_ref, gath_ref, out_ref, rbuf, acc, sem):
    i = pl.program_id(0)
    rows = pl.num_programs(0)
    count = l_ref.shape[1]

    @pl.when(i == 0)
    def _():
        def fetch(t, _):
            pltpu.make_async_copy(
                gath_ref.at[pair_ref[t]], rbuf.at[t // count, t % count], sem.at[t // count]
            ).start()
            return 0

        lax.fori_loop(0, rows * count, fetch, 0)
        acc[...] = jnp.zeros_like(acc)

    pltpu.make_async_copy(gath_ref.at[pl.ds(0, count)], rbuf.at[i], sem.at[i]).wait()
    high = lax.broadcasted_iota(jnp.int32, (T, T), 1) >= H
    for k in range(count):
        t = i * count + k
        odd = odd_ref[t] == 1
        y = jnp.dot(l_ref[0, k], rbuf[i, k], preferred_element_type=jnp.float32)
        kept = jnp.where(odd, y[T:], y[:T])
        moved = jnp.where(odd, y[:T], y[T:])
        acc[node_ref[t]] += jnp.where(high == odd, kept, pltpu.roll(moved, H, 1))

    @pl.when(i == rows - 1)
    def _():
        quarter = out_ref.shape[2]
        for g in range(out_ref.shape[0]):
            out_ref[g] = acc[:, g * quarter : (g + 1) * quarter, :].astype(out_ref.dtype)


def offd_terms(nodes, pairs, odds, left, gathered, groups):
    rows, count, _, _ = left.shape
    total = gathered.shape[0]
    node_count = total // 4
    quarter = T // groups
    return pl.pallas_call(
        offd_kernel,
        grid_spec=pltpu.PrefetchScalarGridSpec(
            num_scalar_prefetch=3,
            grid=(rows,),
            in_specs=[
                pl.BlockSpec((1, count, 2 * T, T), lambda i, *_: (i, 0, 0, 0)),
                pl.BlockSpec(memory_space=pl.ANY),
            ],
            out_specs=pl.BlockSpec((groups, node_count, quarter, T), lambda i, *_: (0, 0, 0, 0)),
            scratch_shapes=[
                pltpu.VMEM((rows, count, T, T), jnp.bfloat16),
                pltpu.VMEM((node_count, T, T), jnp.float32),
                pltpu.SemaphoreType.DMA((rows,)),
            ],
        ),
        out_shape=jax.ShapeDtypeStruct((groups, node_count, quarter, T), jnp.bfloat16),
        compiler_params=pltpu.CompilerParams(vmem_limit_bytes=40 << 20),
        cost_estimate=pl.CostEstimate(
            flops=rows * count * 4 * T**3, bytes_accessed=rows * count * 6 * T * T, transcendentals=0
        ),
        name="offd_terms",
    )(nodes, pairs, odds, left, gathered)


def place_kernel(map_ref, me_ref, x_ref, d_ref, out_ref):
    slots = out_ref.shape[1]
    quarter = out_ref.shape[2]
    high = lax.broadcasted_iota(jnp.int32, (quarter, T), 1) >= H
    me = me_ref[0]

    def place(m, _):
        gid = map_ref[m]
        node, agg = gid // CR1, gid % CR1
        own = node == me
        left = x_ref[2 * agg, node].astype(jnp.float32)
        right = x_ref[2 * agg + 1, node].astype(jnp.float32)
        top = jnp.where(high, pltpu.roll(right, H, 1), left)
        low = jnp.where(high, right, pltpu.roll(left, H, 1))
        out_ref[0, m] = jnp.where(own, d_ref[0, agg], top).astype(out_ref.dtype)
        out_ref[1, m] = jnp.where(own, d_ref[1, agg], low).astype(out_ref.dtype)
        return 0

    lax.fori_loop(0, slots, place, 0, unroll=2)


def place_slots(col_map, me, arrived, own):
    slots = col_map.shape[0]
    quarter = arrived.shape[2]
    vmem = pl.BlockSpec(memory_space=pltpu.VMEM)
    smem = pl.BlockSpec(memory_space=pltpu.SMEM)
    return pl.pallas_call(
        place_kernel,
        in_specs=[smem, smem, vmem, vmem],
        out_specs=vmem,
        out_shape=jax.ShapeDtypeStruct((CR1, slots, quarter, T), jnp.bfloat16),
        compiler_params=pltpu.CompilerParams(vmem_limit_bytes=16 << 20),
        name="place_slots",
    )(col_map, me, arrived, own)


def per_device(
    a_diag, diag_cols, a_offd, offd_cols, prolong, aggregate, send_rows, ghost_agg, coarse_map
):
    groups = lax.axis_size("grp")
    me = lax.axis_index("rows")
    grp = lax.axis_index("grp")
    agg, half = grp // 2, grp % 2
    rows = prolong.shape[0]

    mine = jnp.where((aggregate[:, 0] == agg)[:, None, None], prolong[:, 0], prolong[:, 1])
    mine = jnp.where(half == 0, mine[..., :H], mine[..., H:])
    mine = jnp.concatenate([mine[0::2], mine[1::2]], axis=-1)
    gathered = lax.all_gather(mine, "rows", axis=0, tiled=True)
    a_all = lax.all_gather(a_offd, "grp", axis=0, tiled=False)
    rows_all = lax.all_gather(send_rows, "rows", axis=0, tiled=True)
    cols_all = lax.all_gather(offd_cols, "grp", axis=1, tiled=True)

    ordered = ordered_tiles(prolong, aggregate)
    partial = diag_terms(a_diag, diag_cols, ordered)
    partial = jnp.transpose(partial.reshape(CR1, T, CR1, T), (0, 2, 1, 3))
    own = lax.psum_scatter(partial, "grp", scatter_dimension=2, tiled=True)

    left = left_factors(a_all, ordered)

    cols = cols_all.reshape(-1)
    slots = send_rows.shape[2]
    nodes = cols // slots
    from_me = lax.dynamic_index_in_dim(rows_all, me, 1, keepdims=False).reshape(-1)
    rid = jnp.sum(
        jnp.where(cols[:, None] == jnp.arange(from_me.shape[0], dtype=jnp.int32), from_me, 0), axis=1
    )
    pairs = nodes * (rows // 2) + rid // 2
    offd = offd_terms(nodes, pairs, rid % 2, left, gathered, groups)
    arrived = lax.all_to_all(offd, "grp", split_axis=0, concat_axis=0, tiled=True)
    return place_slots(coarse_map[0], me.reshape(1), arrived, own)


def solution(mesh):
    in_specs = (
        P("rows", "grp", None, None),
        P("rows", "grp"),
        P("rows", "grp", None, None),
        P("rows", "grp"),
        P("rows", None, None, None),
        P("rows", None),
        P("rows", None, None),
        P("rows", None, None, None),
        P("rows", None),
    )
    out_specs = P("rows", None, "grp", None)
    return jax.shard_map(
        per_device, mesh=mesh, in_specs=in_specs, out_specs=out_specs, check_vma=False
    )
```

```python
import functools

import jax
import jax.numpy as jnp
from jax import lax
from jax.experimental import pallas as pl
from jax.experimental.pallas import tpu as pltpu
from jax.sharding import PartitionSpec as P

CR1 = 2
T = 128
H = T // 2


ROWS = 528
ZR = 320
NZ, NY = 8, 4
MESH = pl.DeviceIdType.MESH
PARTS = {"z": (0, ZR), "za": (0, ZR // 2), "zb": (ZR // 2, ZR // 2),
         "y": (ZR, ROWS - ZR), "ya": (ZR, 112), "yb": (ZR + 112, ROWS - ZR - 112)}
DZ = (0, 1, -1, 2, -2, 3, -3, 4)
LATE_UP = (0, 1, 2, 3)


def flood_plan():
    plan = {}

    def add(name, link, there, here, part, after):
        plan[name] = (link, there, here, part, tuple(after))

    for sign, link in ((1, "z+"), (-1, "z-")):
        for d in range(1, 5):
            part = "z" if d < 4 else ("za" if sign == 1 else "zb")
            after = [] if d == 1 else [("Z", sign * (d - 1))]
            here = sign * d if d < 4 else 4
            name = ("Z", here) if d < 4 else ("Z", 4, sign)
            add(name, link, (sign * (d - 1), 0), (here, 0), part, after)
    for e in DZ:
        have = [] if e == 0 else ([("Z", e)] if e != 4 else [("Z", 4, 1), ("Z", 4, -1)])
        for sign, link in ((1, "y+"), (-1, "y-")):
            add(("ZY", e, sign), link, (e, 0), (e, sign), "z", have)
        sign = 1 if e in LATE_UP else -1
        add(("ZY", e, 2), "y+" if sign == 1 else "y-", (e, sign), (e, 2), "z", [("ZY", e, sign)])
    for sign, link in ((1, "y+"), (-1, "y-")):
        add(("Y", sign), link, (0, 0), (0, sign), "y", [])
        add(("Y", 2, sign), link, (0, sign), (0, 2), "ya" if sign == 1 else "yb", [("Y", sign)])
    for sign, link in ((1, "z+"), (-1, "z-")):
        for d in range(1, 5):
            for dy in (0, 1, -1, 2):
                if d == 4 and (dy in (0, 1)) != (sign == 1):
                    continue
                if d > 1:
                    after = [("YZ", sign * (d - 1), dy)]
                elif dy == 0:
                    after = []
                else:
                    after = [("Y", dy)] if dy != 2 else [("Y", 2, 1), ("Y", 2, -1)]
                here = sign * d if d < 4 else 4
                add(("YZ", here, dy), link, (sign * (d - 1), dy), (here, dy), "y", after)
    return plan


def flood_order(plan):
    free = {}
    arrive, waiting = {}, dict(plan)
    rank = {"Y": 0, "Z": 1, "YZ": 2, "ZY": 3}
    while len(arrive) < len(plan):
        best = None
        for name, (link, _, _, part, after) in waiting.items():
            if any(a not in arrive for a in after):
                continue
            start = max([arrive[a] for a in after] + [free.get(link, 0.0)])
            key = (start, rank[name[0]], abs(name[1]), str(name))
            if best is None or key < best[0]:
                best = (key, name, start, link, part)
        _, name, start, link, part = best
        end = start + PARTS[part][1] * 256 / 50e3
        free[link] = end
        arrive[name] = end + 1.5
        del waiting[name]
    return arrive


def gather_kernel(
    agg_ref, dcols_ref, ocols_ref, srows_ref, p_ref, ad_ref, ao_ref,
    gath, left_out, own_ref, tbl_ref, cols_ref,
    mine, ordered, left_t, a_all, left, dacc, drecv, ctab, ext,
    ssem, rsem, xs_sem, xr_sem, lsem,
):
    me = lax.axis_index("rows")
    x = lax.axis_index("grp")
    core = lax.rem(me, 2)
    y = lax.rem(me // 2, NY)
    z = me // (2 * NY)

    def row_of(zz, yy, cc):
        return (zz * NY + yy) * 2 + cc

    up_z, dn_z = lax.rem(z + 1, NZ), lax.rem(z + NZ - 1, NZ)
    up_y, dn_y = lax.rem(y + 1, NY), lax.rem(y + NY - 1, NY)
    xat = [lax.rem(x + d, 4) for d in range(4)]
    link_to = {
        "z+": (row_of(up_z, y, core), x),
        "z-": (row_of(dn_z, y, core), x),
        "y+": (row_of(z, up_y, core), x),
        "y-": (row_of(z, dn_y, core), x),
        "core": (row_of(z, y, 1 - core), x),
        1: (me, xat[1]),
        2: (me, xat[2]),
        3: (me, xat[3]),
    }
    barrier = pltpu.get_barrier_semaphore()
    for device in link_to.values():
        pl.semaphore_signal(barrier, inc=1, device_id=device, device_id_type=MESH)
    pl.semaphore_wait(barrier, len(link_to))

    sends = []

    def remote(src, dst, s, r, device):
        return pltpu.make_async_remote_copy(
            src_ref=src, dst_ref=dst, send_sem=s, recv_sem=r, device_id=device, device_id_type=MESH
        )

    half = ao_ref.shape[0] // 2
    first, second = pl.ds(0, half), pl.ds(half, half)
    a_plan = {
        ("r", 0): (0, 1, first, 1), ("r", 1): (0, 1, second, 1), ("r", 2): (1, 2, first, 1),
        ("l", 1): (0, 3, second, 3), ("l", 0): (0, 3, first, 3), ("l", 2): (3, 2, second, 3),
    }
    a_index = {name: i for i, name in enumerate(a_plan)}

    def a_copy(name, sending):
        src_slot, dst_slot, part, to = a_plan[name]
        dst = a_all.at[dst_slot, part]
        src = (ao_ref if src_slot == 0 else a_all.at[src_slot]).at[part] if sending else dst
        i = a_index[name]
        return remote(src, dst, xs_sem.at[i], xr_sem.at[i], link_to[to])

    def a_send(name):
        copy = a_copy(name, True)
        copy.start()
        sends.append(copy)

    for name in (("r", 0), ("l", 1), ("r", 1), ("l", 0)):
        a_send(name)

    def c_copy(d, sending):
        src = ctab.at[0]
        return remote(src, ctab.at[d], xs_sem.at[5 + d], xr_sem.at[5 + d], link_to[d])

    ctab[0, :, 0 : ocols_ref.shape[1]] = ocols_ref[...]
    for d in (1, 2, 3):
        copy = c_copy(d, True)
        copy.start()
        sends.append(copy)

    agg, side = x // 2, lax.rem(x, 2)
    high = lax.broadcasted_iota(jnp.int32, (T, T), 1) >= H
    rows = p_ref.shape[0]
    for p in range(rows // 2):
        even = jnp.where(agg_ref[2 * p, 0] == agg, p_ref[2 * p, 0], p_ref[2 * p, 1]).astype(jnp.float32)
        odd = jnp.where(agg_ref[2 * p + 1, 0] == agg, p_ref[2 * p + 1, 0], p_ref[2 * p + 1, 1])
        odd = odd.astype(jnp.float32)
        kept = jnp.where(side == 0, even, odd)
        moved = pltpu.roll(jnp.where(side == 0, odd, even), H, 1)
        pair = jnp.where(high == (side == 1), kept, moved)
        mine[p * T : (p + 1) * T, :] = pair.astype(mine.dtype)
    tail = jnp.concatenate(
        [srows_ref[...].astype(jnp.float32), jnp.zeros((14, T), jnp.float32)], axis=0
    )
    mine[4 * T :, :] = tail.astype(mine.dtype)

    plan = flood_plan()
    names = sorted(plan, key=str)
    index = {name: i for i, name in enumerate(names)}
    sib = {}

    def block(offset, rows_at, plane=None):
        dz, dy = offset
        return gath.at[
            core if plane is None else plane,
            lax.rem(z + (NZ - dz), NZ), lax.rem(y + (NY - dy), NY), pl.ds(*rows_at)
        ]

    def f_copy(name, sending):
        link, there, here, part, _ = plan[name]
        at = PARTS[part]
        dst = block(there if sending else here, at)
        src = mine.at[pl.ds(*at)] if sending and there == (0, 0) else dst
        i = index[name]
        return remote(src, dst, ssem.at[i], rsem.at[i], link_to[link])

    def f_send(name):
        copy = f_copy(name, True)
        copy.start()
        sends.append(copy)

    started = set()

    def start_ready(have):
        for name in sorted(plan, key=lambda n: ({"Y": 0, "Z": 1, "YZ": 2, "ZY": 3}[n[0]], abs(n[1]), str(n))):
            if name not in started and all(a in have for a in plan[name][4]):
                started.add(name)
                f_send(name)

    def s_copy(kind, dz, sending):
        i = len(names) + DZ.index(dz) * 2 + (kind == "y")
        plane = core if sending else 1 - core
        at = PARTS[kind]
        ref = gath.at[plane, lax.rem(z + (NZ - dz), NZ), :, pl.ds(*at)]
        return remote(ref, ref, ssem.at[i], rsem.at[i], link_to["core"])

    need = {}
    for dz in DZ:
        zs = [] if dz == 0 else ([("Z", dz)] if dz != 4 else [("Z", 4, 1), ("Z", 4, -1)])
        need[("z", dz)] = zs + [("ZY", dz, s) for s in (1, -1, 2)]
        need[("y", dz)] = (
            [("Y", 1), ("Y", -1), ("Y", 2, 1), ("Y", 2, -1)] if dz == 0 else [("YZ", dz, s) for s in (0, 1, -1, 2)]
        )

    def share(have):
        for key in list(need):
            if all(a in have for a in need[key]):
                copy = s_copy(*key, True)
                copy.start()
                sends.append(copy)
                del need[key]

    have = set()
    start_ready(have)
    keep = pltpu.make_async_copy(mine, gath.at[core, z, y], lsem.at[0])
    keep.start()

    for i in range(rows):
        zero = jnp.where(agg_ref[i, 0] == 0, p_ref[i, 0], p_ref[i, 1])
        one = jnp.where(agg_ref[i, 0] == 0, p_ref[i, 1], p_ref[i, 0])
        ordered[i, :, :T] = zero
        ordered[i, :, T:] = one
    dacc[...] = jnp.zeros_like(dacc)
    per = ao_ref.shape[1]

    def diag_rows(lo, hi):
        def row(i, _):
            left_t[i] = ordered[i].T
            for k in range(per):
                part = jnp.dot(left_t[i], ad_ref[i, k], preferred_element_type=jnp.float32)
                dacc[...] += jnp.dot(
                    part.astype(jnp.bfloat16), ordered[dcols_ref[i, k]], preferred_element_type=jnp.float32
                ).reshape(dacc.shape)
            return 0

        lax.fori_loop(lo, hi, row, 0)

    def left_copy(slot, part):
        ref = left.at[slot, pl.ds(part * half, half)]
        return pltpu.make_async_copy(
            ref, left_out.at[slot, pl.ds(part * half, half)], lsem.at[1 + slot * 2 + part]
        )

    def left_rows(slot, part):
        def row(i, _):
            for k in range(per):
                tile = ao_ref[i, k] if slot == 0 else a_all[slot, i, k]
                left[slot, i, k] = jnp.dot(
                    left_t[i], tile, preferred_element_type=jnp.float32
                ).astype(left.dtype)
            return 0

        lax.fori_loop(part * half, part * half + half, row, 0)
        left_copy(slot, part).start()

    def d_copy(d, sending):
        quarter = dacc.shape[1] // 4
        src = dacc.at[:, pl.ds(pl.multiple_of(xat[d] * quarter, quarter), quarter)]
        return remote(src, drecv.at[d - 1], xs_sem.at[8 + d], xr_sem.at[8 + d], link_to[d])

    def send_diag():
        for d in (1, 2, 3):
            copy = d_copy(d, True)
            copy.start()
            sends.append(copy)

    def a_take(name, then=None):
        a_copy(name, False).wait_recv()
        if then:
            a_send(then)

    events = [(t, 1, name) for name, t in flood_order(plan).items()]
    steps = [
        (1.0, lambda: diag_rows(0, 2)), (3.5, lambda: diag_rows(2, 4)),
        (5.5, lambda: diag_rows(4, 6)), (7.5, lambda: diag_rows(6, 8)),
        (7.6, send_diag),
        (9.5, lambda: a_take(("r", 0), ("r", 2))), (9.6, lambda: a_take(("l", 1), ("l", 2))),
        (10.5, lambda: left_rows(0, 0)), (12.0, lambda: left_rows(0, 1)),
        (13.5, lambda: left_rows(1, 0)), (15.0, lambda: left_rows(3, 1)),
        (18.0, lambda: (a_take(("r", 1)), left_rows(1, 1))),
        (19.5, lambda: (a_take(("l", 0)), left_rows(3, 0))),
    ]
    events += [(t, 0, step) for t, step in steps]
    kept = False
    for _, kind, item in sorted(events, key=lambda e: (e[0], e[1], str(e[2]) if e[1] else "")):
        if kind == 0:
            item()
            continue
        f_copy(item, False).wait_recv()
        have.add(item)
        start_ready(have)
        if not kept:
            kept = True
            keep.wait()
        share(have)
    for name, part in ((("r", 2), 0), (("l", 2), 1)):
        a_take(name)
        left_rows(2, part)

    quarter = dacc.shape[1] // 4
    total = dacc[:, pl.ds(pl.multiple_of(x * quarter, quarter), quarter)]
    for d in (1, 2, 3):
        d_copy(d, False).wait_recv()
        total = total + drecv[d - 1]
        c_copy(d, False).wait_recv()
    own_ref[:, 0] = total[:, :, :T]
    own_ref[:, 1] = total[:, :, T:]
    cols_ref[...] = ctab[...]

    for dz in DZ:
        for kind in ("z", "y"):
            s_copy(kind, dz, False).wait_recv()
    fetch = pltpu.make_async_copy(gath.at[:, :, :, pl.ds(4 * T, 16)], ext, lsem.at[9])
    fetch.start()
    fetch.wait()
    line = me // (T // 4)
    tail = ext[...].reshape(2 * NZ * NY, 16, T).astype(jnp.float32)
    pick = lax.broadcasted_iota(jnp.int32, tail.shape, 1) == line
    tbl_ref[...] = jnp.sum(jnp.where(pick, tail, 0.0), axis=1).astype(jnp.int32)

    for copy in sends:
        copy.wait_send()
    for slot in range(4):
        for part in range(2):
            left_copy(slot, part).wait()


def gather_all(a_diag, diag_cols, a_offd, offd_cols, prolong, aggregate, send_rows):
    rows, per, _, _ = a_offd.shape
    vmem = pl.BlockSpec(memory_space=pltpu.VMEM)
    smem = pl.BlockSpec(memory_space=pltpu.SMEM)
    any_space = pl.BlockSpec(memory_space=pl.ANY)
    copies = len(flood_plan()) + 2 * len(DZ)
    bf16, f32 = jnp.bfloat16, jnp.float32
    return pl.pallas_call(
        gather_kernel,
        in_specs=[smem, smem, vmem, vmem, vmem, vmem, vmem],
        out_specs=[any_space, any_space, vmem, vmem, vmem],
        out_shape=[
            jax.ShapeDtypeStruct((2, NZ, NY, ROWS, T), bf16),
            jax.ShapeDtypeStruct((4, rows, per, 2 * T, T), bf16),
            jax.ShapeDtypeStruct((2, 2, T // 4, T), f32),
            jax.ShapeDtypeStruct((2 * NZ * NY, T), jnp.int32),
            jax.ShapeDtypeStruct((4, rows, T), jnp.int32),
        ],
        scratch_shapes=[
            pltpu.VMEM((ROWS, T), bf16),
            pltpu.VMEM((rows, T, 2 * T), bf16),
            pltpu.VMEM((rows, 2 * T, T), bf16),
            pltpu.VMEM((4, rows, per, T, T), bf16),
            pltpu.VMEM((4, rows, per, 2 * T, T), bf16),
            pltpu.VMEM((2, T, 2 * T), f32),
            pltpu.VMEM((3, 2, T // 4, 2 * T), f32),
            pltpu.VMEM((4, rows, T), jnp.int32),
            pltpu.VMEM((2, NZ, NY, 16, T), bf16),
            pltpu.SemaphoreType.DMA((copies,)),
            pltpu.SemaphoreType.DMA((copies,)),
            pltpu.SemaphoreType.DMA((12,)),
            pltpu.SemaphoreType.DMA((12,)),
            pltpu.SemaphoreType.DMA((10,)),
        ],
        compiler_params=pltpu.CompilerParams(
            collective_id=0, has_side_effects=True, vmem_limit_bytes=32 << 20
        ),
        name="gather_all",
    )(aggregate, diag_cols, offd_cols, send_rows.reshape(2, T), prolong, a_diag, a_offd)


def offd_kernel(me_ref, tbl_ref, cols_ref, l_ref, gath_ref, out_ref, rbuf, acc, sem):
    i = pl.program_id(0)
    rows = pl.num_programs(0)
    groups, _, per, _, _ = l_ref.shape
    count = groups * per
    base = lax.rem(me_ref[0], T // 4) * 4

    def place_of(g, r, k):
        col = cols_ref[g, r, k]
        node = col // 4
        slot = lax.rem(node, 2) * (NZ * NY) + node // 2
        return slot, tbl_ref[slot, base + lax.rem(col, 4)]

    @pl.when(i == 0)
    def _():
        def fetch(r, _):
            for t in range(count):
                slot, row = place_of(t // per, r, t % per)
                pair = gath_ref.at[slot, pl.ds(pl.multiple_of((row // 2) * T, T), T)]
                pltpu.make_async_copy(pair, rbuf.at[r, t], sem.at[r]).start()
            return 0

        lax.fori_loop(0, rows, fetch, 0)
        acc[...] = jnp.zeros_like(acc)

    pltpu.make_async_copy(gath_ref.at[pl.ds(0, count), pl.ds(0, T)], rbuf.at[i], sem.at[i]).wait()
    high = lax.broadcasted_iota(jnp.int32, (T, T), 1) >= H
    for t in range(count):
        slot, row = place_of(t // per, i, t % per)
        odd = lax.rem(row, 2) == 1
        y = jnp.dot(l_ref[t // per, 0, t % per], rbuf[i, t], preferred_element_type=jnp.float32)
        kept = jnp.where(odd, y[T:], y[:T])
        moved = jnp.where(odd, y[:T], y[T:])
        acc[slot] += jnp.where(high == odd, kept, pltpu.roll(moved, H, 1))

    @pl.when(i == rows - 1)
    def _():
        quarter = out_ref.shape[2]
        for g in range(out_ref.shape[0]):
            out_ref[g] = acc[:, g * quarter : (g + 1) * quarter, :].astype(out_ref.dtype)


def offd_terms(me, table, cols, left, gathered):
    groups, rows, per, _, _ = left.shape
    count = groups * per
    nodes = gathered.shape[0]
    quarter = T // groups
    return pl.pallas_call(
        offd_kernel,
        grid_spec=pltpu.PrefetchScalarGridSpec(
            num_scalar_prefetch=3,
            grid=(rows,),
            in_specs=[
                pl.BlockSpec((groups, 1, per, 2 * T, T), lambda i, *_: (0, i, 0, 0, 0)),
                pl.BlockSpec(memory_space=pl.ANY),
            ],
            out_specs=pl.BlockSpec((groups, nodes, quarter, T), lambda i, *_: (0, 0, 0, 0)),
            scratch_shapes=[
                pltpu.VMEM((rows, count, T, T), jnp.bfloat16),
                pltpu.VMEM((nodes, T, T), jnp.float32),
                pltpu.SemaphoreType.DMA((rows,)),
            ],
        ),
        out_shape=jax.ShapeDtypeStruct((groups, nodes, quarter, T), jnp.bfloat16),
        compiler_params=pltpu.CompilerParams(vmem_limit_bytes=40 << 20),
        cost_estimate=pl.CostEstimate(
            flops=rows * count * 4 * T**3, bytes_accessed=rows * count * 6 * T * T, transcendentals=0
        ),
        name="offd_terms",
    )(me, table, cols, left, gathered)


def place_kernel(map_ref, me_ref, x_ref, d_ref, out_ref):
    slots = out_ref.shape[1]
    quarter = out_ref.shape[2]
    high = lax.broadcasted_iota(jnp.int32, (quarter, T), 1) >= H
    me = me_ref[0]

    def place(m, _):
        gid = map_ref[m]
        node, agg = gid // CR1, gid % CR1
        own = node == me
        slot = lax.rem(node, 2) * (NZ * NY) + node // 2
        left = x_ref[2 * agg, slot].astype(jnp.float32)
        right = x_ref[2 * agg + 1, slot].astype(jnp.float32)
        top = jnp.where(high, pltpu.roll(right, H, 1), left)
        low = jnp.where(high, right, pltpu.roll(left, H, 1))
        out_ref[0, m] = jnp.where(own, d_ref[0, agg], top).astype(out_ref.dtype)
        out_ref[1, m] = jnp.where(own, d_ref[1, agg], low).astype(out_ref.dtype)
        return 0

    lax.fori_loop(0, slots, place, 0, unroll=2)


def place_slots(col_map, me, arrived, own):
    slots = col_map.shape[0]
    quarter = arrived.shape[2]
    vmem = pl.BlockSpec(memory_space=pltpu.VMEM)
    smem = pl.BlockSpec(memory_space=pltpu.SMEM)
    return pl.pallas_call(
        place_kernel,
        in_specs=[smem, smem, vmem, vmem],
        out_specs=vmem,
        out_shape=jax.ShapeDtypeStruct((CR1, slots, quarter, T), jnp.bfloat16),
        compiler_params=pltpu.CompilerParams(vmem_limit_bytes=16 << 20),
        name="place_slots",
    )(col_map, me, arrived, own)


def per_device(
    a_diag, diag_cols, a_offd, offd_cols, prolong, aggregate, send_rows, ghost_agg, coarse_map
):
    me = lax.axis_index("rows").reshape(1)
    gathered, left, own, table, cols = gather_all(
        a_diag, diag_cols, a_offd, offd_cols, prolong, aggregate, send_rows
    )
    gathered = gathered.reshape(2 * NZ * NY, ROWS, T)
    offd = offd_terms(me, table, cols, left, gathered)
    arrived = lax.all_to_all(offd, "grp", split_axis=0, concat_axis=0, tiled=True)
    return place_slots(coarse_map[0], me, arrived, own)


def solution(mesh):
    in_specs = (
        P("rows", "grp", None, None),
        P("rows", "grp"),
        P("rows", "grp", None, None),
        P("rows", "grp"),
        P("rows", None, None, None),
        P("rows", None),
        P("rows", None, None),
        P("rows", None, None, None),
        P("rows", None),
    )
    out_specs = P("rows", None, "grp", None)
    return jax.shard_map(
        per_device, mesh=mesh, in_specs=in_specs, out_specs=out_specs, check_vma=False
    )
```

```python
import functools

import jax
import jax.numpy as jnp
from jax import lax
from jax.experimental import pallas as pl
from jax.experimental.pallas import tpu as pltpu
from jax.sharding import PartitionSpec as P

CR1 = 2
T = 128
H = T // 2


ROWS = 528
ZR = 320
NZ, NY = 8, 4
MESH = pl.DeviceIdType.MESH
PARTS = {"z": (0, ZR), "za": (0, ZR // 2), "zb": (ZR // 2, ZR // 2),
         "y": (ZR, ROWS - ZR), "ya": (ZR, 112), "yb": (ZR + 112, ROWS - ZR - 112)}
DZ = (0, 1, -1, 2, -2, 3, -3, 4)
LATE_UP = (0, 1, 2, 3)


def flood_plan():
    plan = {}

    def add(name, link, there, here, part, after):
        plan[name] = (link, there, here, part, tuple(after))

    for sign, link in ((1, "z+"), (-1, "z-")):
        for d in range(1, 5):
            part = "z" if d < 4 else ("za" if sign == 1 else "zb")
            after = [] if d == 1 else [("Z", sign * (d - 1))]
            here = sign * d if d < 4 else 4
            name = ("Z", here) if d < 4 else ("Z", 4, sign)
            add(name, link, (sign * (d - 1), 0), (here, 0), part, after)
    for e in DZ:
        have = [] if e == 0 else ([("Z", e)] if e != 4 else [("Z", 4, 1), ("Z", 4, -1)])
        for sign, link in ((1, "y+"), (-1, "y-")):
            add(("ZY", e, sign), link, (e, 0), (e, sign), "z", have)
        sign = 1 if e in LATE_UP else -1
        add(("ZY", e, 2), "y+" if sign == 1 else "y-", (e, sign), (e, 2), "z", [("ZY", e, sign)])
    for sign, link in ((1, "y+"), (-1, "y-")):
        add(("Y", sign), link, (0, 0), (0, sign), "y", [])
        add(("Y", 2, sign), link, (0, sign), (0, 2), "ya" if sign == 1 else "yb", [("Y", sign)])
    for sign, link in ((1, "z+"), (-1, "z-")):
        for d in range(1, 5):
            for dy in (0, 1, -1, 2):
                if d == 4 and (dy in (0, 1)) != (sign == 1):
                    continue
                if d > 1:
                    after = [("YZ", sign * (d - 1), dy)]
                elif dy == 0:
                    after = []
                else:
                    after = [("Y", dy)] if dy != 2 else [("Y", 2, 1), ("Y", 2, -1)]
                here = sign * d if d < 4 else 4
                add(("YZ", here, dy), link, (sign * (d - 1), dy), (here, dy), "y", after)
    return plan


def flood_order(plan):
    free = {}
    arrive, waiting = {}, dict(plan)
    rank = {"Y": 0, "Z": 1, "YZ": 2, "ZY": 3}
    while len(arrive) < len(plan):
        best = None
        for name, (link, _, _, part, after) in waiting.items():
            if any(a not in arrive for a in after):
                continue
            start = max([arrive[a] for a in after] + [free.get(link, 0.0)])
            key = (start, rank[name[0]], abs(name[1]), str(name))
            if best is None or key < best[0]:
                best = (key, name, start, link, part)
        _, name, start, link, part = best
        end = start + PARTS[part][1] * 256 / 50e3
        free[link] = end
        arrive[name] = end + 1.5
        del waiting[name]
    return arrive


def gather_kernel(
    agg_ref, dcols_ref, ocols_ref, srows_ref, p_hbm, ad_hbm, ao_hbm,
    gath, left, own_ref, tbl_ref, cols_ref,
    p_ref, ad_ref, mine, stage, tiles, ordered, left_t, a_all, dacc, dsend, drecv, ctab,
    ssem, rsem, xs_sem, xr_sem, lsem,
):
    me = lax.axis_index("rows")
    x = lax.axis_index("grp")
    core = lax.rem(me, 2)
    y = lax.rem(me // 2, NY)
    z = me // (2 * NY)

    def row_of(zz, yy, cc):
        return (zz * NY + yy) * 2 + cc

    up_z, dn_z = lax.rem(z + 1, NZ), lax.rem(z + NZ - 1, NZ)
    up_y, dn_y = lax.rem(y + 1, NY), lax.rem(y + NY - 1, NY)
    xat = [lax.rem(x + d, 4) for d in range(4)]
    link_to = {
        "z+": (row_of(up_z, y, core), x),
        "z-": (row_of(dn_z, y, core), x),
        "y+": (row_of(z, up_y, core), x),
        "y-": (row_of(z, dn_y, core), x),
        "core": (row_of(z, y, 1 - core), x),
        1: (me, xat[1]),
        2: (me, xat[2]),
        3: (me, xat[3]),
    }
    barrier = pltpu.get_barrier_semaphore()
    for device in link_to.values():
        pl.semaphore_signal(barrier, inc=1, device_id=device, device_id_type=MESH)

    loads = [
        pltpu.make_async_copy(p_hbm, p_ref, lsem.at[1]),
        pltpu.make_async_copy(ao_hbm, a_all.at[0], lsem.at[2]),
        pltpu.make_async_copy(ad_hbm, ad_ref, lsem.at[3]),
    ]
    for load in loads:
        load.start()

    sends = []

    def remote(src, dst, s, r, device):
        return pltpu.make_async_remote_copy(
            src_ref=src, dst_ref=dst, send_sem=s, recv_sem=r, device_id=device, device_id_type=MESH
        )

    half = ao_hbm.shape[0] // 2
    first, second = pl.ds(0, half), pl.ds(half, half)
    a_plan = {
        ("r", 0): (0, 1, first, 1), ("r", 1): (0, 1, second, 1), ("r", 2): (1, 2, first, 1),
        ("l", 1): (0, 3, second, 3), ("l", 0): (0, 3, first, 3), ("l", 2): (3, 2, second, 3),
    }
    a_index = {name: i for i, name in enumerate(a_plan)}

    def a_copy(name, sending):
        src_slot, dst_slot, part, to = a_plan[name]
        dst = a_all.at[dst_slot, part]
        src = (ao_hbm if src_slot == 0 else a_all.at[src_slot]).at[part] if sending else dst
        i = a_index[name]
        return remote(src, dst, xs_sem.at[i], xr_sem.at[i], link_to[to])

    def a_send(name):
        copy = a_copy(name, True)
        copy.start()
        sends.append(copy)

    def c_copy(d):
        return remote(ctab.at[0], ctab.at[d], xs_sem.at[5 + d], xr_sem.at[5 + d], link_to[d])

    lane = lax.broadcasted_iota(jnp.int32, (T, T), 1)
    rows = p_hbm.shape[0]
    stage[...] = jnp.zeros_like(stage)
    stage[0 : srows_ref.shape[0], 0 : srows_ref.shape[1]] = srows_ref[...].astype(jnp.float32)
    ctab[0, 0 : ocols_ref.shape[0], 0 : ocols_ref.shape[1]] = ocols_ref[...]
    loads[0].wait()

    def tile(i, a):
        flip = agg_ref[0, i] == a
        return jnp.where(flip, p_ref[i, 0], p_ref[i, 1]).astype(jnp.float32)

    for p in range(rows // 2):
        pair = None
        for r in range(2):
            for a in range(2):
                at = r * 64 + a * 32
                moved = pltpu.roll(tile(2 * p + r, a), lax.rem(at + T - 32 * x, T), 1)
                pair = moved if pair is None else jnp.where(lane >= at, moved, pair)
        mine[p * T : (p + 1) * T, :] = pair.astype(mine.dtype)
    mine[4 * T :, :] = stage[...].astype(mine.dtype)

    plan = flood_plan()
    names = sorted(plan, key=str)
    index = {name: i for i, name in enumerate(names)}

    def block(offset, rows_at):
        dz, dy = offset
        return gath.at[core, lax.rem(z + (NZ - dz), NZ), lax.rem(y + (NY - dy), NY), pl.ds(*rows_at)]

    def f_copy(name, sending):
        link, there, here, part, _ = plan[name]
        at = PARTS[part]
        dst = block(there if sending else here, at)
        src = mine.at[pl.ds(*at)] if sending and there == (0, 0) else dst
        i = index[name]
        return remote(src, dst, ssem.at[i], rsem.at[i], link_to[link])

    started = set()

    def start_ready(have):
        order = {"Y": 0, "Z": 1, "YZ": 2, "ZY": 3}
        for name in sorted(plan, key=lambda n: (order[n[0]], abs(n[1]), str(n))):
            if name not in started and all(a in have for a in plan[name][4]):
                started.add(name)
                copy = f_copy(name, True)
                copy.start()
                sends.append(copy)

    def s_copy(kind, dz, sending):
        i = len(names) + DZ.index(dz) * 2 + (kind == "y")
        plane = core if sending else 1 - core
        ref = gath.at[plane, lax.rem(z + (NZ - dz), NZ), :, pl.ds(*PARTS[kind])]
        return remote(ref, ref, ssem.at[i], rsem.at[i], link_to["core"])

    need = {}
    for dz in DZ:
        zs = [] if dz == 0 else ([("Z", dz)] if dz != 4 else [("Z", 4, 1), ("Z", 4, -1)])
        need[("z", dz)] = zs + [("ZY", dz, s) for s in (1, -1, 2)]
        need[("y", dz)] = (
            [("Y", 1), ("Y", -1), ("Y", 2, 1), ("Y", 2, -1)]
            if dz == 0
            else [("YZ", dz, s) for s in (0, 1, -1, 2)]
        )

    def share(have):
        for key in list(need):
            if all(a in have for a in need[key]):
                copy = s_copy(*key, True)
                copy.start()
                sends.append(copy)
                del need[key]

    pl.semaphore_wait(barrier, len(link_to))
    have = set()
    start_ready(have)
    for name in (("r", 0), ("l", 1), ("r", 1), ("l", 0)):
        a_send(name)
    for d in (1, 2, 3):
        copy = c_copy(d)
        copy.start()
        sends.append(copy)
    keep = pltpu.make_async_copy(mine, gath.at[core, z, y], lsem.at[0])
    keep.start()

    per = ao_hbm.shape[1]

    def order_rows(lo, hi):
        def row(i, _):
            zero, one = tile(i, 0), tile(i, 1)
            tiles[0] = zero.astype(tiles.dtype)
            tiles[1] = one.astype(tiles.dtype)
            left_t[i, :T] = tiles[0].T
            left_t[i, T:] = tiles[1].T
            z32, z64, z96 = (pltpu.roll(zero, s, 1) for s in (32, 64, 96))
            o32, o64, o96 = (pltpu.roll(one, s, 1) for s in (32, 64, 96))
            low = jnp.where(lane < 32, zero, jnp.where(lane < 64, o32, jnp.where(lane < 96, z32, o64)))
            top = jnp.where(lane < 32, z64, jnp.where(lane < 64, o96, jnp.where(lane < 96, z96, one)))
            ordered[i, :, :T] = low.astype(ordered.dtype)
            ordered[i, :, T:] = top.astype(ordered.dtype)
            return 0

        lax.fori_loop(lo, hi, row, 0)

    def diag_rows(lo, hi):
        def row(i, _):
            for k in range(per):
                part = jnp.dot(left_t[i], ad_ref[i, k], preferred_element_type=jnp.float32)
                dacc[...] += jnp.dot(
                    part.astype(jnp.bfloat16), ordered[dcols_ref[k, i]], preferred_element_type=jnp.float32
                )
            return 0

        lax.fori_loop(lo, hi, row, 0)

    def left_rows(slot, part):
        def row(i, _):
            for k in range(per):
                left[slot, i, k] = jnp.dot(
                    left_t[i], a_all[slot, i, k], preferred_element_type=jnp.float32
                ).astype(left.dtype)
            return 0

        lax.fori_loop(part * half, part * half + half, row, 0)

    def d_copy(d):
        return remote(
            dsend.at[xat[d]], drecv.at[d - 1], xs_sem.at[8 + d], xr_sem.at[8 + d], link_to[d]
        )

    def send_diag():
        for q in range(4):
            at = slice((q // 2) * T, (q // 2 + 1) * T)
            zero, one = dacc[:T, at], dacc[T:, at]
            if q % 2 == 0:
                one = pltpu.roll(one, H, 1)
            else:
                zero = pltpu.roll(zero, H, 1)
            dsend[q] = jnp.where(lane < H, zero, one)
        for d in (1, 2, 3):
            copy = d_copy(d)
            copy.start()
            sends.append(copy)

    def a_take(name, then=None):
        a_copy(name, False).wait_recv()
        if then:
            a_send(then)

    def begin():
        dacc[...] = jnp.zeros_like(dacc)
        loads[1].wait()
        loads[2].wait()
        order_rows(0, rows)

    events = [(t, 1, name) for name, t in flood_order(plan).items()]
    steps = [
        (0.0, begin), (1.5, lambda: diag_rows(0, 2)), (3.5, lambda: diag_rows(2, 4)),
        (5.5, lambda: diag_rows(4, 6)), (7.5, lambda: diag_rows(6, 8)),
        (7.6, send_diag),
        (9.5, lambda: a_take(("r", 0), ("r", 2))), (9.6, lambda: a_take(("l", 1), ("l", 2))),
        (10.5, lambda: left_rows(0, 0)), (12.0, lambda: left_rows(0, 1)),
        (13.5, lambda: left_rows(1, 0)), (15.0, lambda: left_rows(3, 1)),
        (18.0, lambda: (a_take(("r", 1)), left_rows(1, 1))),
        (19.5, lambda: (a_take(("l", 0)), left_rows(3, 0))),
    ]
    events += [(t, 0, step) for t, step in steps]
    kept = False
    for _, kind, item in sorted(events, key=lambda e: (e[0], e[1], str(e[2]) if e[1] else "")):
        if kind == 0:
            item()
            continue
        f_copy(item, False).wait_recv()
        have.add(item)
        start_ready(have)
        if not kept:
            kept = True
            keep.wait()
        share(have)
    for name, part in ((("r", 2), 0), (("l", 2), 1)):
        a_take(name)
        left_rows(2, part)

    total = dsend[x]
    for d in (1, 2, 3):
        d_copy(d).wait_recv()
        total = total + drecv[d - 1]
        c_copy(d).wait_recv()
    own_ref[...] = total
    cols_ref[...] = ctab[...]

    for dz in DZ:
        for kind in ("z", "y"):
            s_copy(kind, dz, False).wait_recv()
    tail = gath[:, :, :, 4 * T :, :].reshape(2 * NZ * NY * 16, T)
    pick = (lax.broadcasted_iota(jnp.int32, (T, T), 0) == me).astype(jnp.bfloat16)
    spread = jnp.dot(tail, pick, preferred_element_type=jnp.float32).reshape(2 * NZ * NY, 16, T)
    line = lax.broadcasted_iota(jnp.int32, spread.shape, 1) == lax.broadcasted_iota(
        jnp.int32, spread.shape, 2
    )
    tbl_ref[...] = jnp.sum(jnp.where(line, spread, 0.0), axis=1).astype(jnp.int32)

    for copy in sends:
        copy.wait_send()


def gather_all(a_diag, diag_cols, a_offd, offd_cols, prolong, aggregate, send_rows):
    rows, per, _, _ = a_offd.shape
    vmem = pl.BlockSpec(memory_space=pltpu.VMEM)
    smem = pl.BlockSpec(memory_space=pltpu.SMEM)
    hbm = pl.BlockSpec(memory_space=pltpu.HBM)
    copies = len(flood_plan()) + 2 * len(DZ)
    bf16, f32 = jnp.bfloat16, jnp.float32
    return pl.pallas_call(
        gather_kernel,
        in_specs=[smem, smem, vmem, vmem, hbm, hbm, hbm],
        out_specs=[vmem, vmem, vmem, vmem, vmem],
        out_shape=[
            jax.ShapeDtypeStruct((2, NZ, NY, ROWS, T), bf16),
            jax.ShapeDtypeStruct((4, rows, per, 2 * T, T), bf16),
            jax.ShapeDtypeStruct((T, T), f32),
            jax.ShapeDtypeStruct((2 * NZ * NY, T), jnp.int32),
            jax.ShapeDtypeStruct((4, 8, T), jnp.int32),
        ],
        scratch_shapes=[
            pltpu.VMEM((rows, 2, T, T), bf16),
            pltpu.VMEM((rows, per, T, T), bf16),
            pltpu.VMEM((ROWS, T), bf16),
            pltpu.VMEM((16, T), f32),
            pltpu.VMEM((2, T, T), bf16),
            pltpu.VMEM((rows, T, 2 * T), bf16),
            pltpu.VMEM((rows, 2 * T, T), bf16),
            pltpu.VMEM((4, rows, per, T, T), bf16),
            pltpu.VMEM((2 * T, 2 * T), f32),
            pltpu.VMEM((4, T, T), f32),
            pltpu.VMEM((3, T, T), f32),
            pltpu.VMEM((4, 8, T), jnp.int32),
            pltpu.SemaphoreType.DMA((copies,)),
            pltpu.SemaphoreType.DMA((copies,)),
            pltpu.SemaphoreType.DMA((12,)),
            pltpu.SemaphoreType.DMA((12,)),
            pltpu.SemaphoreType.DMA((4,)),
        ],
        compiler_params=pltpu.CompilerParams(
            collective_id=0, has_side_effects=True, vmem_limit_bytes=32 << 20
        ),
        name="gather_all",
    )(aggregate.T, diag_cols.T, offd_cols.T, send_rows[0].T, prolong, a_diag, a_offd)


def offd_kernel(me_ref, map_ref, tbl_ref, cols_ref, l_ref, gath_ref, d_ref, out_ref, acc):
    groups, rows, per, _, _ = l_ref.shape
    high = lax.broadcasted_iota(jnp.int32, (T, T), 1) >= H
    acc[...] = jnp.zeros_like(acc)

    def slot_of(node):
        return lax.rem(node, 2) * (NZ * NY) + node // 2

    def row(i, _):
        for t in range(groups * per):
            g, k = t // per, t % per
            col = cols_ref[g, k, i]
            slot = slot_of(col // 4)
            sent = tbl_ref[slot, lax.rem(col, 4)]
            odd = lax.rem(sent, 2) == 1
            right = gath_ref[slot, pl.ds(pl.multiple_of((sent // 2) * T, T), T), :]
            y = jnp.dot(l_ref[g, i, k], right, preferred_element_type=jnp.float32)
            kept = jnp.where(odd, y[T:], y[:T])
            moved = jnp.where(odd, y[:T], y[T:])
            acc[slot] += jnp.where(high == odd, kept, pltpu.roll(moved, H, 1))
        return 0

    lax.fori_loop(0, rows, row, 0)
    acc[slot_of(me_ref[0])] = d_ref[...]

    lane = lax.broadcasted_iota(jnp.int32, (T, T), 1)
    even = lax.rem(lane // 32, 2) == 0

    def pack(p, _):
        def part(j):
            gid = map_ref[2 * p + j]
            shift = lax.rem((j - lax.rem(gid, CR1)) * 32 + T, T)
            return pltpu.roll(acc[slot_of(gid // CR1)], shift, 1)

        both = jnp.where(even, part(0), part(1)).astype(out_ref.dtype)
        quarter = out_ref.shape[2]
        for g in range(out_ref.shape[0]):
            out_ref[g, p] = both[g * quarter : (g + 1) * quarter]
        return 0

    lax.fori_loop(0, out_ref.shape[1], pack, 0)


def offd_terms(me, col_map, table, cols, left, gathered, own):
    groups, rows, per, _, _ = left.shape
    nodes = gathered.shape[0]
    vmem = pl.BlockSpec(memory_space=pltpu.VMEM)
    smem = pl.BlockSpec(memory_space=pltpu.SMEM)
    return pl.pallas_call(
        offd_kernel,
        in_specs=[smem, smem, smem, smem, vmem, vmem, vmem],
        out_specs=vmem,
        out_shape=jax.ShapeDtypeStruct((groups, col_map.shape[0] // 2, T // groups, T), jnp.bfloat16),
        scratch_shapes=[pltpu.VMEM((nodes, T, T), jnp.float32)],
        compiler_params=pltpu.CompilerParams(vmem_limit_bytes=32 << 20),
        name="offd_terms",
    )(me, col_map, table, cols, left, gathered, own)


def swap_kernel(src, out, hold, ssem, rsem, lsem):
    me = lax.axis_index("rows")
    x = lax.axis_index("grp")
    at = [lax.rem(x + d, 4) for d in range(4)]
    up, down = (me, at[1]), (me, at[3])
    barrier = pltpu.get_barrier_semaphore()
    for device in (up, down):
        pl.semaphore_signal(barrier, inc=1, device_id=device, device_id_type=MESH)
    pl.semaphore_wait(barrier, 2)
    pairs = src.shape[1]
    cut = pairs // 2
    low, top = pl.ds(0, cut), pl.ds(cut, pairs - cut)

    def remote(a, b, i, device):
        return pltpu.make_async_remote_copy(
            src_ref=a, dst_ref=b, send_sem=ssem.at[i], recv_sem=rsem.at[i],
            device_id=device, device_id_type=MESH,
        )

    far = src.at[at[2]]
    sends = [
        remote(far.at[low], hold.at[low], 0, up),
        remote(far.at[top], hold.at[top], 1, down),
        remote(src.at[at[1]], out.at[x], 2, up),
        remote(src.at[at[3]], out.at[x], 3, down),
    ]
    for copy in sends:
        copy.start()
    stay = pltpu.make_async_copy(src.at[x], out.at[x], lsem)
    stay.start()
    remote(hold.at[low], hold.at[low], 0, up).wait_recv()
    sends.append(remote(hold.at[low], out.at[at[3], low], 4, up))
    sends[-1].start()
    remote(hold.at[top], hold.at[top], 1, down).wait_recv()
    sends.append(remote(hold.at[top], out.at[at[1], top], 5, down))
    sends[-1].start()
    remote(out.at[at[3]], out.at[at[3]], 2, up).wait_recv()
    remote(out.at[at[1]], out.at[at[1]], 3, down).wait_recv()
    remote(out.at[at[2], low], out.at[at[2], low], 4, up).wait_recv()
    remote(out.at[at[2], top], out.at[at[2], top], 5, down).wait_recv()
    stay.wait()
    for copy in sends:
        copy.wait_send()


def swap_slices(src):
    vmem = pl.BlockSpec(memory_space=pltpu.VMEM)
    return pl.pallas_call(
        swap_kernel,
        in_specs=[vmem],
        out_specs=vmem,
        out_shape=jax.ShapeDtypeStruct(src.shape, src.dtype),
        scratch_shapes=[
            pltpu.VMEM(src.shape[1:], src.dtype),
            pltpu.SemaphoreType.DMA((6,)),
            pltpu.SemaphoreType.DMA((6,)),
            pltpu.SemaphoreType.DMA,
        ],
        compiler_params=pltpu.CompilerParams(
            collective_id=1, has_side_effects=True, vmem_limit_bytes=16 << 20
        ),
        name="swap_slices",
    )(src)


def place_kernel(x_ref, out_ref):
    pairs, quarter = x_ref.shape[1], x_ref.shape[2]
    lane = lax.broadcasted_iota(jnp.int32, (quarter, T), 1)
    odd32 = lax.rem(lane // 32, 2) == 1
    odd64 = lane >= H

    def swap(a, b, shift, odd):
        return (
            jnp.where(odd, pltpu.roll(b, shift, 1), a),
            jnp.where(odd, b, pltpu.roll(a, T - shift, 1)),
        )

    for p in range(pairs):
        w = [x_ref[s, p].astype(jnp.float32) for s in range(4)]
        a0, a1 = swap(w[0], w[1], 32, odd32)
        b0, b1 = swap(w[2], w[3], 32, odd32)
        c00, c10 = swap(a0, b0, H, odd64)
        c01, c11 = swap(a1, b1, H, odd64)
        out_ref[0, 2 * p] = c00.astype(out_ref.dtype)
        out_ref[0, 2 * p + 1] = c01.astype(out_ref.dtype)
        out_ref[1, 2 * p] = c10.astype(out_ref.dtype)
        out_ref[1, 2 * p + 1] = c11.astype(out_ref.dtype)


def place_slots(arrived):
    groups, pairs, quarter, _ = arrived.shape
    step = 7
    return pl.pallas_call(
        place_kernel,
        grid=(pairs // step,),
        in_specs=[pl.BlockSpec((groups, step, quarter, T), lambda i: (0, i, 0, 0))],
        out_specs=pl.BlockSpec((CR1, 2 * step, quarter, T), lambda i: (0, i, 0, 0)),
        out_shape=jax.ShapeDtypeStruct((CR1, 2 * pairs, quarter, T), jnp.bfloat16),
        name="place_slots",
    )(arrived)


def per_device(
    a_diag, diag_cols, a_offd, offd_cols, prolong, aggregate, send_rows, ghost_agg, coarse_map
):
    me = lax.axis_index("rows").reshape(1)
    gathered, left, own, table, cols = gather_all(
        a_diag, diag_cols, a_offd, offd_cols, prolong, aggregate, send_rows
    )
    gathered = gathered.reshape(2 * NZ * NY, ROWS, T)
    offd = offd_terms(me, coarse_map[0], table, cols, left, gathered, own)
    return place_slots(swap_slices(offd))


def solution(mesh):
    in_specs = (
        P("rows", "grp", None, None),
        P("rows", "grp"),
        P("rows", "grp", None, None),
        P("rows", "grp"),
        P("rows", None, None, None),
        P("rows", None),
        P("rows", None, None),
        P("rows", None, None, None),
        P("rows", None),
    )
    out_specs = P("rows", None, "grp", None)
    return jax.shard_map(
        per_device, mesh=mesh, in_specs=in_specs, out_specs=out_specs, check_vma=False
    )
```

```python
import functools

import jax
import jax.numpy as jnp
from jax import lax
from jax.experimental import pallas as pl
from jax.experimental.pallas import tpu as pltpu
from jax.sharding import PartitionSpec as P

CR1 = 2
T = 128
H = T // 2


ROWS = 528
ZR = 320
NZ, NY = 8, 4
MESH = pl.DeviceIdType.MESH
PARTS = {"z": (0, ZR), "za": (0, ZR // 2), "zb": (ZR // 2, ZR // 2),
         "y": (ZR, ROWS - ZR), "ya": (ZR, 112), "yb": (ZR + 112, ROWS - ZR - 112)}
DZ = (0, 1, -1, 2, -2, 3, -3, 4)
LATE_UP = (0, 1, 2, 3)


def flood_plan():
    plan = {}

    def add(name, link, there, here, part, after):
        plan[name] = (link, there, here, part, tuple(after))

    for sign, link in ((1, "z+"), (-1, "z-")):
        for d in range(1, 5):
            part = "z" if d < 4 else ("za" if sign == 1 else "zb")
            after = [] if d == 1 else [("Z", sign * (d - 1))]
            here = sign * d if d < 4 else 4
            name = ("Z", here) if d < 4 else ("Z", 4, sign)
            add(name, link, (sign * (d - 1), 0), (here, 0), part, after)
    for e in DZ:
        have = [] if e == 0 else ([("Z", e)] if e != 4 else [("Z", 4, 1), ("Z", 4, -1)])
        for sign, link in ((1, "y+"), (-1, "y-")):
            add(("ZY", e, sign), link, (e, 0), (e, sign), "z", have)
        sign = 1 if e in LATE_UP else -1
        add(("ZY", e, 2), "y+" if sign == 1 else "y-", (e, sign), (e, 2), "z", [("ZY", e, sign)])
    for sign, link in ((1, "y+"), (-1, "y-")):
        add(("Y", sign), link, (0, 0), (0, sign), "y", [])
        add(("Y", 2, sign), link, (0, sign), (0, 2), "ya" if sign == 1 else "yb", [("Y", sign)])
    for sign, link in ((1, "z+"), (-1, "z-")):
        for d in range(1, 5):
            for dy in (0, 1, -1, 2):
                if d == 4 and (dy in (0, 1)) != (sign == 1):
                    continue
                if d > 1:
                    after = [("YZ", sign * (d - 1), dy)]
                elif dy == 0:
                    after = []
                else:
                    after = [("Y", dy)] if dy != 2 else [("Y", 2, 1), ("Y", 2, -1)]
                here = sign * d if d < 4 else 4
                add(("YZ", here, dy), link, (sign * (d - 1), dy), (here, dy), "y", after)
    return plan


def flood_order(plan):
    free = {}
    arrive, waiting = {}, dict(plan)
    rank = {"Y": 0, "Z": 1, "YZ": 2, "ZY": 3}
    while len(arrive) < len(plan):
        best = None
        for name, (link, _, _, part, after) in waiting.items():
            if any(a not in arrive for a in after):
                continue
            start = max([arrive[a] for a in after] + [free.get(link, 0.0)])
            key = (start, rank[name[0]], abs(name[1]), str(name))
            if best is None or key < best[0]:
                best = (key, name, start, link, part)
        _, name, start, link, part = best
        end = start + PARTS[part][1] * 256 / 50e3
        free[link] = end
        arrive[name] = end + 1.5
        del waiting[name]
    return arrive


def gather_kernel(
    agg_ref, dcols_ref, ocols_ref, srows_ref, p_hbm, ad_hbm, ao_hbm,
    gath, left, own_ref, tbl_ref, cols_ref,
    p_ref, ad_ref, mine, stage, tiles, ordered, left_t, a_all, dacc, dsend, drecv, ctab,
    ssem, rsem, xs_sem, xr_sem, lsem,
):
    me = lax.axis_index("rows")
    x = lax.axis_index("grp")
    core = lax.rem(me, 2)
    y = lax.rem(me // 2, NY)
    z = me // (2 * NY)

    def row_of(zz, yy, cc):
        return (zz * NY + yy) * 2 + cc

    up_z, dn_z = lax.rem(z + 1, NZ), lax.rem(z + NZ - 1, NZ)
    up_y, dn_y = lax.rem(y + 1, NY), lax.rem(y + NY - 1, NY)
    xat = [lax.rem(x + d, 4) for d in range(4)]
    link_to = {
        "z+": (row_of(up_z, y, core), x),
        "z-": (row_of(dn_z, y, core), x),
        "y+": (row_of(z, up_y, core), x),
        "y-": (row_of(z, dn_y, core), x),
        "core": (row_of(z, y, 1 - core), x),
        1: (me, xat[1]),
        2: (me, xat[2]),
        3: (me, xat[3]),
    }
    barrier = pltpu.get_barrier_semaphore()
    for device in link_to.values():
        pl.semaphore_signal(barrier, inc=1, device_id=device, device_id_type=MESH)

    loads = [
        pltpu.make_async_copy(p_hbm, p_ref, lsem.at[1]),
        pltpu.make_async_copy(ao_hbm, a_all.at[0], lsem.at[2]),
        pltpu.make_async_copy(ad_hbm, ad_ref, lsem.at[3]),
    ]
    for load in loads:
        load.start()

    sends = []

    def remote(src, dst, s, r, device):
        return pltpu.make_async_remote_copy(
            src_ref=src, dst_ref=dst, send_sem=s, recv_sem=r, device_id=device, device_id_type=MESH
        )

    half = ao_hbm.shape[0] // 2
    first, second = pl.ds(0, half), pl.ds(half, half)
    a_plan = {
        ("r", 0): (0, 1, first, 1), ("r", 1): (0, 1, second, 1), ("r", 2): (1, 2, first, 1),
        ("l", 1): (0, 3, second, 3), ("l", 0): (0, 3, first, 3), ("l", 2): (3, 2, second, 3),
    }
    a_index = {name: i for i, name in enumerate(a_plan)}

    def a_copy(name, sending):
        src_slot, dst_slot, part, to = a_plan[name]
        dst = a_all.at[dst_slot, part]
        src = (ao_hbm if src_slot == 0 else a_all.at[src_slot]).at[part] if sending else dst
        i = a_index[name]
        return remote(src, dst, xs_sem.at[i], xr_sem.at[i], link_to[to])

    def a_send(name):
        copy = a_copy(name, True)
        copy.start()
        sends.append(copy)

    def c_copy(d):
        return remote(ctab.at[0], ctab.at[d], xs_sem.at[5 + d], xr_sem.at[5 + d], link_to[d])

    lane = lax.broadcasted_iota(jnp.int32, (T, T), 1)
    rows = p_hbm.shape[0]
    stage[...] = jnp.zeros_like(stage)
    stage[0 : srows_ref.shape[0], 0 : srows_ref.shape[1]] = srows_ref[...].astype(jnp.float32)
    ctab[0, 0 : ocols_ref.shape[0], 0 : ocols_ref.shape[1]] = ocols_ref[...]
    loads[0].wait()

    def tile(i, a):
        flip = agg_ref[0, i] == a
        return jnp.where(flip, p_ref[i, 0], p_ref[i, 1]).astype(jnp.float32)

    for p in range(rows // 2):
        pair = None
        for r in range(2):
            for a in range(2):
                at = r * 64 + a * 32
                moved = pltpu.roll(tile(2 * p + r, a), lax.rem(at + T - 32 * x, T), 1)
                pair = moved if pair is None else jnp.where(lane >= at, moved, pair)
        mine[p * T : (p + 1) * T, :] = pair.astype(mine.dtype)
    mine[4 * T :, :] = stage[...].astype(mine.dtype)

    plan = flood_plan()
    names = sorted(plan, key=str)
    index = {name: i for i, name in enumerate(names)}

    def block(offset, rows_at):
        dz, dy = offset
        return gath.at[core, lax.rem(z + (NZ - dz), NZ), lax.rem(y + (NY - dy), NY), pl.ds(*rows_at)]

    def f_copy(name, sending):
        link, there, here, part, _ = plan[name]
        at = PARTS[part]
        dst = block(there if sending else here, at)
        src = mine.at[pl.ds(*at)] if sending and there == (0, 0) else dst
        i = index[name]
        return remote(src, dst, ssem.at[i], rsem.at[i], link_to[link])

    started = set()

    def start_ready(have):
        order = {"Y": 0, "Z": 1, "YZ": 2, "ZY": 3}
        for name in sorted(plan, key=lambda n: (order[n[0]], abs(n[1]), str(n))):
            if name not in started and all(a in have for a in plan[name][4]):
                started.add(name)
                copy = f_copy(name, True)
                copy.start()
                sends.append(copy)

    def s_copy(kind, dz, sending):
        i = len(names) + DZ.index(dz) * 2 + (kind == "y")
        plane = core if sending else 1 - core
        ref = gath.at[plane, lax.rem(z + (NZ - dz), NZ), :, pl.ds(*PARTS[kind])]
        return remote(ref, ref, ssem.at[i], rsem.at[i], link_to["core"])

    need = {}
    for dz in DZ:
        zs = [] if dz == 0 else ([("Z", dz)] if dz != 4 else [("Z", 4, 1), ("Z", 4, -1)])
        need[("z", dz)] = zs + [("ZY", dz, s) for s in (1, -1, 2)]
        need[("y", dz)] = (
            [("Y", 1), ("Y", -1), ("Y", 2, 1), ("Y", 2, -1)]
            if dz == 0
            else [("YZ", dz, s) for s in (0, 1, -1, 2)]
        )

    def share(have):
        for key in list(need):
            if all(a in have for a in need[key]):
                copy = s_copy(*key, True)
                copy.start()
                sends.append(copy)
                del need[key]

    pl.semaphore_wait(barrier, len(link_to))
    have = set()
    start_ready(have)
    for name in (("r", 0), ("l", 1), ("r", 1), ("l", 0)):
        a_send(name)
    for d in (1, 2, 3):
        copy = c_copy(d)
        copy.start()
        sends.append(copy)
    keep = pltpu.make_async_copy(mine, gath.at[core, z, y], lsem.at[0])
    keep.start()

    per = ao_hbm.shape[1]

    def order_rows(lo, hi):
        def row(i, _):
            zero, one = tile(i, 0), tile(i, 1)
            tiles[0] = zero.astype(tiles.dtype)
            tiles[1] = one.astype(tiles.dtype)
            left_t[i, :T] = tiles[0].T
            left_t[i, T:] = tiles[1].T
            z32, z64, z96 = (pltpu.roll(zero, s, 1) for s in (32, 64, 96))
            o32, o64, o96 = (pltpu.roll(one, s, 1) for s in (32, 64, 96))
            low = jnp.where(lane < 32, zero, jnp.where(lane < 64, o32, jnp.where(lane < 96, z32, o64)))
            top = jnp.where(lane < 32, z64, jnp.where(lane < 64, o96, jnp.where(lane < 96, z96, one)))
            ordered[i, :, :T] = low.astype(ordered.dtype)
            ordered[i, :, T:] = top.astype(ordered.dtype)
            return 0

        lax.fori_loop(lo, hi, row, 0)

    def diag_rows(lo, hi):
        def row(i, _):
            for k in range(per):
                part = jnp.dot(left_t[i], ad_ref[i, k], preferred_element_type=jnp.float32)
                dacc[...] += jnp.dot(
                    part.astype(jnp.bfloat16), ordered[dcols_ref[k, i]], preferred_element_type=jnp.float32
                )
            return 0

        lax.fori_loop(lo, hi, row, 0)

    def left_rows(slot, part):
        def row(i, _):
            for k in range(per):
                left[slot, i, k] = jnp.dot(
                    left_t[i], a_all[slot, i, k], preferred_element_type=jnp.float32
                ).astype(left.dtype)
            return 0

        lax.fori_loop(part * half, part * half + half, row, 0)

    def d_copy(d):
        return remote(
            dsend.at[xat[d]], drecv.at[d - 1], xs_sem.at[8 + d], xr_sem.at[8 + d], link_to[d]
        )

    def send_diag():
        for q in range(4):
            at = slice((q // 2) * T, (q // 2 + 1) * T)
            zero, one = dacc[:T, at], dacc[T:, at]
            if q % 2 == 0:
                one = pltpu.roll(one, H, 1)
            else:
                zero = pltpu.roll(zero, H, 1)
            dsend[q] = jnp.where(lane < H, zero, one)
        for d in (1, 2, 3):
            copy = d_copy(d)
            copy.start()
            sends.append(copy)

    def a_take(name, then=None):
        a_copy(name, False).wait_recv()
        if then:
            a_send(then)

    def begin():
        dacc[...] = jnp.zeros_like(dacc)
        loads[1].wait()
        loads[2].wait()
        order_rows(0, rows)

    events = [(t, 1, name) for name, t in flood_order(plan).items()]
    steps = [
        (0.0, begin), (1.5, lambda: diag_rows(0, 2)), (3.5, lambda: diag_rows(2, 4)),
        (5.5, lambda: diag_rows(4, 6)), (7.5, lambda: diag_rows(6, 8)),
        (7.6, send_diag),
        (9.5, lambda: a_take(("r", 0), ("r", 2))), (9.6, lambda: a_take(("l", 1), ("l", 2))),
        (10.5, lambda: left_rows(0, 0)), (12.0, lambda: left_rows(0, 1)),
        (13.5, lambda: left_rows(1, 0)), (15.0, lambda: left_rows(3, 1)),
        (18.0, lambda: (a_take(("r", 1)), left_rows(1, 1))),
        (19.5, lambda: (a_take(("l", 0)), left_rows(3, 0))),
    ]
    events += [(t, 0, step) for t, step in steps]
    kept = False
    for _, kind, item in sorted(events, key=lambda e: (e[0], e[1], str(e[2]) if e[1] else "")):
        if kind == 0:
            item()
            continue
        f_copy(item, False).wait_recv()
        have.add(item)
        start_ready(have)
        if not kept:
            kept = True
            keep.wait()
        share(have)
    for name, part in ((("r", 2), 0), (("l", 2), 1)):
        a_take(name)
        left_rows(2, part)

    total = dsend[x]
    for d in (1, 2, 3):
        d_copy(d).wait_recv()
        total = total + drecv[d - 1]
        c_copy(d).wait_recv()
    own_ref[...] = total
    cols_ref[...] = ctab[...]

    for dz in DZ:
        for kind in ("z", "y"):
            s_copy(kind, dz, False).wait_recv()
    tail = gath[:, :, :, 4 * T :, :].reshape(2 * NZ * NY * 16, T)
    pick = (lax.broadcasted_iota(jnp.int32, (T, T), 0) == me).astype(jnp.bfloat16)
    spread = jnp.dot(tail, pick, preferred_element_type=jnp.float32).reshape(2 * NZ * NY, 16, T)
    line = lax.broadcasted_iota(jnp.int32, spread.shape, 1) == lax.broadcasted_iota(
        jnp.int32, spread.shape, 2
    )
    tbl_ref[...] = jnp.sum(jnp.where(line, spread, 0.0), axis=1).astype(jnp.int32)

    for copy in sends:
        copy.wait_send()


def gather_all(a_diag, diag_cols, a_offd, offd_cols, prolong, aggregate, send_rows):
    rows, per, _, _ = a_offd.shape
    vmem = pl.BlockSpec(memory_space=pltpu.VMEM)
    smem = pl.BlockSpec(memory_space=pltpu.SMEM)
    hbm = pl.BlockSpec(memory_space=pltpu.HBM)
    copies = len(flood_plan()) + 2 * len(DZ)
    bf16, f32 = jnp.bfloat16, jnp.float32
    return pl.pallas_call(
        gather_kernel,
        in_specs=[smem, smem, vmem, vmem, hbm, hbm, hbm],
        out_specs=[vmem, vmem, vmem, vmem, vmem],
        out_shape=[
            jax.ShapeDtypeStruct((2, NZ, NY, ROWS, T), bf16),
            jax.ShapeDtypeStruct((4, rows, per, 2 * T, T), bf16),
            jax.ShapeDtypeStruct((T, T), f32),
            jax.ShapeDtypeStruct((2 * NZ * NY, T), jnp.int32),
            jax.ShapeDtypeStruct((4, 8, T), jnp.int32),
        ],
        scratch_shapes=[
            pltpu.VMEM((rows, 2, T, T), bf16),
            pltpu.VMEM((rows, per, T, T), bf16),
            pltpu.VMEM((ROWS, T), bf16),
            pltpu.VMEM((16, T), f32),
            pltpu.VMEM((2, T, T), bf16),
            pltpu.VMEM((rows, T, 2 * T), bf16),
            pltpu.VMEM((rows, 2 * T, T), bf16),
            pltpu.VMEM((4, rows, per, T, T), bf16),
            pltpu.VMEM((2 * T, 2 * T), f32),
            pltpu.VMEM((4, T, T), f32),
            pltpu.VMEM((3, T, T), f32),
            pltpu.VMEM((4, 8, T), jnp.int32),
            pltpu.SemaphoreType.DMA((copies,)),
            pltpu.SemaphoreType.DMA((copies,)),
            pltpu.SemaphoreType.DMA((12,)),
            pltpu.SemaphoreType.DMA((12,)),
            pltpu.SemaphoreType.DMA((4,)),
        ],
        compiler_params=pltpu.CompilerParams(
            collective_id=0, has_side_effects=True, vmem_limit_bytes=32 << 20
        ),
        name="gather_all",
    )(
        *(
            pltpu.with_memory_space_constraint(item, pltpu.HBM)
            for item in (aggregate.T, diag_cols.T, offd_cols.T, send_rows[0].T, prolong, a_diag, a_offd)
        )
    )


def offd_kernel(me_ref, map_ref, tbl_ref, cols_ref, l_ref, gath_ref, d_ref, out_ref, acc):
    groups, rows, per, _, _ = l_ref.shape
    high = lax.broadcasted_iota(jnp.int32, (T, T), 1) >= H
    acc[...] = jnp.zeros_like(acc)

    def slot_of(node):
        return lax.rem(node, 2) * (NZ * NY) + node // 2

    def row(i, _):
        for t in range(groups * per):
            g, k = t // per, t % per
            col = cols_ref[g, k, i]
            slot = slot_of(col // 4)
            sent = tbl_ref[slot, lax.rem(col, 4)]
            odd = lax.rem(sent, 2) == 1
            right = gath_ref[slot, pl.ds(pl.multiple_of((sent // 2) * T, T), T), :]
            y = jnp.dot(l_ref[g, i, k], right, preferred_element_type=jnp.float32)
            kept = jnp.where(odd, y[T:], y[:T])
            moved = jnp.where(odd, y[:T], y[T:])
            acc[slot] += jnp.where(high == odd, kept, pltpu.roll(moved, H, 1))
        return 0

    lax.fori_loop(0, rows, row, 0, unroll=2)
    acc[slot_of(me_ref[0])] = d_ref[...]

    lane = lax.broadcasted_iota(jnp.int32, (T, T), 1)
    even = lax.rem(lane // 32, 2) == 0

    def pack(p, _):
        def part(j):
            gid = map_ref[2 * p + j]
            shift = lax.rem((j - lax.rem(gid, CR1)) * 32 + T, T)
            return pltpu.roll(acc[slot_of(gid // CR1)], shift, 1)

        both = jnp.where(even, part(0), part(1)).astype(out_ref.dtype)
        quarter = out_ref.shape[2]
        for g in range(out_ref.shape[0]):
            out_ref[g, p] = both[g * quarter : (g + 1) * quarter]
        return 0

    lax.fori_loop(0, out_ref.shape[1], pack, 0, unroll=7)


def offd_terms(me, col_map, table, cols, left, gathered, own):
    groups, rows, per, _, _ = left.shape
    nodes = gathered.shape[0]
    vmem = pl.BlockSpec(memory_space=pltpu.VMEM)
    smem = pl.BlockSpec(memory_space=pltpu.SMEM)
    return pl.pallas_call(
        offd_kernel,
        in_specs=[smem, smem, smem, smem, vmem, vmem, vmem],
        out_specs=vmem,
        out_shape=jax.ShapeDtypeStruct((groups, col_map.shape[0] // 2, T // groups, T), jnp.bfloat16),
        scratch_shapes=[pltpu.VMEM((nodes, T, T), jnp.float32)],
        compiler_params=pltpu.CompilerParams(vmem_limit_bytes=32 << 20),
        name="offd_terms",
    )(me, col_map, table, cols, left, gathered, own)


def swap_kernel(src, out, ssem, rsem, lsem):
    me = lax.axis_index("rows")
    x = lax.axis_index("grp")
    at = [lax.rem(x + d, 4) for d in range(4)]
    barrier = pltpu.get_barrier_semaphore()
    for d in (2, 1, 3):
        pl.semaphore_signal(barrier, inc=1, device_id=(me, at[d]), device_id_type=MESH)
    stay = pltpu.make_async_copy(src.at[x], out.at[x], lsem)
    stay.start()
    pl.semaphore_wait(barrier, 3)

    def remote(d, a, b):
        return pltpu.make_async_remote_copy(
            src_ref=a, dst_ref=b, send_sem=ssem.at[d - 1], recv_sem=rsem.at[d - 1],
            device_id=(me, at[d]), device_id_type=MESH,
        )

    for d in (2, 1, 3):
        remote(d, src.at[at[d]], out.at[x]).start()
    for d in (1, 3, 2):
        came = out.at[at[4 - d]]
        remote(d, came, came).wait_recv()
    stay.wait()
    for d in (1, 3, 2):
        remote(d, src.at[at[d]], out.at[x]).wait_send()


def swap_slices(src):
    vmem = pl.BlockSpec(memory_space=pltpu.VMEM)
    return pl.pallas_call(
        swap_kernel,
        in_specs=[vmem],
        out_specs=vmem,
        out_shape=jax.ShapeDtypeStruct(src.shape, src.dtype),
        scratch_shapes=[
            pltpu.SemaphoreType.DMA((3,)),
            pltpu.SemaphoreType.DMA((3,)),
            pltpu.SemaphoreType.DMA,
        ],
        compiler_params=pltpu.CompilerParams(
            collective_id=1, has_side_effects=True, vmem_limit_bytes=16 << 20
        ),
        name="swap_slices",
    )(src)


def place_kernel(x_ref, out_hbm, buf, sem):
    pairs, quarter = x_ref.shape[1], x_ref.shape[2]
    chunks = sem.shape[1]
    step = pairs // chunks

    def copies(n):
        at = pl.ds(2 * step * n, 2 * step)
        return [pltpu.make_async_copy(buf.at[r, at], out_hbm.at[r, at], sem.at[r, n]) for r in range(CR1)]

    row = lax.broadcasted_iota(jnp.int32, (4 * T, 4 * T), 0)
    col = lax.broadcasted_iota(jnp.int32, (4 * T, 4 * T), 1)
    move = (row % 32 == col % 32) & ((row // 32) % 4 == col // T) & (row // T == (col // 32) % 4)
    move = jnp.where(move, 1.0, 0.0).astype(jnp.bfloat16)
    for n in range(chunks):
        at = pl.ds(n * step, step)
        x = jnp.concatenate([x_ref[s, at].reshape(step * quarter, T) for s in range(4)], axis=1)
        o = jnp.dot(x, move, preferred_element_type=jnp.float32).astype(buf.dtype)
        for r in range(CR1):
            for j in range(2):
                piece = o[:, (r * 2 + j) * T : (r * 2 + j + 1) * T].reshape(step, quarter, T)
                for p in range(step):
                    buf[r, 2 * (n * step + p) + j] = piece[p]
        for copy in copies(n):
            copy.start()
    for n in range(chunks):
        for copy in copies(n):
            copy.wait()


def place_slots(arrived):
    groups, pairs, quarter, _ = arrived.shape
    shape = (CR1, 2 * pairs, quarter, T)
    return pl.pallas_call(
        place_kernel,
        in_specs=[pl.BlockSpec(memory_space=pltpu.VMEM)],
        out_specs=pl.BlockSpec(memory_space=pltpu.HBM),
        out_shape=jax.ShapeDtypeStruct(shape, jnp.bfloat16),
        scratch_shapes=[pltpu.VMEM(shape, jnp.bfloat16), pltpu.SemaphoreType.DMA((CR1, 7))],
        name="place_slots",
    )(arrived)


def per_device(
    a_diag, diag_cols, a_offd, offd_cols, prolong, aggregate, send_rows, ghost_agg, coarse_map
):
    me = lax.axis_index("rows").reshape(1)
    gathered, left, own, table, cols = gather_all(
        a_diag, diag_cols, a_offd, offd_cols, prolong, aggregate, send_rows
    )
    gathered = gathered.reshape(2 * NZ * NY, ROWS, T)
    offd = offd_terms(me, coarse_map[0], table, cols, left, gathered, own)
    return place_slots(swap_slices(offd))


def solution(mesh):
    in_specs = (
        P("rows", "grp", None, None),
        P("rows", "grp"),
        P("rows", "grp", None, None),
        P("rows", "grp"),
        P("rows", None, None, None),
        P("rows", None),
        P("rows", None, None),
        P("rows", None, None, None),
        P("rows", None),
    )
    out_specs = P("rows", None, "grp", None)
    return jax.shard_map(
        per_device, mesh=mesh, in_specs=in_specs, out_specs=out_specs, check_vma=False
    )
```

```python
import functools

import jax
import jax.numpy as jnp
from jax import lax
from jax.experimental import pallas as pl
from jax.experimental.pallas import tpu as pltpu
from jax.sharding import PartitionSpec as P

CR1 = 2
T = 128
H = T // 2


ROWS = 528
ZR = 320
NZ, NY = 8, 4
MESH = pl.DeviceIdType.MESH
PARTS = {"z": (0, ZR), "za": (0, ZR // 2), "zb": (ZR // 2, ZR // 2), "y": (ZR, ROWS - ZR)}
DZ = (0, 1, -1, 2, -2, 3, -3, 4)
LATE_UP = (0, 1, 2, 3)


def flood_plan():
    plan = {}

    def add(name, way, there, here, part, after):
        plan[name] = (way, there, here, part, tuple(after))

    for s in (1, -1):
        add(("Z", s), ("z", s), (0, 0), (s, 0), "z", [])
        add(("Z", 2 * s), ("z", 2 * s), (0, 0), (2 * s, 0), "z", [])
        add(("Z", 3 * s), ("z", s), (2 * s, 0), (3 * s, 0), "z", [("Z", 2 * s)])
        add(("Z", 4, s), ("z", 2 * s), (2 * s, 0), (4, 0), "za" if s == 1 else "zb", [("Z", 2 * s)])
        add(("Y", s), ("y", s), (0, 0), (0, s), "y", [])
    add(("Y", 2), ("y", 2), (0, 0), (0, 2), "y", [])
    for e in DZ:
        have = [] if e == 0 else ([("Z", e)] if e != 4 else [("Z", 4, 1), ("Z", 4, -1)])
        for s in (1, -1):
            add(("ZY", e, s), ("y", s), (e, 0), (e, s), "z", have)
        s = 1 if e in LATE_UP else -1
        add(("ZY", e, 2), ("y", s), (e, s), (e, 2), "z", [("ZY", e, s)])
    for s in (1, -1):
        for d in range(1, 5):
            for dy in (0, 1, -1, 2):
                if d == 4 and (dy in (0, 1)) != (s == 1):
                    continue
                if d > 1:
                    after = [("YZ", s * (d - 1), dy)]
                else:
                    after = [("Y", dy)] if dy else []
                here = s * d if d < 4 else 4
                add(("YZ", here, dy), ("z", s), (s * (d - 1), dy), (here, dy), "y", after)
    return plan


def flood_rank(plan):
    kids = {}
    for name, item in plan.items():
        for a in item[4]:
            kids.setdefault(a, []).append(name)
    memo = {}

    def depth(name):
        if name not in memo:
            memo[name] = 1 + max([depth(k) for k in kids.get(name, [])], default=0)
        return memo[name]

    kind = {"Y": 0, "Z": 1, "YZ": 2, "ZY": 3}
    return {n: (-depth(n), kind[n[0]], abs(n[1]), str(n)) for n in plan}


def flood_order(plan, latency=2.5, rate=49e3):
    rank = flood_rank(plan)
    free = {}
    arrive, waiting = {}, dict(plan)
    while waiting:
        best = None
        for name, ((axis, hop), _, _, part, after) in waiting.items():
            if any(a not in arrive for a in after):
                continue
            if axis == "y" and hop == 2:
                links = ((("y", 1), 1), (("y", -1), 1))
            else:
                links = (((axis, 1 if hop > 0 else -1), abs(hop)),)
            start = max([arrive[a] for a in after] + [free.get(link, 0.0) for link, _ in links])
            key = (start,) + rank[name]
            if best is None or key < best[0]:
                best = (key, name, start, links, PARTS[part][1] * 256 / rate)
        _, name, start, links, took = best
        for link, hops in links:
            free[link] = start + hops * took
        arrive[name] = start + took + latency
        del waiting[name]
    return arrive


def gather_kernel(
    agg_ref, dcols_ref, ocols_ref, srows_ref, p_hbm, ad_hbm, ao_hbm,
    gath, left, own_ref, tbl_ref, cols_ref,
    p_ref, ad_ref, mine, stage, tiles, ordered, left_t, a_all, dacc, dsend, drecv, ctab,
    ssem, rsem, xs_sem, xr_sem, lsem,
):
    me = lax.axis_index("rows")
    x = lax.axis_index("grp")
    core = lax.rem(me, 2)
    y = lax.rem(me // 2, NY)
    z = me // (2 * NY)

    def row_of(zz, yy, cc):
        return (zz * NY + yy) * 2 + cc

    xat = [lax.rem(x + d, 4) for d in range(4)]
    link_to = {("z", d): (row_of(lax.rem(z + (NZ + d), NZ), y, core), x) for d in (1, -1, 2, -2)}
    link_to.update({("y", d): (row_of(z, lax.rem(y + (NY + d), NY), core), x) for d in (1, -1, 2)})
    link_to["core"] = (row_of(z, y, 1 - core), x)
    link_to.update({d: (me, xat[d]) for d in (1, 2, 3)})
    barrier = pltpu.get_barrier_semaphore()
    for device in link_to.values():
        pl.semaphore_signal(barrier, inc=1, device_id=device, device_id_type=MESH)

    loads = [
        pltpu.make_async_copy(p_hbm, p_ref, lsem.at[1]),
        pltpu.make_async_copy(ao_hbm, a_all.at[0], lsem.at[2]),
        pltpu.make_async_copy(ad_hbm, ad_ref, lsem.at[3]),
    ]
    for load in loads:
        load.start()

    sends = []

    def remote(src, dst, s, r, device):
        return pltpu.make_async_remote_copy(
            src_ref=src, dst_ref=dst, send_sem=s, recv_sem=r, device_id=device, device_id_type=MESH
        )

    half = ao_hbm.shape[0] // 2

    def a_copy(d, part, sending):
        at = pl.ds(part * half, half)
        dst = a_all.at[d, at]
        i = 2 * (d - 1) + part
        return remote(ao_hbm.at[at] if sending else dst, dst, xs_sem.at[i], xr_sem.at[i], link_to[d])

    def c_copy(d):
        return remote(ctab.at[0], ctab.at[d], xs_sem.at[5 + d], xr_sem.at[5 + d], link_to[d])

    lane = lax.broadcasted_iota(jnp.int32, (T, T), 1)
    rows = p_hbm.shape[0]
    stage[...] = jnp.zeros_like(stage)
    stage[0 : srows_ref.shape[0], 0 : srows_ref.shape[1]] = srows_ref[...].astype(jnp.float32)
    ctab[0, 0 : ocols_ref.shape[0], 0 : ocols_ref.shape[1]] = ocols_ref[...]
    loads[0].wait()

    def tile(i, a):
        flip = agg_ref[0, i] == a
        return jnp.where(flip, p_ref[i, 0], p_ref[i, 1]).astype(jnp.float32)

    for p in range(rows // 2):
        pair = None
        for r in range(2):
            for a in range(2):
                at = r * 64 + a * 32
                moved = pltpu.roll(tile(2 * p + r, a), lax.rem(at + T - 32 * x, T), 1)
                pair = moved if pair is None else jnp.where(lane >= at, moved, pair)
        mine[p * T : (p + 1) * T, :] = pair.astype(mine.dtype)
    mine[4 * T :, :] = stage[...].astype(mine.dtype)

    plan = flood_plan()
    names = sorted(plan, key=str)
    index = {name: i for i, name in enumerate(names)}

    def block(offset, rows_at):
        dz, dy = offset
        return gath.at[core, lax.rem(z + (NZ - dz), NZ), lax.rem(y + (NY - dy), NY), pl.ds(*rows_at)]

    def f_copy(name, sending):
        link, there, here, part, _ = plan[name]
        at = PARTS[part]
        dst = block(there if sending else here, at)
        src = mine.at[pl.ds(*at)] if sending and there == (0, 0) else dst
        i = index[name]
        return remote(src, dst, ssem.at[i], rsem.at[i], link_to[link])

    started = set()

    rank = flood_rank(plan)

    def start_ready(have):
        for name in sorted(plan, key=rank.get):
            if name not in started and all(a in have for a in plan[name][4]):
                started.add(name)
                copy = f_copy(name, True)
                copy.start()
                sends.append(copy)

    def s_copy(kind, dz, sending):
        i = len(names) + DZ.index(dz) * 2 + (kind == "y")
        plane = core if sending else 1 - core
        ref = gath.at[plane, lax.rem(z + (NZ - dz), NZ), :, pl.ds(*PARTS[kind])]
        return remote(ref, ref, ssem.at[i], rsem.at[i], link_to["core"])

    need = {}
    for dz in DZ:
        zs = [] if dz == 0 else ([("Z", dz)] if dz != 4 else [("Z", 4, 1), ("Z", 4, -1)])
        need[("z", dz)] = zs + [("ZY", dz, s) for s in (1, -1, 2)]
        need[("y", dz)] = (
            [("Y", 1), ("Y", -1), ("Y", 2)]
            if dz == 0
            else [("YZ", dz, s) for s in (0, 1, -1, 2)]
        )

    def share(have):
        for key in list(need):
            if all(a in have for a in need[key]):
                copy = s_copy(*key, True)
                copy.start()
                sends.append(copy)
                del need[key]

    pl.semaphore_wait(barrier, len(link_to))
    have = set()
    start_ready(have)
    for d, part in ((1, 0), (3, 0), (2, 0), (2, 1), (1, 1), (3, 1)):
        copy = a_copy(d, part, True)
        copy.start()
        sends.append(copy)
    for d in (1, 2, 3):
        copy = c_copy(d)
        copy.start()
        sends.append(copy)
    keep = pltpu.make_async_copy(mine, gath.at[core, z, y], lsem.at[0])
    keep.start()

    per = ao_hbm.shape[1]

    def order_rows(lo, hi):
        def row(i, _):
            zero, one = tile(i, 0), tile(i, 1)
            tiles[0] = zero.astype(tiles.dtype)
            tiles[1] = one.astype(tiles.dtype)
            left_t[i, :T] = tiles[0].T
            left_t[i, T:] = tiles[1].T
            z32, z64, z96 = (pltpu.roll(zero, s, 1) for s in (32, 64, 96))
            o32, o64, o96 = (pltpu.roll(one, s, 1) for s in (32, 64, 96))
            low = jnp.where(lane < 32, zero, jnp.where(lane < 64, o32, jnp.where(lane < 96, z32, o64)))
            top = jnp.where(lane < 32, z64, jnp.where(lane < 64, o96, jnp.where(lane < 96, z96, one)))
            ordered[i, :, :T] = low.astype(ordered.dtype)
            ordered[i, :, T:] = top.astype(ordered.dtype)
            return 0

        lax.fori_loop(lo, hi, row, 0)

    def diag_rows(lo, hi):
        def row(i, _):
            for k in range(per):
                part = jnp.dot(left_t[i], ad_ref[i, k], preferred_element_type=jnp.float32)
                dacc[...] += jnp.dot(
                    part.astype(jnp.bfloat16), ordered[dcols_ref[k, i]], preferred_element_type=jnp.float32
                )
            return 0

        lax.fori_loop(lo, hi, row, 0)

    def left_rows(slot, part):
        def row(i, _):
            for k in range(per):
                left[slot, i, k] = jnp.dot(
                    left_t[i], a_all[slot, i, k], preferred_element_type=jnp.float32
                ).astype(left.dtype)
            return 0

        lax.fori_loop(part * half, part * half + half, row, 0)

    def d_copy(d):
        return remote(
            dsend.at[xat[d]], drecv.at[d - 1], xs_sem.at[8 + d], xr_sem.at[8 + d], link_to[d]
        )

    def send_diag():
        for q in range(4):
            at = slice((q // 2) * T, (q // 2 + 1) * T)
            zero, one = dacc[:T, at], dacc[T:, at]
            if q % 2 == 0:
                one = pltpu.roll(one, H, 1)
            else:
                zero = pltpu.roll(zero, H, 1)
            dsend[q] = jnp.where(lane < H, zero, one)
        for d in (1, 2, 3):
            copy = d_copy(d)
            copy.start()
            sends.append(copy)

    def a_take(d, part):
        a_copy(d, part, False).wait_recv()
        left_rows(d, part)

    def begin():
        dacc[...] = jnp.zeros_like(dacc)
        loads[1].wait()
        loads[2].wait()
        order_rows(0, rows)

    events = [(t, 1, name) for name, t in flood_order(plan).items()]
    steps = [
        (0.0, begin), (1.5, lambda: diag_rows(0, 2)), (3.5, lambda: diag_rows(2, 4)),
        (5.5, lambda: diag_rows(4, 6)), (7.5, lambda: diag_rows(6, 8)),
        (7.6, send_diag),
        (10.5, lambda: left_rows(0, 0)), (12.0, lambda: left_rows(0, 1)),
        (17.0, lambda: a_take(1, 0)), (19.0, lambda: a_take(3, 0)),
        (22.0, lambda: a_take(2, 0)), (24.0, lambda: a_take(2, 1)),
    ]
    events += [(t, 0, step) for t, step in steps]
    kept = False
    for _, kind, item in sorted(events, key=lambda e: (e[0], e[1], str(e[2]) if e[1] else "")):
        if kind == 0:
            item()
            continue
        f_copy(item, False).wait_recv()
        have.add(item)
        start_ready(have)
        if not kept:
            kept = True
            keep.wait()
        share(have)
    a_take(1, 1)
    a_take(3, 1)

    total = dsend[x]
    for d in (1, 2, 3):
        d_copy(d).wait_recv()
        total = total + drecv[d - 1]
        c_copy(d).wait_recv()
    own_ref[...] = total
    cols_ref[...] = ctab[...]

    for dz in DZ:
        for kind in ("z", "y"):
            s_copy(kind, dz, False).wait_recv()
    tail = gath[:, :, :, 4 * T :, :].reshape(2 * NZ * NY * 16, T)
    pick = (lax.broadcasted_iota(jnp.int32, (T, T), 0) == me).astype(jnp.bfloat16)
    spread = jnp.dot(tail, pick, preferred_element_type=jnp.float32).reshape(2 * NZ * NY, 16, T)
    line = lax.broadcasted_iota(jnp.int32, spread.shape, 1) == lax.broadcasted_iota(
        jnp.int32, spread.shape, 2
    )
    tbl_ref[...] = jnp.sum(jnp.where(line, spread, 0.0), axis=1).astype(jnp.int32)

    for copy in sends:
        copy.wait_send()


def gather_all(a_diag, diag_cols, a_offd, offd_cols, prolong, aggregate, send_rows):
    rows, per, _, _ = a_offd.shape
    vmem = pl.BlockSpec(memory_space=pltpu.VMEM)
    smem = pl.BlockSpec(memory_space=pltpu.SMEM)
    hbm = pl.BlockSpec(memory_space=pltpu.HBM)
    copies = len(flood_plan()) + 2 * len(DZ)
    bf16, f32 = jnp.bfloat16, jnp.float32
    return pl.pallas_call(
        gather_kernel,
        in_specs=[smem, smem, vmem, vmem, hbm, hbm, hbm],
        out_specs=[vmem, vmem, vmem, vmem, vmem],
        out_shape=[
            jax.ShapeDtypeStruct((2, NZ, NY, ROWS, T), bf16),
            jax.ShapeDtypeStruct((4, rows, per, 2 * T, T), bf16),
            jax.ShapeDtypeStruct((T, T), f32),
            jax.ShapeDtypeStruct((2 * NZ * NY, T), jnp.int32),
            jax.ShapeDtypeStruct((4, 8, T), jnp.int32),
        ],
        scratch_shapes=[
            pltpu.VMEM((rows, 2, T, T), bf16),
            pltpu.VMEM((rows, per, T, T), bf16),
            pltpu.VMEM((ROWS, T), bf16),
            pltpu.VMEM((16, T), f32),
            pltpu.VMEM((2, T, T), bf16),
            pltpu.VMEM((rows, T, 2 * T), bf16),
            pltpu.VMEM((rows, 2 * T, T), bf16),
            pltpu.VMEM((4, rows, per, T, T), bf16),
            pltpu.VMEM((2 * T, 2 * T), f32),
            pltpu.VMEM((4, T, T), f32),
            pltpu.VMEM((3, T, T), f32),
            pltpu.VMEM((4, 8, T), jnp.int32),
            pltpu.SemaphoreType.DMA((copies,)),
            pltpu.SemaphoreType.DMA((copies,)),
            pltpu.SemaphoreType.DMA((12,)),
            pltpu.SemaphoreType.DMA((12,)),
            pltpu.SemaphoreType.DMA((4,)),
        ],
        compiler_params=pltpu.CompilerParams(
            collective_id=0, has_side_effects=True, vmem_limit_bytes=32 << 20
        ),
        name="gather_all",
    )(
        *(
            pltpu.with_memory_space_constraint(item, pltpu.HBM)
            for item in (aggregate.T, diag_cols.T, offd_cols.T, send_rows[0].T, prolong, a_diag, a_offd)
        )
    )


def offd_kernel(me_ref, map_ref, tbl_ref, cols_ref, l_ref, gath_ref, d_ref, out_ref, acc):
    groups, rows, per, _, _ = l_ref.shape
    high = lax.broadcasted_iota(jnp.int32, (T, T), 1) >= H
    acc[...] = jnp.zeros_like(acc)

    def slot_of(node):
        return lax.rem(node, 2) * (NZ * NY) + node // 2

    def row(i, _):
        for t in range(groups * per):
            g, k = t // per, t % per
            col = cols_ref[g, k, i]
            slot = slot_of(col // 4)
            sent = tbl_ref[slot, lax.rem(col, 4)]
            odd = lax.rem(sent, 2) == 1
            right = gath_ref[slot, pl.ds(pl.multiple_of((sent // 2) * T, T), T), :]
            y = jnp.dot(l_ref[g, i, k], right, preferred_element_type=jnp.float32)
            kept = jnp.where(odd, y[T:], y[:T])
            moved = jnp.where(odd, y[:T], y[T:])
            acc[slot] += jnp.where(high == odd, kept, pltpu.roll(moved, H, 1))
        return 0

    lax.fori_loop(0, rows, row, 0, unroll=2)
    acc[slot_of(me_ref[0])] = d_ref[...]

    lane = lax.broadcasted_iota(jnp.int32, (T, T), 1)
    even = lax.rem(lane // 32, 2) == 0

    def pack(p, _):
        def part(j):
            gid = map_ref[2 * p + j]
            shift = lax.rem((j - lax.rem(gid, CR1)) * 32 + T, T)
            return pltpu.roll(acc[slot_of(gid // CR1)], shift, 1)

        both = jnp.where(even, part(0), part(1)).astype(out_ref.dtype)
        quarter = out_ref.shape[2]
        for g in range(out_ref.shape[0]):
            out_ref[g, p] = both[g * quarter : (g + 1) * quarter]
        return 0

    lax.fori_loop(0, out_ref.shape[1], pack, 0, unroll=7)


def offd_terms(me, col_map, table, cols, left, gathered, own):
    groups, rows, per, _, _ = left.shape
    nodes = gathered.shape[0]
    vmem = pl.BlockSpec(memory_space=pltpu.VMEM)
    smem = pl.BlockSpec(memory_space=pltpu.SMEM)
    return pl.pallas_call(
        offd_kernel,
        in_specs=[smem, smem, smem, smem, vmem, vmem, vmem],
        out_specs=vmem,
        out_shape=jax.ShapeDtypeStruct((groups, col_map.shape[0] // 2, T // groups, T), jnp.bfloat16),
        scratch_shapes=[pltpu.VMEM((nodes, T, T), jnp.float32)],
        compiler_params=pltpu.CompilerParams(vmem_limit_bytes=32 << 20),
        name="offd_terms",
    )(me, col_map, table, cols, left, gathered, own)


def swap_kernel(src, out, ssem, rsem, lsem):
    me = lax.axis_index("rows")
    x = lax.axis_index("grp")
    at = [lax.rem(x + d, 4) for d in range(4)]
    barrier = pltpu.get_barrier_semaphore()
    for d in (2, 1, 3):
        pl.semaphore_signal(barrier, inc=1, device_id=(me, at[d]), device_id_type=MESH)
    stay = pltpu.make_async_copy(src.at[x], out.at[x], lsem)
    stay.start()
    pl.semaphore_wait(barrier, 3)

    def remote(d, a, b):
        return pltpu.make_async_remote_copy(
            src_ref=a, dst_ref=b, send_sem=ssem.at[d - 1], recv_sem=rsem.at[d - 1],
            device_id=(me, at[d]), device_id_type=MESH,
        )

    for d in (2, 1, 3):
        remote(d, src.at[at[d]], out.at[x]).start()
    for d in (1, 3, 2):
        came = out.at[at[4 - d]]
        remote(d, came, came).wait_recv()
    stay.wait()
    for d in (1, 3, 2):
        remote(d, src.at[at[d]], out.at[x]).wait_send()


def swap_slices(src):
    vmem = pl.BlockSpec(memory_space=pltpu.VMEM)
    return pl.pallas_call(
        swap_kernel,
        in_specs=[vmem],
        out_specs=vmem,
        out_shape=jax.ShapeDtypeStruct(src.shape, src.dtype),
        scratch_shapes=[
            pltpu.SemaphoreType.DMA((3,)),
            pltpu.SemaphoreType.DMA((3,)),
            pltpu.SemaphoreType.DMA,
        ],
        compiler_params=pltpu.CompilerParams(
            collective_id=1, has_side_effects=True, vmem_limit_bytes=16 << 20
        ),
        name="swap_slices",
    )(src)


def place_kernel(x_ref, out_hbm, buf, sem):
    pairs, quarter = x_ref.shape[1], x_ref.shape[2]
    chunks = sem.shape[1]
    step = pairs // chunks

    def copies(n):
        at = pl.ds(2 * step * n, 2 * step)
        return [pltpu.make_async_copy(buf.at[r, at], out_hbm.at[r, at], sem.at[r, n]) for r in range(CR1)]

    row = lax.broadcasted_iota(jnp.int32, (4 * T, 4 * T), 0)
    col = lax.broadcasted_iota(jnp.int32, (4 * T, 4 * T), 1)
    move = (row % 32 == col % 32) & ((row // 32) % 4 == col // T) & (row // T == (col // 32) % 4)
    move = jnp.where(move, 1.0, 0.0).astype(jnp.bfloat16)
    for n in range(chunks):
        at = pl.ds(n * step, step)
        x = jnp.concatenate([x_ref[s, at].reshape(step * quarter, T) for s in range(4)], axis=1)
        o = jnp.dot(x, move, preferred_element_type=jnp.float32).astype(buf.dtype)
        for r in range(CR1):
            for j in range(2):
                piece = o[:, (r * 2 + j) * T : (r * 2 + j + 1) * T].reshape(step, quarter, T)
                for p in range(step):
                    buf[r, 2 * (n * step + p) + j] = piece[p]
        for copy in copies(n):
            copy.start()
    for n in range(chunks):
        for copy in copies(n):
            copy.wait()


def place_slots(arrived):
    groups, pairs, quarter, _ = arrived.shape
    shape = (CR1, 2 * pairs, quarter, T)
    return pl.pallas_call(
        place_kernel,
        in_specs=[pl.BlockSpec(memory_space=pltpu.VMEM)],
        out_specs=pl.BlockSpec(memory_space=pltpu.HBM),
        out_shape=jax.ShapeDtypeStruct(shape, jnp.bfloat16),
        scratch_shapes=[pltpu.VMEM(shape, jnp.bfloat16), pltpu.SemaphoreType.DMA((CR1, 7))],
        compiler_params=pltpu.CompilerParams(vmem_limit_bytes=16 << 20),
        name="place_slots",
    )(arrived)


def per_device(
    a_diag, diag_cols, a_offd, offd_cols, prolong, aggregate, send_rows, ghost_agg, coarse_map
):
    me = lax.axis_index("rows").reshape(1)
    gathered, left, own, table, cols = gather_all(
        a_diag, diag_cols, a_offd, offd_cols, prolong, aggregate, send_rows
    )
    gathered = gathered.reshape(2 * NZ * NY, ROWS, T)
    offd = offd_terms(me, coarse_map[0], table, cols, left, gathered, own)
    return place_slots(swap_slices(offd))


def solution(mesh):
    in_specs = (
        P("rows", "grp", None, None),
        P("rows", "grp"),
        P("rows", "grp", None, None),
        P("rows", "grp"),
        P("rows", None, None, None),
        P("rows", None),
        P("rows", None, None),
        P("rows", None, None, None),
        P("rows", None),
    )
    out_specs = P("rows", None, "grp", None)
    return jax.shard_map(
        per_device, mesh=mesh, in_specs=in_specs, out_specs=out_specs, check_vma=False
    )
```

```python
import functools

import jax
import jax.numpy as jnp
from jax import lax
from jax.experimental import pallas as pl
from jax.experimental.pallas import tpu as pltpu
from jax.sharding import PartitionSpec as P

CR1 = 2
T = 128
H = T // 2


ROWS = 528
ZR = 320
NZ, NY = 8, 4
MESH = pl.DeviceIdType.MESH
PARTS = {"z": (0, ZR), "za": (0, ZR // 2), "zb": (ZR // 2, ZR // 2),
         "y": (ZR, ROWS - ZR), "ya": (ZR, 112), "yb": (ZR + 112, ROWS - ZR - 112)}
DZ = (0, 1, -1, 2, -2, 3, -3, 4)
LATE_UP = (0, 1, 2, 3)


def flood_plan():
    plan = {}

    def add(name, link, there, here, part, after):
        plan[name] = (link, there, here, part, tuple(after))

    for sign, link in ((1, "z+"), (-1, "z-")):
        for d in range(1, 5):
            part = "z" if d < 4 else ("za" if sign == 1 else "zb")
            after = [] if d == 1 else [("Z", sign * (d - 1))]
            here = sign * d if d < 4 else 4
            name = ("Z", here) if d < 4 else ("Z", 4, sign)
            add(name, link, (sign * (d - 1), 0), (here, 0), part, after)
    for e in DZ:
        have = [] if e == 0 else ([("Z", e)] if e != 4 else [("Z", 4, 1), ("Z", 4, -1)])
        for sign, link in ((1, "y+"), (-1, "y-")):
            add(("ZY", e, sign), link, (e, 0), (e, sign), "z", have)
        sign = 1 if e in LATE_UP else -1
        add(("ZY", e, 2), "y+" if sign == 1 else "y-", (e, sign), (e, 2), "z", [("ZY", e, sign)])
    for sign, link in ((1, "y+"), (-1, "y-")):
        add(("Y", sign), link, (0, 0), (0, sign), "y", [])
        add(("Y", 2, sign), link, (0, sign), (0, 2), "ya" if sign == 1 else "yb", [("Y", sign)])
    for sign, link in ((1, "z+"), (-1, "z-")):
        for d in range(1, 5):
            for dy in (0, 1, -1, 2):
                if d == 4 and (dy in (0, 1)) != (sign == 1):
                    continue
                if d > 1:
                    after = [("YZ", sign * (d - 1), dy)]
                elif dy == 0:
                    after = []
                else:
                    after = [("Y", dy)] if dy != 2 else [("Y", 2, 1), ("Y", 2, -1)]
                here = sign * d if d < 4 else 4
                add(("YZ", here, dy), link, (sign * (d - 1), dy), (here, dy), "y", after)
    return plan


def flood_order(plan):
    free = {}
    arrive, waiting = {}, dict(plan)
    rank = {"Y": 0, "Z": 1, "YZ": 2, "ZY": 3}
    while len(arrive) < len(plan):
        best = None
        for name, (link, _, _, part, after) in waiting.items():
            if any(a not in arrive for a in after):
                continue
            start = max([arrive[a] for a in after] + [free.get(link, 0.0)])
            key = (start, rank[name[0]], abs(name[1]), str(name))
            if best is None or key < best[0]:
                best = (key, name, start, link, part)
        _, name, start, link, part = best
        end = start + PARTS[part][1] * 256 / 50e3
        free[link] = end
        arrive[name] = end + 1.5
        del waiting[name]
    return arrive


def gather_kernel(
    agg_ref, dcols_ref, ocols_ref, srows_ref, p_hbm, ad_hbm, ao_hbm,
    gath, left, own_ref, tbl_ref, cols_ref,
    p_ref, ad_ref, mine, stage, tiles, ordered, left_t, a_all, dacc, dsend, drecv, ctab,
    ssem, rsem, xs_sem, xr_sem, lsem,
):
    me = lax.axis_index("rows")
    x = lax.axis_index("grp")
    core = lax.rem(me, 2)
    y = lax.rem(me // 2, NY)
    z = me // (2 * NY)

    def row_of(zz, yy, cc):
        return (zz * NY + yy) * 2 + cc

    up_z, dn_z = lax.rem(z + 1, NZ), lax.rem(z + NZ - 1, NZ)
    up_y, dn_y = lax.rem(y + 1, NY), lax.rem(y + NY - 1, NY)
    xat = [lax.rem(x + d, 4) for d in range(4)]
    link_to = {
        "z+": (row_of(up_z, y, core), x),
        "z-": (row_of(dn_z, y, core), x),
        "y+": (row_of(z, up_y, core), x),
        "y-": (row_of(z, dn_y, core), x),
        "core": (row_of(z, y, 1 - core), x),
        1: (me, xat[1]),
        2: (me, xat[2]),
        3: (me, xat[3]),
    }
    barrier = pltpu.get_barrier_semaphore()
    for device in link_to.values():
        pl.semaphore_signal(barrier, inc=1, device_id=device, device_id_type=MESH)

    loads = [
        pltpu.make_async_copy(p_hbm, p_ref, lsem.at[1]),
        pltpu.make_async_copy(ao_hbm, a_all.at[0], lsem.at[2]),
        pltpu.make_async_copy(ad_hbm, ad_ref, lsem.at[3]),
    ]
    for load in loads:
        load.start()

    sends = []

    def remote(src, dst, s, r, device):
        return pltpu.make_async_remote_copy(
            src_ref=src, dst_ref=dst, send_sem=s, recv_sem=r, device_id=device, device_id_type=MESH
        )

    half = ao_hbm.shape[0] // 2
    first, second = pl.ds(0, half), pl.ds(half, half)
    a_plan = {
        ("r", 0): (0, 1, first, 1), ("r", 1): (0, 1, second, 1), ("r", 2): (1, 2, first, 1),
        ("l", 1): (0, 3, second, 3), ("l", 0): (0, 3, first, 3), ("l", 2): (3, 2, second, 3),
    }
    a_index = {name: i for i, name in enumerate(a_plan)}

    def a_copy(name, sending):
        src_slot, dst_slot, part, to = a_plan[name]
        dst = a_all.at[dst_slot, part]
        src = (ao_hbm if src_slot == 0 else a_all.at[src_slot]).at[part] if sending else dst
        i = a_index[name]
        return remote(src, dst, xs_sem.at[i], xr_sem.at[i], link_to[to])

    def a_send(name):
        copy = a_copy(name, True)
        copy.start()
        sends.append(copy)

    def c_copy(d):
        return remote(ctab.at[0], ctab.at[d], xs_sem.at[5 + d], xr_sem.at[5 + d], link_to[d])

    lane = lax.broadcasted_iota(jnp.int32, (T, T), 1)
    rows = p_hbm.shape[0]
    stage[...] = jnp.zeros_like(stage)
    stage[0 : srows_ref.shape[0], 0 : srows_ref.shape[1]] = srows_ref[...].astype(jnp.float32)
    ctab[0, 0 : ocols_ref.shape[0], 0 : ocols_ref.shape[1]] = ocols_ref[...]
    pl.semaphore_wait(barrier, len(link_to))
    for name in (("r", 0), ("l", 1), ("r", 1), ("l", 0)):
        a_send(name)
    loads[0].wait()

    def tile(i, a):
        flip = agg_ref[0, i] == a
        return jnp.where(flip, p_ref[i, 0], p_ref[i, 1]).astype(jnp.float32)

    for p in range(rows // 2):
        pair = None
        for r in range(2):
            for a in range(2):
                at = r * 64 + a * 32
                moved = pltpu.roll(tile(2 * p + r, a), lax.rem(at + T - 32 * x, T), 1)
                pair = moved if pair is None else jnp.where(lane >= at, moved, pair)
        mine[p * T : (p + 1) * T, :] = pair.astype(mine.dtype)
    mine[4 * T :, :] = stage[...].astype(mine.dtype)

    plan = flood_plan()
    names = sorted(plan, key=str)
    index = {name: i for i, name in enumerate(names)}

    def block(offset, rows_at):
        dz, dy = offset
        return gath.at[core, lax.rem(z + (NZ - dz), NZ), lax.rem(y + (NY - dy), NY), pl.ds(*rows_at)]

    def f_copy(name, sending):
        link, there, here, part, _ = plan[name]
        at = PARTS[part]
        dst = block(there if sending else here, at)
        src = mine.at[pl.ds(*at)] if sending and there == (0, 0) else dst
        i = index[name]
        return remote(src, dst, ssem.at[i], rsem.at[i], link_to[link])

    started = set()

    def start_ready(have):
        order = {"Y": 0, "Z": 1, "YZ": 2, "ZY": 3}
        for name in sorted(plan, key=lambda n: (order[n[0]], abs(n[1]), str(n))):
            if name not in started and all(a in have for a in plan[name][4]):
                started.add(name)
                copy = f_copy(name, True)
                copy.start()
                sends.append(copy)

    def s_copy(kind, dz, sending):
        i = len(names) + DZ.index(dz) * 2 + (kind == "y")
        plane = core if sending else 1 - core
        ref = gath.at[plane, lax.rem(z + (NZ - dz), NZ), :, pl.ds(*PARTS[kind])]
        return remote(ref, ref, ssem.at[i], rsem.at[i], link_to["core"])

    need = {}
    for dz in DZ:
        zs = [] if dz == 0 else ([("Z", dz)] if dz != 4 else [("Z", 4, 1), ("Z", 4, -1)])
        need[("z", dz)] = zs + [("ZY", dz, s) for s in (1, -1, 2)]
        need[("y", dz)] = (
            [("Y", 1), ("Y", -1), ("Y", 2, 1), ("Y", 2, -1)]
            if dz == 0
            else [("YZ", dz, s) for s in (0, 1, -1, 2)]
        )

    def share(have):
        for key in list(need):
            if all(a in have for a in need[key]):
                copy = s_copy(*key, True)
                copy.start()
                sends.append(copy)
                del need[key]

    have = set()
    start_ready(have)
    for d in (1, 2, 3):
        copy = c_copy(d)
        copy.start()
        sends.append(copy)
    keep = pltpu.make_async_copy(mine, gath.at[core, z, y], lsem.at[0])
    keep.start()

    per = ao_hbm.shape[1]

    def order_rows(lo, hi):
        def row(i, _):
            zero, one = tile(i, 0), tile(i, 1)
            tiles[0] = zero.astype(tiles.dtype)
            tiles[1] = one.astype(tiles.dtype)
            left_t[i, :T] = tiles[0].T
            left_t[i, T:] = tiles[1].T
            z32, z64, z96 = (pltpu.roll(zero, s, 1) for s in (32, 64, 96))
            o32, o64, o96 = (pltpu.roll(one, s, 1) for s in (32, 64, 96))
            low = jnp.where(lane < 32, zero, jnp.where(lane < 64, o32, jnp.where(lane < 96, z32, o64)))
            top = jnp.where(lane < 32, z64, jnp.where(lane < 64, o96, jnp.where(lane < 96, z96, one)))
            ordered[i, :, :T] = low.astype(ordered.dtype)
            ordered[i, :, T:] = top.astype(ordered.dtype)
            return 0

        lax.fori_loop(lo, hi, row, 0)

    def diag_rows(lo, hi):
        def row(i, _):
            for k in range(per):
                part = jnp.dot(left_t[i], ad_ref[i, k], preferred_element_type=jnp.float32)
                dacc[...] += jnp.dot(
                    part.astype(jnp.bfloat16), ordered[dcols_ref[k, i]], preferred_element_type=jnp.float32
                )
            return 0

        lax.fori_loop(lo, hi, row, 0)

    def left_rows(slot, part):
        def row(i, _):
            for k in range(per):
                left[slot, i, k] = jnp.dot(
                    left_t[i], a_all[slot, i, k], preferred_element_type=jnp.float32
                ).astype(left.dtype)
            return 0

        lax.fori_loop(part * half, part * half + half, row, 0)

    def d_copy(d):
        return remote(
            dsend.at[xat[d]], drecv.at[d - 1], xs_sem.at[8 + d], xr_sem.at[8 + d], link_to[d]
        )

    def send_diag():
        for q in range(4):
            at = slice((q // 2) * T, (q // 2 + 1) * T)
            zero, one = dacc[:T, at], dacc[T:, at]
            if q % 2 == 0:
                one = pltpu.roll(one, H, 1)
            else:
                zero = pltpu.roll(zero, H, 1)
            dsend[q] = jnp.where(lane < H, zero, one)
        for d in (1, 2, 3):
            copy = d_copy(d)
            copy.start()
            sends.append(copy)

    def a_take(name, then=None):
        a_copy(name, False).wait_recv()
        if then:
            a_send(then)

    def begin():
        dacc[...] = jnp.zeros_like(dacc)
        loads[1].wait()
        loads[2].wait()
        order_rows(0, rows)

    events = [(t, 1, name) for name, t in flood_order(plan).items()]
    steps = [
        (0.0, begin), (1.5, lambda: diag_rows(0, 2)), (3.5, lambda: diag_rows(2, 4)),
        (5.5, lambda: diag_rows(4, 6)), (7.5, lambda: diag_rows(6, 8)),
        (7.6, send_diag),
        (9.5, lambda: a_take(("r", 0), ("r", 2))), (9.6, lambda: a_take(("l", 1), ("l", 2))),
        (10.5, lambda: left_rows(0, 0)), (12.0, lambda: left_rows(0, 1)),
        (13.5, lambda: left_rows(1, 0)), (15.0, lambda: left_rows(3, 1)),
        (18.0, lambda: (a_take(("r", 1)), left_rows(1, 1))),
        (19.5, lambda: (a_take(("l", 0)), left_rows(3, 0))),
    ]
    events += [(t, 0, step) for t, step in steps]
    kept = False
    for _, kind, item in sorted(events, key=lambda e: (e[0], e[1], str(e[2]) if e[1] else "")):
        if kind == 0:
            item()
            continue
        f_copy(item, False).wait_recv()
        have.add(item)
        start_ready(have)
        if not kept:
            kept = True
            keep.wait()
        share(have)
    for name, part in ((("r", 2), 0), (("l", 2), 1)):
        a_take(name)
        left_rows(2, part)

    total = dsend[x]
    for d in (1, 2, 3):
        d_copy(d).wait_recv()
        total = total + drecv[d - 1]
        c_copy(d).wait_recv()
    own_ref[...] = total
    cols_ref[...] = ctab[...]

    for dz in DZ:
        for kind in ("z", "y"):
            s_copy(kind, dz, False).wait_recv()
    tail = gath[:, :, :, 4 * T :, :].reshape(2 * NZ * NY * 16, T)
    pick = (lax.broadcasted_iota(jnp.int32, (T, T), 0) == me).astype(jnp.bfloat16)
    spread = jnp.dot(tail, pick, preferred_element_type=jnp.float32).reshape(2 * NZ * NY, 16, T)
    line = lax.broadcasted_iota(jnp.int32, spread.shape, 1) == lax.broadcasted_iota(
        jnp.int32, spread.shape, 2
    )
    tbl_ref[...] = jnp.sum(jnp.where(line, spread, 0.0), axis=1).astype(jnp.int32)

    for copy in sends:
        copy.wait_send()


def gather_all(a_diag, diag_cols, a_offd, offd_cols, prolong, aggregate, send_rows):
    rows, per, _, _ = a_offd.shape
    vmem = pl.BlockSpec(memory_space=pltpu.VMEM)
    smem = pl.BlockSpec(memory_space=pltpu.SMEM)
    hbm = pl.BlockSpec(memory_space=pltpu.HBM)
    copies = len(flood_plan()) + 2 * len(DZ)
    bf16, f32 = jnp.bfloat16, jnp.float32
    return pl.pallas_call(
        gather_kernel,
        in_specs=[smem, smem, vmem, vmem, hbm, hbm, hbm],
        out_specs=[vmem, vmem, vmem, vmem, vmem],
        out_shape=[
            jax.ShapeDtypeStruct((2, NZ, NY, ROWS, T), bf16),
            jax.ShapeDtypeStruct((4, rows, per, 2 * T, T), bf16),
            jax.ShapeDtypeStruct((T, T), f32),
            jax.ShapeDtypeStruct((2 * NZ * NY, T), jnp.int32),
            jax.ShapeDtypeStruct((4, 8, T), jnp.int32),
        ],
        scratch_shapes=[
            pltpu.VMEM((rows, 2, T, T), bf16),
            pltpu.VMEM((rows, per, T, T), bf16),
            pltpu.VMEM((ROWS, T), bf16),
            pltpu.VMEM((16, T), f32),
            pltpu.VMEM((2, T, T), bf16),
            pltpu.VMEM((rows, T, 2 * T), bf16),
            pltpu.VMEM((rows, 2 * T, T), bf16),
            pltpu.VMEM((4, rows, per, T, T), bf16),
            pltpu.VMEM((2 * T, 2 * T), f32),
            pltpu.VMEM((4, T, T), f32),
            pltpu.VMEM((3, T, T), f32),
            pltpu.VMEM((4, 8, T), jnp.int32),
            pltpu.SemaphoreType.DMA((copies,)),
            pltpu.SemaphoreType.DMA((copies,)),
            pltpu.SemaphoreType.DMA((12,)),
            pltpu.SemaphoreType.DMA((12,)),
            pltpu.SemaphoreType.DMA((4,)),
        ],
        compiler_params=pltpu.CompilerParams(
            collective_id=0, has_side_effects=True, vmem_limit_bytes=32 << 20
        ),
        name="gather_all",
    )(
        *(
            pltpu.with_memory_space_constraint(item, pltpu.HBM)
            for item in (aggregate.T, diag_cols.T, offd_cols.T, send_rows[0].T, prolong, a_diag, a_offd)
        )
    )


def slot_of(node):
    return lax.rem(node, 2) * (NZ * NY) + node // 2


def offd_kernel(me_ref, tbl_ref, cols_ref, l_ref, gath_ref, d_ref, acc):
    groups, rows, per, _, _ = l_ref.shape
    high = lax.broadcasted_iota(jnp.int32, (T, T), 1) >= H
    acc[...] = jnp.zeros_like(acc)

    def row(i, _):
        for t in range(groups * per):
            g, k = t // per, t % per
            col = cols_ref[g, k, i]
            slot = slot_of(col // 4)
            sent = tbl_ref[slot, lax.rem(col, 4)]
            odd = lax.rem(sent, 2) == 1
            right = gath_ref[slot, pl.ds(pl.multiple_of((sent // 2) * T, T), T), :]
            y = jnp.dot(l_ref[g, i, k], right, preferred_element_type=jnp.float32)
            kept = jnp.where(odd, y[T:], y[:T])
            moved = jnp.where(odd, y[:T], y[T:])
            acc[slot] += jnp.where(high == odd, kept, pltpu.roll(moved, H, 1))
        return 0

    lax.fori_loop(0, rows, row, 0, unroll=2)
    acc[slot_of(me_ref[0])] = d_ref[...]


def offd_terms(me, table, cols, left, gathered, own):
    vmem = pl.BlockSpec(memory_space=pltpu.VMEM)
    smem = pl.BlockSpec(memory_space=pltpu.SMEM)
    return pl.pallas_call(
        offd_kernel,
        in_specs=[smem, smem, smem, vmem, vmem, vmem],
        out_specs=vmem,
        out_shape=jax.ShapeDtypeStruct((gathered.shape[0], T, T), jnp.float32),
        compiler_params=pltpu.CompilerParams(vmem_limit_bytes=32 << 20),
        name="offd_terms",
    )(me, table, cols, left, gathered, own)


def swap_kernel(map_ref, acc, out, src, ssem, rsem, lsem):
    me = lax.axis_index("rows")
    x = lax.axis_index("grp")
    at = [lax.rem(x + d, 4) for d in range(4)]
    barrier = pltpu.get_barrier_semaphore()
    for d in (2, 1, 3):
        pl.semaphore_signal(barrier, inc=1, device_id=(me, at[d]), device_id_type=MESH)
    pairs, quarter = src.shape[1], src.shape[2]
    chunks = ssem.shape[1]
    step = pairs // chunks

    lane = lax.broadcasted_iota(jnp.int32, (T, T), 1)
    even = lax.rem(lane // 32, 2) == 0

    def pack(p):
        def part(j):
            gid = map_ref[2 * p + j]
            value = acc[slot_of(gid // CR1)]
            return jnp.where(lax.rem(gid, CR1) == j, value, pltpu.roll(value, 32 if j else T - 32, 1))

        both = jnp.where(even, part(0), part(1)).astype(src.dtype)
        for g in range(src.shape[0]):
            src[g, p] = both[g * quarter : (g + 1) * quarter]

    def remote(d, c, a, b):
        piece = pl.ds(c * step, step)
        return pltpu.make_async_remote_copy(
            src_ref=a.at[piece], dst_ref=b.at[piece],
            send_sem=ssem.at[d - 1, c], recv_sem=rsem.at[d - 1, c],
            device_id=(me, at[d]), device_id_type=MESH,
        )

    for c in range(chunks):
        for p in range(c * step, (c + 1) * step):
            pack(p)
        if c == 0:
            pl.semaphore_wait(barrier, 3)
        for d in (2, 1, 3):
            remote(d, c, src.at[at[d]], out.at[x]).start()
    stay = pltpu.make_async_copy(src.at[x], out.at[x], lsem)
    stay.start()
    for c in range(chunks):
        for d in (1, 3, 2):
            came = out.at[at[4 - d]]
            remote(d, c, came, came).wait_recv()
    stay.wait()
    for c in range(chunks):
        for d in (1, 3, 2):
            remote(d, c, src.at[at[d]], out.at[x]).wait_send()


def swap_slices(col_map, sums):
    vmem = pl.BlockSpec(memory_space=pltpu.VMEM)
    shape = (4, col_map.shape[0] // 2, T // 4, T)
    chunks = 7
    return pl.pallas_call(
        swap_kernel,
        in_specs=[pl.BlockSpec(memory_space=pltpu.SMEM), vmem],
        out_specs=vmem,
        out_shape=jax.ShapeDtypeStruct(shape, jnp.bfloat16),
        scratch_shapes=[
            pltpu.VMEM(shape, jnp.bfloat16),
            pltpu.SemaphoreType.DMA((3, chunks)),
            pltpu.SemaphoreType.DMA((3, chunks)),
            pltpu.SemaphoreType.DMA,
        ],
        compiler_params=pltpu.CompilerParams(
            collective_id=1, has_side_effects=True, vmem_limit_bytes=16 << 20
        ),
        name="swap_slices",
    )(col_map, sums)


def place_kernel(x_ref, out_hbm, buf, sem):
    pairs, quarter = x_ref.shape[1], x_ref.shape[2]
    chunks = sem.shape[1]
    step = pairs // chunks

    def copies(n):
        at = pl.ds(2 * step * n, 2 * step)
        return [pltpu.make_async_copy(buf.at[r, at], out_hbm.at[r, at], sem.at[r, n]) for r in range(CR1)]

    row = lax.broadcasted_iota(jnp.int32, (4 * T, 4 * T), 0)
    col = lax.broadcasted_iota(jnp.int32, (4 * T, 4 * T), 1)
    move = (row % 32 == col % 32) & ((row // 32) % 4 == col // T) & (row // T == (col // 32) % 4)
    move = jnp.where(move, 1.0, 0.0).astype(jnp.bfloat16)
    for n in range(chunks):
        at = pl.ds(n * step, step)
        x = jnp.concatenate([x_ref[s, at].reshape(step * quarter, T) for s in range(4)], axis=1)
        o = jnp.dot(x, move, preferred_element_type=jnp.float32).astype(buf.dtype)
        for r in range(CR1):
            for j in range(2):
                piece = o[:, (r * 2 + j) * T : (r * 2 + j + 1) * T].reshape(step, quarter, T)
                for p in range(step):
                    buf[r, 2 * (n * step + p) + j] = piece[p]
        for copy in copies(n):
            copy.start()
    for n in range(chunks):
        for copy in copies(n):
            copy.wait()


def place_slots(arrived):
    groups, pairs, quarter, _ = arrived.shape
    shape = (CR1, 2 * pairs, quarter, T)
    return pl.pallas_call(
        place_kernel,
        in_specs=[pl.BlockSpec(memory_space=pltpu.VMEM)],
        out_specs=pl.BlockSpec(memory_space=pltpu.HBM),
        out_shape=jax.ShapeDtypeStruct(shape, jnp.bfloat16),
        scratch_shapes=[pltpu.VMEM(shape, jnp.bfloat16), pltpu.SemaphoreType.DMA((CR1, 7))],
        compiler_params=pltpu.CompilerParams(vmem_limit_bytes=16 << 20),
        name="place_slots",
    )(arrived)


def per_device(
    a_diag, diag_cols, a_offd, offd_cols, prolong, aggregate, send_rows, ghost_agg, coarse_map
):
    me = lax.axis_index("rows").reshape(1)
    gathered, left, own, table, cols = gather_all(
        a_diag, diag_cols, a_offd, offd_cols, prolong, aggregate, send_rows
    )
    gathered = gathered.reshape(2 * NZ * NY, ROWS, T)
    sums = offd_terms(me, table, cols, left, gathered, own)
    return place_slots(swap_slices(coarse_map[0], sums))


def solution(mesh):
    in_specs = (
        P("rows", "grp", None, None),
        P("rows", "grp"),
        P("rows", "grp", None, None),
        P("rows", "grp"),
        P("rows", None, None, None),
        P("rows", None),
        P("rows", None, None),
        P("rows", None, None, None),
        P("rows", None),
    )
    out_specs = P("rows", None, "grp", None)
    return jax.shard_map(
        per_device, mesh=mesh, in_specs=in_specs, out_specs=out_specs, check_vma=False
    )
```

```python
import functools

import jax
import jax.numpy as jnp
from jax import lax
from jax.experimental import pallas as pl
from jax.experimental.pallas import tpu as pltpu
from jax.sharding import PartitionSpec as P

CR1 = 2
T = 128


ROWS = 528
ZR = 320
NZ, NY = 8, 4
MESH = pl.DeviceIdType.MESH
PARTS = {"z": (0, ZR), "za": (0, ZR // 2), "zb": (ZR // 2, ZR // 2),
         "y": (ZR, ROWS - ZR), "ya": (ZR, 112), "yb": (ZR + 112, ROWS - ZR - 112)}
DZ = (0, 1, -1, 2, -2, 3, -3, 4)
LATE_UP = (0, 1, 2, 3)


def flood_plan():
    plan = {}

    def add(name, link, there, here, part, after):
        plan[name] = (link, there, here, part, tuple(after))

    for sign, link in ((1, "z+"), (-1, "z-")):
        for d in range(1, 5):
            part = "z" if d < 4 else ("za" if sign == 1 else "zb")
            after = [] if d == 1 else [("Z", sign * (d - 1))]
            here = sign * d if d < 4 else 4
            name = ("Z", here) if d < 4 else ("Z", 4, sign)
            add(name, link, (sign * (d - 1), 0), (here, 0), part, after)
    for e in DZ:
        have = [] if e == 0 else ([("Z", e)] if e != 4 else [("Z", 4, 1), ("Z", 4, -1)])
        for sign, link in ((1, "y+"), (-1, "y-")):
            add(("ZY", e, sign), link, (e, 0), (e, sign), "z", have)
        sign = 1 if e in LATE_UP else -1
        add(("ZY", e, 2), "y+" if sign == 1 else "y-", (e, sign), (e, 2), "z", [("ZY", e, sign)])
    for sign, link in ((1, "y+"), (-1, "y-")):
        add(("Y", sign), link, (0, 0), (0, sign), "y", [])
        add(("Y", 2, sign), link, (0, sign), (0, 2), "ya" if sign == 1 else "yb", [("Y", sign)])
    for sign, link in ((1, "z+"), (-1, "z-")):
        for d in range(1, 5):
            for dy in (0, 1, -1, 2):
                if d == 4 and (dy in (0, 1)) != (sign == 1):
                    continue
                if d > 1:
                    after = [("YZ", sign * (d - 1), dy)]
                elif dy == 0:
                    after = []
                else:
                    after = [("Y", dy)] if dy != 2 else [("Y", 2, 1), ("Y", 2, -1)]
                here = sign * d if d < 4 else 4
                add(("YZ", here, dy), link, (sign * (d - 1), dy), (here, dy), "y", after)
    return plan


def flood_order(plan):
    free = {}
    arrive, waiting = {}, dict(plan)
    rank = {"Y": 0, "Z": 1, "YZ": 2, "ZY": 3}
    while len(arrive) < len(plan):
        best = None
        for name, (link, _, _, part, after) in waiting.items():
            if any(a not in arrive for a in after):
                continue
            start = max([arrive[a] for a in after] + [free.get(link, 0.0)])
            key = (start, rank[name[0]], abs(name[1]), str(name))
            if best is None or key < best[0]:
                best = (key, name, start, link, part)
        _, name, start, link, part = best
        end = start + PARTS[part][1] * 256 / 50e3
        free[link] = end
        arrive[name] = end + 1.5
        del waiting[name]
    return arrive


def gather_kernel(
    agg_ref, dcols_ref, ocols_ref, srows_ref, p_hbm, ad_hbm, ao_hbm,
    gath, left, own_ref, tbl_ref, cols_ref,
    p_ref, ad_ref, mine, stage, ordered, right_t, a_all, dacc, drecv, ctab,
    ssem, rsem, xs_sem, xr_sem, lsem,
):
    me = lax.axis_index("rows")
    x = lax.axis_index("grp")
    core = lax.rem(me, 2)
    y = lax.rem(me // 2, NY)
    z = me // (2 * NY)

    def row_of(zz, yy, cc):
        return (zz * NY + yy) * 2 + cc

    up_z, dn_z = lax.rem(z + 1, NZ), lax.rem(z + NZ - 1, NZ)
    up_y, dn_y = lax.rem(y + 1, NY), lax.rem(y + NY - 1, NY)
    xat = [lax.rem(x + d, 4) for d in range(4)]
    link_to = {
        "z+": (row_of(up_z, y, core), x),
        "z-": (row_of(dn_z, y, core), x),
        "y+": (row_of(z, up_y, core), x),
        "y-": (row_of(z, dn_y, core), x),
        "core": (row_of(z, y, 1 - core), x),
        1: (me, xat[1]),
        2: (me, xat[2]),
        3: (me, xat[3]),
    }
    barrier = pltpu.get_barrier_semaphore()
    for device in link_to.values():
        pl.semaphore_signal(barrier, inc=1, device_id=device, device_id_type=MESH)

    loads = [
        pltpu.make_async_copy(p_hbm, p_ref, lsem.at[1]),
        pltpu.make_async_copy(ao_hbm, a_all.at[0], lsem.at[2]),
        pltpu.make_async_copy(ad_hbm, ad_ref, lsem.at[3]),
    ]
    for load in loads:
        load.start()

    sends = []

    def remote(src, dst, s, r, device):
        return pltpu.make_async_remote_copy(
            src_ref=src, dst_ref=dst, send_sem=s, recv_sem=r, device_id=device, device_id_type=MESH
        )

    half = ao_hbm.shape[0] // 2
    first, second = pl.ds(0, half), pl.ds(half, half)
    a_plan = {
        ("r", 0): (0, 1, first, 1), ("r", 1): (0, 1, second, 1), ("r", 2): (1, 2, first, 1),
        ("l", 1): (0, 3, second, 3), ("l", 0): (0, 3, first, 3), ("l", 2): (3, 2, second, 3),
    }
    a_index = {name: i for i, name in enumerate(a_plan)}

    def a_copy(name, sending):
        src_slot, dst_slot, part, to = a_plan[name]
        dst = a_all.at[dst_slot, part]
        src = (ao_hbm if src_slot == 0 else a_all.at[src_slot]).at[part] if sending else dst
        i = a_index[name]
        return remote(src, dst, xs_sem.at[i], xr_sem.at[i], link_to[to])

    def a_send(name):
        copy = a_copy(name, True)
        copy.start()
        sends.append(copy)

    def c_copy(d):
        return remote(ctab.at[0], ctab.at[d], xs_sem.at[5 + d], xr_sem.at[5 + d], link_to[d])

    rows = p_hbm.shape[0]
    stage[...] = jnp.zeros_like(stage)
    stage[0 : srows_ref.shape[0], 0 : srows_ref.shape[1]] = srows_ref[...].astype(jnp.float32)
    ctab[0, 0 : ocols_ref.shape[0], 0 : ocols_ref.shape[1]] = ocols_ref[...]
    pl.semaphore_wait(barrier, len(link_to))
    for name in (("r", 0), ("l", 1), ("r", 1), ("l", 0)):
        a_send(name)
    loads[0].wait()

    for i in range(rows):
        for a in range(2):
            tile = jnp.where(agg_ref[0, i] == a, p_ref[i, 0], p_ref[i, 1])
            ordered[i, :, a * T : (a + 1) * T] = tile
            flat = tile.T
            for g in range(4):
                right_t[i, g * 64 + a * 32 : g * 64 + a * 32 + 32, :] = flat[g * 32 : (g + 1) * 32]
        mine[i * 64 : (i + 1) * 64, :] = right_t[i, pl.ds(pl.multiple_of(x * 64, 64), 64), :]
    mine[4 * T :, :] = stage[...].astype(mine.dtype)

    plan = flood_plan()
    names = sorted(plan, key=str)
    index = {name: i for i, name in enumerate(names)}

    def block(offset, rows_at):
        dz, dy = offset
        return gath.at[core, lax.rem(z + (NZ - dz), NZ), lax.rem(y + (NY - dy), NY), pl.ds(*rows_at)]

    def f_copy(name, sending):
        link, there, here, part, _ = plan[name]
        at = PARTS[part]
        dst = block(there if sending else here, at)
        src = mine.at[pl.ds(*at)] if sending and there == (0, 0) else dst
        i = index[name]
        return remote(src, dst, ssem.at[i], rsem.at[i], link_to[link])

    started = set()

    def start_ready(have):
        order = {"Y": 0, "Z": 1, "YZ": 2, "ZY": 3}
        for name in sorted(plan, key=lambda n: (order[n[0]], abs(n[1]), str(n))):
            if name not in started and all(a in have for a in plan[name][4]):
                started.add(name)
                copy = f_copy(name, True)
                copy.start()
                sends.append(copy)

    def s_copy(kind, dz, sending):
        i = len(names) + DZ.index(dz) * 2 + (kind == "y")
        plane = core if sending else 1 - core
        ref = gath.at[plane, lax.rem(z + (NZ - dz), NZ), :, pl.ds(*PARTS[kind])]
        return remote(ref, ref, ssem.at[i], rsem.at[i], link_to["core"])

    need = {}
    for dz in DZ:
        zs = [] if dz == 0 else ([("Z", dz)] if dz != 4 else [("Z", 4, 1), ("Z", 4, -1)])
        need[("z", dz)] = zs + [("ZY", dz, s) for s in (1, -1, 2)]
        need[("y", dz)] = (
            [("Y", 1), ("Y", -1), ("Y", 2, 1), ("Y", 2, -1)]
            if dz == 0
            else [("YZ", dz, s) for s in (0, 1, -1, 2)]
        )

    def share(have):
        for key in list(need):
            if all(a in have for a in need[key]):
                copy = s_copy(*key, True)
                copy.start()
                sends.append(copy)
                del need[key]

    have = set()
    start_ready(have)
    for d in (1, 2, 3):
        copy = c_copy(d)
        copy.start()
        sends.append(copy)
    keep = pltpu.make_async_copy(mine, gath.at[core, z, y], lsem.at[0])
    keep.start()

    per = ao_hbm.shape[1]

    def transposed_left(tile, i):
        return lax.dot_general(
            tile, ordered[i], (((0,), (0,)), ((), ())), preferred_element_type=jnp.float32
        ).astype(jnp.bfloat16)

    def diag_rows(lo, hi):
        def row(i, _):
            for k in range(per):
                dacc[...] += jnp.dot(
                    right_t[dcols_ref[k, i]],
                    transposed_left(ad_ref[i, k], i),
                    preferred_element_type=jnp.float32,
                )
            return 0

        lax.fori_loop(lo, hi, row, 0)

    def left_rows(slot, part):
        def row(i, _):
            for k in range(per):
                left[slot, i, k] = transposed_left(a_all[slot, i, k], i)
            return 0

        lax.fori_loop(part * half, part * half + half, row, 0)

    def share_of(quarter):
        return pl.ds(pl.multiple_of(quarter * 64, 64), 64)

    def d_copy(d):
        return remote(
            dacc.at[share_of(xat[d])], drecv.at[d - 1], xs_sem.at[8 + d], xr_sem.at[8 + d], link_to[d]
        )

    def send_diag():
        for d in (1, 2, 3):
            copy = d_copy(d)
            copy.start()
            sends.append(copy)

    def a_take(name, then=None):
        a_copy(name, False).wait_recv()
        if then:
            a_send(then)

    def begin():
        dacc[...] = jnp.zeros_like(dacc)
        loads[1].wait()
        loads[2].wait()

    events = [(t, 1, name) for name, t in flood_order(plan).items()]
    steps = [
        (0.0, begin), (1.5, lambda: diag_rows(0, 2)), (3.5, lambda: diag_rows(2, 4)),
        (5.5, lambda: diag_rows(4, 6)), (7.5, lambda: diag_rows(6, 8)),
        (7.6, send_diag),
        (9.5, lambda: a_take(("r", 0), ("r", 2))), (9.6, lambda: a_take(("l", 1), ("l", 2))),
        (10.5, lambda: left_rows(0, 0)), (12.0, lambda: left_rows(0, 1)),
        (13.5, lambda: left_rows(1, 0)), (15.0, lambda: left_rows(3, 1)),
        (18.0, lambda: (a_take(("r", 1)), left_rows(1, 1))),
        (19.5, lambda: (a_take(("l", 0)), left_rows(3, 0))),
    ]
    events += [(t, 0, step) for t, step in steps]
    kept = False
    for _, kind, item in sorted(events, key=lambda e: (e[0], e[1], str(e[2]) if e[1] else "")):
        if kind == 0:
            item()
            continue
        f_copy(item, False).wait_recv()
        have.add(item)
        start_ready(have)
        if not kept:
            kept = True
            keep.wait()
        share(have)
    for name, part in ((("r", 2), 0), (("l", 2), 1)):
        a_take(name)
        left_rows(2, part)

    total = dacc[share_of(x), :]
    for d in (1, 2, 3):
        d_copy(d).wait_recv()
        total = total + drecv[d - 1]
        c_copy(d).wait_recv()
    own_ref[...] = total
    cols_ref[...] = ctab[...]

    for dz in DZ:
        for kind in ("z", "y"):
            s_copy(kind, dz, False).wait_recv()
    tail = gath[:, :, :, 4 * T :, :].reshape(2 * NZ * NY * 16, T)
    pick = (lax.broadcasted_iota(jnp.int32, (T, T), 0) == me).astype(jnp.bfloat16)
    spread = jnp.dot(tail, pick, preferred_element_type=jnp.float32).reshape(2 * NZ * NY, 16, T)
    line = lax.broadcasted_iota(jnp.int32, spread.shape, 1) == lax.broadcasted_iota(
        jnp.int32, spread.shape, 2
    )
    tbl_ref[...] = jnp.sum(jnp.where(line, spread, 0.0), axis=1).astype(jnp.int32)

    for copy in sends:
        copy.wait_send()


def gather_all(a_diag, diag_cols, a_offd, offd_cols, prolong, aggregate, send_rows):
    rows, per, _, _ = a_offd.shape
    vmem = pl.BlockSpec(memory_space=pltpu.VMEM)
    smem = pl.BlockSpec(memory_space=pltpu.SMEM)
    hbm = pl.BlockSpec(memory_space=pltpu.HBM)
    copies = len(flood_plan()) + 2 * len(DZ)
    bf16, f32 = jnp.bfloat16, jnp.float32
    return pl.pallas_call(
        gather_kernel,
        in_specs=[smem, smem, vmem, vmem, hbm, hbm, hbm],
        out_specs=[vmem, vmem, vmem, vmem, vmem],
        out_shape=[
            jax.ShapeDtypeStruct((2, NZ, NY, ROWS, T), bf16),
            jax.ShapeDtypeStruct((4, rows, per, T, 2 * T), bf16),
            jax.ShapeDtypeStruct((64, 2 * T), f32),
            jax.ShapeDtypeStruct((2 * NZ * NY, T), jnp.int32),
            jax.ShapeDtypeStruct((4, 8, T), jnp.int32),
        ],
        scratch_shapes=[
            pltpu.VMEM((rows, 2, T, T), bf16),
            pltpu.VMEM((rows, per, T, T), bf16),
            pltpu.VMEM((ROWS, T), bf16),
            pltpu.VMEM((16, T), f32),
            pltpu.VMEM((rows, T, 2 * T), bf16),
            pltpu.VMEM((rows, 2 * T, T), bf16),
            pltpu.VMEM((4, rows, per, T, T), bf16),
            pltpu.VMEM((2 * T, 2 * T), f32),
            pltpu.VMEM((3, 64, 2 * T), f32),
            pltpu.VMEM((4, 8, T), jnp.int32),
            pltpu.SemaphoreType.DMA((copies,)),
            pltpu.SemaphoreType.DMA((copies,)),
            pltpu.SemaphoreType.DMA((12,)),
            pltpu.SemaphoreType.DMA((12,)),
            pltpu.SemaphoreType.DMA((4,)),
        ],
        compiler_params=pltpu.CompilerParams(
            collective_id=0, has_side_effects=True, vmem_limit_bytes=32 << 20
        ),
        name="gather_all",
    )(
        *(
            pltpu.with_memory_space_constraint(item, pltpu.HBM)
            for item in (aggregate.T, diag_cols.T, offd_cols.T, send_rows[0].T, prolong, a_diag, a_offd)
        )
    )


def slot_of(node):
    return lax.rem(node, 2) * (NZ * NY) + node // 2


def offd_kernel(me_ref, tbl_ref, cols_ref, l_ref, gath_ref, d_ref, acc):
    groups, rows, per, _, _ = l_ref.shape
    acc[...] = jnp.zeros_like(acc)

    def row(i, _):
        for t in range(groups * per):
            g, k = t // per, t % per
            col = cols_ref[g, k, i]
            slot = slot_of(col // 4)
            at = pl.multiple_of(tbl_ref[slot, lax.rem(col, 4)] * 64, 64)
            acc[slot] += jnp.dot(
                gath_ref[slot, pl.ds(at, 64), :], l_ref[g, i, k], preferred_element_type=jnp.float32
            )
        return 0

    lax.fori_loop(0, rows, row, 0, unroll=2)
    acc[slot_of(me_ref[0])] = d_ref[...]


def offd_terms(me, table, cols, left, gathered, own):
    vmem = pl.BlockSpec(memory_space=pltpu.VMEM)
    smem = pl.BlockSpec(memory_space=pltpu.SMEM)
    return pl.pallas_call(
        offd_kernel,
        in_specs=[smem, smem, smem, vmem, vmem, vmem],
        out_specs=vmem,
        out_shape=jax.ShapeDtypeStruct((gathered.shape[0], 64, 2 * T), jnp.float32),
        compiler_params=pltpu.CompilerParams(vmem_limit_bytes=32 << 20),
        name="offd_terms",
    )(me, table, cols, left, gathered, own)


def swap_kernel(map_ref, acc, out, src, ssem, rsem, lsem):
    me = lax.axis_index("rows")
    x = lax.axis_index("grp")
    at = [lax.rem(x + d, 4) for d in range(4)]
    barrier = pltpu.get_barrier_semaphore()
    for d in (2, 1, 3):
        pl.semaphore_signal(barrier, inc=1, device_id=(me, at[d]), device_id_type=MESH)
    pairs, quarter = src.shape[1], src.shape[2]
    chunks = ssem.shape[1]
    step = pairs // chunks

    def pack(p):
        items = []
        for a in range(CR1):
            for j in range(2):
                gid = map_ref[2 * p + j]
                both = acc[slot_of(gid // CR1), :, a * T : (a + 1) * T]
                items.append(jnp.where(lax.rem(gid, CR1) == 0, both[:32], both[32:]))
        both = jnp.concatenate(items, axis=0).T.astype(src.dtype)
        for g in range(src.shape[0]):
            src[g, p] = both[g * quarter : (g + 1) * quarter]

    def remote(d, c, a, b):
        piece = pl.ds(c * step, step)
        return pltpu.make_async_remote_copy(
            src_ref=a.at[piece], dst_ref=b.at[piece],
            send_sem=ssem.at[d - 1, c], recv_sem=rsem.at[d - 1, c],
            device_id=(me, at[d]), device_id_type=MESH,
        )

    for c in range(chunks):
        for p in range(c * step, (c + 1) * step):
            pack(p)
        if c == 0:
            pl.semaphore_wait(barrier, 3)
        for d in (2, 1, 3):
            remote(d, c, src.at[at[d]], out.at[x]).start()
    stay = pltpu.make_async_copy(src.at[x], out.at[x], lsem)
    stay.start()
    for c in range(chunks):
        for d in (1, 3, 2):
            came = out.at[at[4 - d]]
            remote(d, c, came, came).wait_recv()
    stay.wait()
    for c in range(chunks):
        for d in (1, 3, 2):
            remote(d, c, src.at[at[d]], out.at[x]).wait_send()


def swap_slices(col_map, sums):
    vmem = pl.BlockSpec(memory_space=pltpu.VMEM)
    shape = (4, col_map.shape[0] // 2, T // 4, T)
    chunks = 7
    return pl.pallas_call(
        swap_kernel,
        in_specs=[pl.BlockSpec(memory_space=pltpu.SMEM), vmem],
        out_specs=vmem,
        out_shape=jax.ShapeDtypeStruct(shape, jnp.bfloat16),
        scratch_shapes=[
            pltpu.VMEM(shape, jnp.bfloat16),
            pltpu.SemaphoreType.DMA((3, chunks)),
            pltpu.SemaphoreType.DMA((3, chunks)),
            pltpu.SemaphoreType.DMA,
        ],
        compiler_params=pltpu.CompilerParams(
            collective_id=1, has_side_effects=True, vmem_limit_bytes=16 << 20
        ),
        name="swap_slices",
    )(col_map, sums)


def place_kernel(x_ref, out_hbm, buf, sem):
    pairs, quarter = x_ref.shape[1], x_ref.shape[2]
    chunks = sem.shape[1]
    step = pairs // chunks

    def copies(n):
        at = pl.ds(2 * step * n, 2 * step)
        return [pltpu.make_async_copy(buf.at[r, at], out_hbm.at[r, at], sem.at[r, n]) for r in range(CR1)]

    row = lax.broadcasted_iota(jnp.int32, (4 * T, 4 * T), 0)
    col = lax.broadcasted_iota(jnp.int32, (4 * T, 4 * T), 1)
    move = (row % 32 == col % 32) & ((row // 32) % 4 == col // T) & (row // T == (col // 32) % 4)
    move = jnp.where(move, 1.0, 0.0).astype(jnp.bfloat16)
    for n in range(chunks):
        at = pl.ds(n * step, step)
        x = jnp.concatenate([x_ref[s, at].reshape(step * quarter, T) for s in range(4)], axis=1)
        o = jnp.dot(x, move, preferred_element_type=jnp.float32).astype(buf.dtype)
        for r in range(CR1):
            for j in range(2):
                piece = o[:, (r * 2 + j) * T : (r * 2 + j + 1) * T].reshape(step, quarter, T)
                for p in range(step):
                    buf[r, 2 * (n * step + p) + j] = piece[p]
        for copy in copies(n):
            copy.start()
    for n in range(chunks):
        for copy in copies(n):
            copy.wait()


def place_slots(arrived):
    groups, pairs, quarter, _ = arrived.shape
    shape = (CR1, 2 * pairs, quarter, T)
    return pl.pallas_call(
        place_kernel,
        in_specs=[pl.BlockSpec(memory_space=pltpu.VMEM)],
        out_specs=pl.BlockSpec(memory_space=pltpu.HBM),
        out_shape=jax.ShapeDtypeStruct(shape, jnp.bfloat16),
        scratch_shapes=[pltpu.VMEM(shape, jnp.bfloat16), pltpu.SemaphoreType.DMA((CR1, 7))],
        compiler_params=pltpu.CompilerParams(vmem_limit_bytes=16 << 20),
        name="place_slots",
    )(arrived)


def per_device(
    a_diag, diag_cols, a_offd, offd_cols, prolong, aggregate, send_rows, ghost_agg, coarse_map
):
    me = lax.axis_index("rows").reshape(1)
    gathered, left, own, table, cols = gather_all(
        a_diag, diag_cols, a_offd, offd_cols, prolong, aggregate, send_rows
    )
    gathered = gathered.reshape(2 * NZ * NY, ROWS, T)
    sums = offd_terms(me, table, cols, left, gathered, own)
    return place_slots(swap_slices(coarse_map[0], sums))


def solution(mesh):
    in_specs = (
        P("rows", "grp", None, None),
        P("rows", "grp"),
        P("rows", "grp", None, None),
        P("rows", "grp"),
        P("rows", None, None, None),
        P("rows", None),
        P("rows", None, None),
        P("rows", None, None, None),
        P("rows", None),
    )
    out_specs = P("rows", None, "grp", None)
    return jax.shard_map(
        per_device, mesh=mesh, in_specs=in_specs, out_specs=out_specs, check_vma=False
    )
```

```python
import functools

import jax
import jax.numpy as jnp
from jax import lax
from jax.experimental import pallas as pl
from jax.experimental.pallas import tpu as pltpu
from jax.sharding import PartitionSpec as P

CR1 = 2
T = 128


ROWS = 528
ZR = 288
NZ, NY = 8, 4
MESH = pl.DeviceIdType.MESH
PARTS = {"z": (0, ZR), "za": (0, ZR // 2), "zb": (ZR // 2, ZR // 2),
         "y": (ZR, ROWS - ZR), "ya": (ZR, 112), "yb": (ZR + 112, ROWS - ZR - 112)}
DZ = (0, 1, -1, 2, -2, 3, -3, 4)
LATE_UP = (0, 1, 2, 3)
SHARES = [
    (kind, dz, dy)
    for dz in DZ
    for kind in ("z", "y")
    for dy in ((None,) if abs(dz) < 3 else (0, 1, -1, 2))
]


def flood_plan():
    plan = {}

    def add(name, link, there, here, part, after):
        plan[name] = (link, there, here, part, tuple(after))

    for sign, link in ((1, "z+"), (-1, "z-")):
        for d in range(1, 5):
            part = "z" if d < 4 else ("za" if sign == 1 else "zb")
            after = [] if d == 1 else [("Z", sign * (d - 1))]
            here = sign * d if d < 4 else 4
            name = ("Z", here) if d < 4 else ("Z", 4, sign)
            add(name, link, (sign * (d - 1), 0), (here, 0), part, after)
    for e in DZ:
        have = [] if e == 0 else ([("Z", e)] if e != 4 else [("Z", 4, 1), ("Z", 4, -1)])
        for sign, link in ((1, "y+"), (-1, "y-")):
            add(("ZY", e, sign), link, (e, 0), (e, sign), "z", have)
        sign = 1 if e in LATE_UP else -1
        add(("ZY", e, 2), "y+" if sign == 1 else "y-", (e, sign), (e, 2), "z", [("ZY", e, sign)])
    for sign, link in ((1, "y+"), (-1, "y-")):
        add(("Y", sign), link, (0, 0), (0, sign), "y", [])
        add(("Y", 2, sign), link, (0, sign), (0, 2), "ya" if sign == 1 else "yb", [("Y", sign)])
    for sign, link in ((1, "z+"), (-1, "z-")):
        for d in range(1, 5):
            for dy in (0, 1, -1, 2):
                if d == 4 and (dy in (0, 1)) != (sign == 1):
                    continue
                if d > 1:
                    after = [("YZ", sign * (d - 1), dy)]
                elif dy == 0:
                    after = []
                else:
                    after = [("Y", dy)] if dy != 2 else [("Y", 2, 1), ("Y", 2, -1)]
                here = sign * d if d < 4 else 4
                add(("YZ", here, dy), link, (sign * (d - 1), dy), (here, dy), "y", after)
    return plan


def flood_rank(plan):
    kids = {}
    for name, item in plan.items():
        for a in item[4]:
            kids.setdefault(a, []).append(name)
    memo = {}

    def depth(name):
        if name not in memo:
            memo[name] = 1 + max([depth(k) for k in kids.get(name, [])], default=0)
        return memo[name]

    kind = {"Y": 0, "Z": 1, "YZ": 2, "ZY": 3}
    return {n: (-depth(n), kind[n[0]], abs(n[1]), str(n)) for n in plan}


def flood_order(plan, latency=2.5, rate=49e3):
    rank = flood_rank(plan)
    free = {}
    arrive, waiting = {}, dict(plan)
    while waiting:
        best = None
        for name, (link, _, _, part, after) in waiting.items():
            if any(a not in arrive for a in after):
                continue
            start = max([arrive[a] for a in after] + [free.get(link, 0.0)])
            key = (start,) + rank[name]
            if best is None or key < best[0]:
                best = (key, name, start, link, PARTS[part][1] * 256 / rate)
        _, name, start, link, took = best
        free[link] = start + took
        arrive[name] = start + took + latency
        del waiting[name]
    return arrive


def gather_kernel(
    agg_ref, dcols_ref, ocols_ref, srows_ref, p_hbm, ad_hbm, ao_hbm,
    gath, left, own_ref, tbl_ref, cols_ref,
    p_ref, ad_ref, mine, stage, ordered, right_t, a_all, dacc, drecv, ctab,
    ssem, rsem, xs_sem, xr_sem, lsem,
):
    me = lax.axis_index("rows")
    x = lax.axis_index("grp")
    core = lax.rem(me, 2)
    y = lax.rem(me // 2, NY)
    z = me // (2 * NY)

    def row_of(zz, yy, cc):
        return (zz * NY + yy) * 2 + cc

    up_z, dn_z = lax.rem(z + 1, NZ), lax.rem(z + NZ - 1, NZ)
    up_y, dn_y = lax.rem(y + 1, NY), lax.rem(y + NY - 1, NY)
    xat = [lax.rem(x + d, 4) for d in range(4)]
    link_to = {
        "z+": (row_of(up_z, y, core), x),
        "z-": (row_of(dn_z, y, core), x),
        "y+": (row_of(z, up_y, core), x),
        "y-": (row_of(z, dn_y, core), x),
        "core": (row_of(z, y, 1 - core), x),
        1: (me, xat[1]),
        2: (me, xat[2]),
        3: (me, xat[3]),
    }
    barrier = pltpu.get_barrier_semaphore()
    for device in link_to.values():
        pl.semaphore_signal(barrier, inc=1, device_id=device, device_id_type=MESH)

    loads = [
        pltpu.make_async_copy(p_hbm, p_ref, lsem.at[1]),
        pltpu.make_async_copy(ao_hbm, a_all.at[0], lsem.at[2]),
        pltpu.make_async_copy(ad_hbm, ad_ref, lsem.at[3]),
    ]
    for load in loads:
        load.start()

    sends = []

    def remote(src, dst, s, r, device):
        return pltpu.make_async_remote_copy(
            src_ref=src, dst_ref=dst, send_sem=s, recv_sem=r, device_id=device, device_id_type=MESH
        )

    half = ao_hbm.shape[0] // 2
    first, second = pl.ds(0, half), pl.ds(half, half)
    a_plan = {
        ("r", 0): (0, 1, first, 1), ("r", 1): (0, 1, second, 1), ("r", 2): (1, 2, first, 1),
        ("l", 1): (0, 3, second, 3), ("l", 0): (0, 3, first, 3), ("l", 2): (3, 2, second, 3),
    }
    a_index = {name: i for i, name in enumerate(a_plan)}

    def a_copy(name, sending):
        src_slot, dst_slot, part, to = a_plan[name]
        dst = a_all.at[dst_slot, part]
        src = (ao_hbm if src_slot == 0 else a_all.at[src_slot]).at[part] if sending else dst
        i = a_index[name]
        return remote(src, dst, xs_sem.at[i], xr_sem.at[i], link_to[to])

    def a_send(name):
        copy = a_copy(name, True)
        copy.start()
        sends.append(copy)

    def c_copy(d):
        return remote(ctab.at[0], ctab.at[d], xs_sem.at[5 + d], xr_sem.at[5 + d], link_to[d])

    rows = p_hbm.shape[0]
    stage[...] = jnp.zeros_like(stage)
    stage[0 : srows_ref.shape[0], 0 : srows_ref.shape[1]] = srows_ref[...].astype(jnp.float32)
    ctab[0, 0 : ocols_ref.shape[0], 0 : ocols_ref.shape[1]] = ocols_ref[...]
    pl.semaphore_wait(barrier, len(link_to))
    for name in (("r", 0), ("l", 1), ("r", 1), ("l", 0)):
        a_send(name)
    loads[0].wait()

    for i in range(rows):
        for a in range(2):
            tile = jnp.where(agg_ref[0, i] == a, p_ref[i, 0], p_ref[i, 1])
            ordered[i, :, a * T : (a + 1) * T] = tile
            flat = tile.T
            for g in range(4):
                right_t[i, g * 64 + a * 32 : g * 64 + a * 32 + 32, :] = flat[g * 32 : (g + 1) * 32]
        mine[i * 64 : (i + 1) * 64, :] = right_t[i, pl.ds(pl.multiple_of(x * 64, 64), 64), :]
    mine[4 * T :, :] = stage[...].astype(mine.dtype)

    plan = flood_plan()
    names = sorted(plan, key=str)
    index = {name: i for i, name in enumerate(names)}

    def block(offset, rows_at):
        dz, dy = offset
        return gath.at[core, lax.rem(z + (NZ - dz), NZ), lax.rem(y + (NY - dy), NY), pl.ds(*rows_at)]

    def f_copy(name, sending):
        link, there, here, part, _ = plan[name]
        at = PARTS[part]
        dst = block(there if sending else here, at)
        src = mine.at[pl.ds(*at)] if sending and there == (0, 0) else dst
        i = index[name]
        return remote(src, dst, ssem.at[i], rsem.at[i], link_to[link])

    started = set()

    rank = flood_rank(plan)

    def start_ready(have):
        for name in sorted(plan, key=rank.get):
            if name not in started and all(a in have for a in plan[name][4]):
                started.add(name)
                copy = f_copy(name, True)
                copy.start()
                sends.append(copy)

    def s_copy(key, sending):
        kind, dz, dy = key
        i = len(names) + SHARES.index(key)
        at = pl.ds(*PARTS[kind])
        plane = gath.at[core if sending else 1 - core, lax.rem(z + (NZ - dz), NZ)]
        ref = plane.at[:, at] if dy is None else plane.at[lax.rem(y + (NY - dy), NY), at]
        return remote(ref, ref, ssem.at[i], rsem.at[i], link_to["core"])

    need = {}
    for kind, dz, dy in SHARES:
        zs = [] if dz == 0 else ([("Z", dz)] if dz != 4 else [("Z", 4, 1), ("Z", 4, -1)])
        parts = {}
        if kind == "z":
            parts = {0: zs, **{d: [("ZY", dz, d)] for d in (1, -1, 2)}}
        elif dz == 0:
            parts = {0: [], 1: [("Y", 1)], -1: [("Y", -1)], 2: [("Y", 2, 1), ("Y", 2, -1)]}
        else:
            parts = {d: [("YZ", dz, d)] for d in (0, 1, -1, 2)}
        need[kind, dz, dy] = sum(parts.values(), []) if dy is None else parts[dy]

    def share(have):
        for key in list(need):
            if all(a in have for a in need[key]):
                copy = s_copy(key, True)
                copy.start()
                sends.append(copy)
                del need[key]

    have = set()
    start_ready(have)
    for d in (1, 2, 3):
        copy = c_copy(d)
        copy.start()
        sends.append(copy)
    keep = pltpu.make_async_copy(mine, gath.at[core, z, y], lsem.at[0])
    keep.start()

    per = ao_hbm.shape[1]

    def transposed_left(tile, i):
        return lax.dot_general(
            tile, ordered[i], (((0,), (0,)), ((), ())), preferred_element_type=jnp.float32
        ).astype(jnp.bfloat16)

    def diag_rows(lo, hi):
        def row(i, _):
            for k in range(per):
                dacc[...] += jnp.dot(
                    right_t[dcols_ref[k, i]],
                    transposed_left(ad_ref[i, k], i),
                    preferred_element_type=jnp.float32,
                )
            return 0

        lax.fori_loop(lo, hi, row, 0)

    def left_rows(slot, part):
        def row(i, _):
            for k in range(per):
                left[slot, i, k] = transposed_left(a_all[slot, i, k], i)
            return 0

        lax.fori_loop(part * half, part * half + half, row, 0)

    def share_of(quarter):
        return pl.ds(pl.multiple_of(quarter * 64, 64), 64)

    def d_copy(d):
        return remote(
            dacc.at[share_of(xat[d])], drecv.at[d - 1], xs_sem.at[8 + d], xr_sem.at[8 + d], link_to[d]
        )

    def send_diag():
        for d in (1, 2, 3):
            copy = d_copy(d)
            copy.start()
            sends.append(copy)

    def a_take(name, then=None):
        a_copy(name, False).wait_recv()
        if then:
            a_send(then)

    def begin():
        dacc[...] = jnp.zeros_like(dacc)
        loads[1].wait()
        loads[2].wait()

    events = [(t, 1, name) for name, t in flood_order(plan).items()]
    steps = [
        (0.0, begin),
        (0.5, lambda: diag_rows(0, 1)),
        (1.4, lambda: diag_rows(1, 2)),
        (2.3, lambda: diag_rows(2, 3)),
        (3.2, lambda: diag_rows(3, 4)),
        (4.1, lambda: diag_rows(4, 5)),
        (5.0, lambda: diag_rows(5, 6)),
        (5.9, lambda: diag_rows(6, 7)),
        (6.8, lambda: diag_rows(7, 8)),
        (7.6, send_diag),
        (9.5, lambda: a_take(("r", 0), ("r", 2))), (9.6, lambda: a_take(("l", 1), ("l", 2))),
        (10.5, lambda: left_rows(0, 0)), (12.0, lambda: left_rows(0, 1)),
        (13.5, lambda: left_rows(1, 0)), (15.0, lambda: left_rows(3, 1)),
        (18.0, lambda: (a_take(("r", 1)), left_rows(1, 1))),
        (19.5, lambda: (a_take(("l", 0)), left_rows(3, 0))),
    ]
    events += [(t, 0, step) for t, step in steps]
    kept = False
    for _, kind, item in sorted(events, key=lambda e: (e[0], e[1], str(e[2]) if e[1] else "")):
        if kind == 0:
            item()
            continue
        f_copy(item, False).wait_recv()
        have.add(item)
        start_ready(have)
        if not kept:
            kept = True
            keep.wait()
        share(have)
    for name, part in ((("r", 2), 0), (("l", 2), 1)):
        a_take(name)
        left_rows(2, part)

    total = dacc[share_of(x), :]
    for d in (1, 2, 3):
        d_copy(d).wait_recv()
        total = total + drecv[d - 1]
        c_copy(d).wait_recv()
    own_ref[...] = total
    cols_ref[...] = ctab[...]

    for key in SHARES:
        s_copy(key, False).wait_recv()
    tail = gath[:, :, :, 4 * T :, :].reshape(2 * NZ * NY * 16, T)
    pick = (lax.broadcasted_iota(jnp.int32, (T, T), 0) == me).astype(jnp.bfloat16)
    spread = jnp.dot(tail, pick, preferred_element_type=jnp.float32).reshape(2 * NZ * NY, 16, T)
    line = lax.broadcasted_iota(jnp.int32, spread.shape, 1) == lax.broadcasted_iota(
        jnp.int32, spread.shape, 2
    )
    tbl_ref[...] = jnp.sum(jnp.where(line, spread, 0.0), axis=1).astype(jnp.int32)

    for copy in sends:
        copy.wait_send()


def gather_all(a_diag, diag_cols, a_offd, offd_cols, prolong, aggregate, send_rows):
    rows, per, _, _ = a_offd.shape
    vmem = pl.BlockSpec(memory_space=pltpu.VMEM)
    smem = pl.BlockSpec(memory_space=pltpu.SMEM)
    hbm = pl.BlockSpec(memory_space=pltpu.HBM)
    copies = len(flood_plan()) + len(SHARES)
    bf16, f32 = jnp.bfloat16, jnp.float32
    return pl.pallas_call(
        gather_kernel,
        in_specs=[smem, smem, vmem, vmem, hbm, hbm, hbm],
        out_specs=[vmem, vmem, vmem, vmem, vmem],
        out_shape=[
            jax.ShapeDtypeStruct((2, NZ, NY, ROWS, T), bf16),
            jax.ShapeDtypeStruct((4, rows, per, T, 2 * T), bf16),
            jax.ShapeDtypeStruct((64, 2 * T), f32),
            jax.ShapeDtypeStruct((2 * NZ * NY, T), jnp.int32),
            jax.ShapeDtypeStruct((4, 8, T), jnp.int32),
        ],
        scratch_shapes=[
            pltpu.VMEM((rows, 2, T, T), bf16),
            pltpu.VMEM((rows, per, T, T), bf16),
            pltpu.VMEM((ROWS, T), bf16),
            pltpu.VMEM((16, T), f32),
            pltpu.VMEM((rows, T, 2 * T), bf16),
            pltpu.VMEM((rows, 2 * T, T), bf16),
            pltpu.VMEM((4, rows, per, T, T), bf16),
            pltpu.VMEM((2 * T, 2 * T), f32),
            pltpu.VMEM((3, 64, 2 * T), f32),
            pltpu.VMEM((4, 8, T), jnp.int32),
            pltpu.SemaphoreType.DMA((copies,)),
            pltpu.SemaphoreType.DMA((copies,)),
            pltpu.SemaphoreType.DMA((12,)),
            pltpu.SemaphoreType.DMA((12,)),
            pltpu.SemaphoreType.DMA((4,)),
        ],
        compiler_params=pltpu.CompilerParams(
            collective_id=0, has_side_effects=True, vmem_limit_bytes=32 << 20
        ),
        name="gather_all",
    )(
        *(
            pltpu.with_memory_space_constraint(item, pltpu.HBM)
            for item in (aggregate.T, diag_cols.T, offd_cols.T, send_rows[0].T, prolong, a_diag, a_offd)
        )
    )


def slot_of(node):
    return lax.rem(node, 2) * (NZ * NY) + node // 2


def offd_kernel(me_ref, tbl_ref, cols_ref, l_ref, gath_ref, d_ref, acc):
    groups, rows, per, _, _ = l_ref.shape
    acc[...] = jnp.zeros_like(acc)

    def row(i, _):
        for t in range(groups * per):
            g, k = t // per, t % per
            col = cols_ref[g, k, i]
            slot = slot_of(col // 4)
            at = pl.multiple_of(tbl_ref[slot, lax.rem(col, 4)] * 64, 64)
            acc[slot] += jnp.dot(
                gath_ref[slot, pl.ds(at, 64), :], l_ref[g, i, k], preferred_element_type=jnp.float32
            )
        return 0

    lax.fori_loop(0, rows, row, 0, unroll=2)
    acc[slot_of(me_ref[0])] = d_ref[...]


def offd_terms(me, table, cols, left, gathered, own):
    vmem = pl.BlockSpec(memory_space=pltpu.VMEM)
    smem = pl.BlockSpec(memory_space=pltpu.SMEM)
    return pl.pallas_call(
        offd_kernel,
        in_specs=[smem, smem, smem, vmem, vmem, vmem],
        out_specs=vmem,
        out_shape=jax.ShapeDtypeStruct((gathered.shape[0], 64, 2 * T), jnp.float32),
        compiler_params=pltpu.CompilerParams(vmem_limit_bytes=32 << 20),
        name="offd_terms",
    )(me, table, cols, left, gathered, own)


def swap_kernel(map_ref, acc, out, src, ssem, rsem, lsem):
    me = lax.axis_index("rows")
    x = lax.axis_index("grp")
    at = [lax.rem(x + d, 4) for d in range(4)]
    barrier = pltpu.get_barrier_semaphore()
    for d in (2, 1, 3):
        pl.semaphore_signal(barrier, inc=1, device_id=(me, at[d]), device_id_type=MESH)
    pairs, quarter = src.shape[1], src.shape[2]
    chunks = ssem.shape[1]
    step = pairs // chunks

    def pack(p):
        items = []
        for a in range(CR1):
            for j in range(2):
                gid = map_ref[2 * p + j]
                both = acc[slot_of(gid // CR1), :, a * T : (a + 1) * T]
                items.append(jnp.where(lax.rem(gid, CR1) == 0, both[:32], both[32:]))
        both = jnp.concatenate(items, axis=0).T.astype(src.dtype)
        for g in range(src.shape[0]):
            src[g, p] = both[g * quarter : (g + 1) * quarter]

    def remote(d, c, a, b):
        piece = pl.ds(c * step, step)
        return pltpu.make_async_remote_copy(
            src_ref=a.at[piece], dst_ref=b.at[piece],
            send_sem=ssem.at[d - 1, c], recv_sem=rsem.at[d - 1, c],
            device_id=(me, at[d]), device_id_type=MESH,
        )

    for c in range(chunks):
        for p in range(c * step, (c + 1) * step):
            pack(p)
        if c == 0:
            pl.semaphore_wait(barrier, 3)
        for d in (2, 1, 3):
            remote(d, c, src.at[at[d]], out.at[x]).start()
    stay = pltpu.make_async_copy(src.at[x], out.at[x], lsem)
    stay.start()
    for c in range(chunks):
        for d in (1, 3, 2):
            came = out.at[at[4 - d]]
            remote(d, c, came, came).wait_recv()
    stay.wait()
    for c in range(chunks):
        for d in (1, 3, 2):
            remote(d, c, src.at[at[d]], out.at[x]).wait_send()


def swap_slices(col_map, sums):
    vmem = pl.BlockSpec(memory_space=pltpu.VMEM)
    shape = (4, col_map.shape[0] // 2, T // 4, T)
    chunks = 7
    return pl.pallas_call(
        swap_kernel,
        in_specs=[pl.BlockSpec(memory_space=pltpu.SMEM), vmem],
        out_specs=vmem,
        out_shape=jax.ShapeDtypeStruct(shape, jnp.bfloat16),
        scratch_shapes=[
            pltpu.VMEM(shape, jnp.bfloat16),
            pltpu.SemaphoreType.DMA((3, chunks)),
            pltpu.SemaphoreType.DMA((3, chunks)),
            pltpu.SemaphoreType.DMA,
        ],
        compiler_params=pltpu.CompilerParams(
            collective_id=1, has_side_effects=True, vmem_limit_bytes=16 << 20
        ),
        name="swap_slices",
    )(col_map, sums)


def place_kernel(x_ref, out_hbm, buf, sem):
    pairs, quarter = x_ref.shape[1], x_ref.shape[2]
    chunks = sem.shape[1]
    step = pairs // chunks

    def copies(n):
        at = pl.ds(2 * step * n, 2 * step)
        return [pltpu.make_async_copy(buf.at[r, at], out_hbm.at[r, at], sem.at[r, n]) for r in range(CR1)]

    row = lax.broadcasted_iota(jnp.int32, (4 * T, 4 * T), 0)
    col = lax.broadcasted_iota(jnp.int32, (4 * T, 4 * T), 1)
    move = (row % 32 == col % 32) & ((row // 32) % 4 == col // T) & (row // T == (col // 32) % 4)
    move = jnp.where(move, 1.0, 0.0).astype(jnp.bfloat16)
    for n in range(chunks):
        at = pl.ds(n * step, step)
        x = jnp.concatenate([x_ref[s, at].reshape(step * quarter, T) for s in range(4)], axis=1)
        o = jnp.dot(x, move, preferred_element_type=jnp.float32).astype(buf.dtype)
        for r in range(CR1):
            for j in range(2):
                piece = o[:, (r * 2 + j) * T : (r * 2 + j + 1) * T].reshape(step, quarter, T)
                for p in range(step):
                    buf[r, 2 * (n * step + p) + j] = piece[p]
        for copy in copies(n):
            copy.start()
    for n in range(chunks):
        for copy in copies(n):
            copy.wait()


def place_slots(arrived):
    groups, pairs, quarter, _ = arrived.shape
    shape = (CR1, 2 * pairs, quarter, T)
    return pl.pallas_call(
        place_kernel,
        in_specs=[pl.BlockSpec(memory_space=pltpu.VMEM)],
        out_specs=pl.BlockSpec(memory_space=pltpu.HBM),
        out_shape=jax.ShapeDtypeStruct(shape, jnp.bfloat16),
        scratch_shapes=[pltpu.VMEM(shape, jnp.bfloat16), pltpu.SemaphoreType.DMA((CR1, 7))],
        compiler_params=pltpu.CompilerParams(vmem_limit_bytes=16 << 20),
        name="place_slots",
    )(arrived)


def per_device(
    a_diag, diag_cols, a_offd, offd_cols, prolong, aggregate, send_rows, ghost_agg, coarse_map
):
    me = lax.axis_index("rows").reshape(1)
    gathered, left, own, table, cols = gather_all(
        a_diag, diag_cols, a_offd, offd_cols, prolong, aggregate, send_rows
    )
    gathered = gathered.reshape(2 * NZ * NY, ROWS, T)
    sums = offd_terms(me, table, cols, left, gathered, own)
    return place_slots(swap_slices(coarse_map[0], sums))


def solution(mesh):
    in_specs = (
        P("rows", "grp", None, None),
        P("rows", "grp"),
        P("rows", "grp", None, None),
        P("rows", "grp"),
        P("rows", None, None, None),
        P("rows", None),
        P("rows", None, None),
        P("rows", None, None, None),
        P("rows", None),
    )
    out_specs = P("rows", None, "grp", None)
    return jax.shard_map(
        per_device, mesh=mesh, in_specs=in_specs, out_specs=out_specs, check_vma=False
    )
```

```python
import functools

import jax
import jax.numpy as jnp
from jax import lax
from jax.experimental import pallas as pl
from jax.experimental.pallas import tpu as pltpu
from jax.sharding import PartitionSpec as P

CR1 = 2
T = 128


ROWS = 528
ZR = 288
NZ, NY = 8, 4
MESH = pl.DeviceIdType.MESH
PARTS = {"z": (0, ZR), "za": (0, ZR // 2), "zb": (ZR // 2, ZR // 2),
         "y": (ZR, ROWS - ZR), "ya": (ZR, 112), "yb": (ZR + 112, ROWS - ZR - 112)}
DZ = (0, 1, -1, 2, -2, 3, -3, 4)
LATE_UP = (0, 1, 2, 3)
SHARES = [
    (kind, dz, dy)
    for dz in DZ
    for kind in ("z", "y")
    for dy in ((None,) if abs(dz) < 3 else (0, 1, -1, 2))
]


def flood_plan():
    plan = {}

    def add(name, link, there, here, part, after):
        plan[name] = (link, there, here, part, tuple(after))

    for sign, link in ((1, "z+"), (-1, "z-")):
        for d in range(1, 5):
            part = "z" if d < 4 else ("za" if sign == 1 else "zb")
            after = [] if d == 1 else [("Z", sign * (d - 1))]
            here = sign * d if d < 4 else 4
            name = ("Z", here) if d < 4 else ("Z", 4, sign)
            add(name, link, (sign * (d - 1), 0), (here, 0), part, after)
    for e in DZ:
        have = [] if e == 0 else ([("Z", e)] if e != 4 else [("Z", 4, 1), ("Z", 4, -1)])
        for sign, link in ((1, "y+"), (-1, "y-")):
            add(("ZY", e, sign), link, (e, 0), (e, sign), "z", have)
        sign = 1 if e in LATE_UP else -1
        add(("ZY", e, 2), "y+" if sign == 1 else "y-", (e, sign), (e, 2), "z", [("ZY", e, sign)])
    for sign, link in ((1, "y+"), (-1, "y-")):
        add(("Y", sign), link, (0, 0), (0, sign), "y", [])
        add(("Y", 2, sign), link, (0, sign), (0, 2), "ya" if sign == 1 else "yb", [("Y", sign)])
    for sign, link in ((1, "z+"), (-1, "z-")):
        for d in range(1, 5):
            for dy in (0, 1, -1, 2):
                if d == 4 and (dy in (0, 1)) != (sign == 1):
                    continue
                if d > 1:
                    after = [("YZ", sign * (d - 1), dy)]
                elif dy == 0:
                    after = []
                else:
                    after = [("Y", dy)] if dy != 2 else [("Y", 2, 1), ("Y", 2, -1)]
                here = sign * d if d < 4 else 4
                add(("YZ", here, dy), link, (sign * (d - 1), dy), (here, dy), "y", after)
    return plan


def flood_rank(plan):
    kids = {}
    for name, item in plan.items():
        for a in item[4]:
            kids.setdefault(a, []).append(name)
    memo = {}

    def depth(name):
        if name not in memo:
            memo[name] = 1 + max([depth(k) for k in kids.get(name, [])], default=0)
        return memo[name]

    kind = {"Y": 0, "Z": 1, "YZ": 2, "ZY": 3}
    return {n: (-depth(n), kind[n[0]], abs(n[1]), str(n)) for n in plan}


def flood_order(plan, latency=2.5, rate=49e3):
    rank = flood_rank(plan)
    free = {}
    arrive, waiting = {}, dict(plan)
    while waiting:
        best = None
        for name, (link, _, _, part, after) in waiting.items():
            if any(a not in arrive for a in after):
                continue
            start = max([arrive[a] for a in after] + [free.get(link, 0.0)])
            key = (start,) + rank[name]
            if best is None or key < best[0]:
                best = (key, name, start, link, PARTS[part][1] * 256 / rate)
        _, name, start, link, took = best
        free[link] = start + took
        arrive[name] = start + took + latency
        del waiting[name]
    return arrive


def gather_kernel(
    agg_ref, dcols_ref, ocols_ref, srows_ref, p_hbm, ad_hbm, ao_hbm,
    gath, left, own_ref, tbl_ref, cols_ref,
    p_ref, ad_ref, mine, stage, ordered, right_t, a_all, dacc, drecv, ctab,
    ssem, rsem, xs_sem, xr_sem, lsem,
):
    me = lax.axis_index("rows")
    x = lax.axis_index("grp")
    core = lax.rem(me, 2)
    y = lax.rem(me // 2, NY)
    z = me // (2 * NY)

    def row_of(zz, yy, cc):
        return (zz * NY + yy) * 2 + cc

    up_z, dn_z = lax.rem(z + 1, NZ), lax.rem(z + NZ - 1, NZ)
    up_y, dn_y = lax.rem(y + 1, NY), lax.rem(y + NY - 1, NY)
    xat = [lax.rem(x + d, 4) for d in range(4)]
    link_to = {
        "z+": (row_of(up_z, y, core), x),
        "z-": (row_of(dn_z, y, core), x),
        "y+": (row_of(z, up_y, core), x),
        "y-": (row_of(z, dn_y, core), x),
        "core": (row_of(z, y, 1 - core), x),
        1: (me, xat[1]),
        2: (me, xat[2]),
        3: (me, xat[3]),
    }
    barrier = pltpu.get_barrier_semaphore()
    for device in link_to.values():
        pl.semaphore_signal(barrier, inc=1, device_id=device, device_id_type=MESH)

    loads = [
        pltpu.make_async_copy(p_hbm, p_ref, lsem.at[1]),
        pltpu.make_async_copy(ao_hbm, a_all.at[0], lsem.at[2]),
        pltpu.make_async_copy(ad_hbm, ad_ref, lsem.at[3]),
    ]
    for load in loads:
        load.start()

    sends = []

    def remote(src, dst, s, r, device):
        return pltpu.make_async_remote_copy(
            src_ref=src, dst_ref=dst, send_sem=s, recv_sem=r, device_id=device, device_id_type=MESH
        )

    half = ao_hbm.shape[0] // 2
    first, second = pl.ds(0, half), pl.ds(half, half)
    a_plan = {
        ("r", 0): (0, 1, first, 1), ("r", 1): (0, 1, second, 1), ("r", 2): (1, 2, first, 1),
        ("l", 1): (0, 3, second, 3), ("l", 0): (0, 3, first, 3), ("l", 2): (3, 2, second, 3),
    }
    a_index = {name: i for i, name in enumerate(a_plan)}

    def a_copy(name, sending):
        src_slot, dst_slot, part, to = a_plan[name]
        dst = a_all.at[dst_slot, part]
        src = (ao_hbm if src_slot == 0 else a_all.at[src_slot]).at[part] if sending else dst
        i = a_index[name]
        return remote(src, dst, xs_sem.at[i], xr_sem.at[i], link_to[to])

    def a_send(name):
        copy = a_copy(name, True)
        copy.start()
        sends.append(copy)

    def c_copy(d):
        return remote(ctab.at[0], ctab.at[d], xs_sem.at[5 + d], xr_sem.at[5 + d], link_to[d])

    rows = p_hbm.shape[0]
    stage[...] = jnp.zeros_like(stage)
    stage[0 : srows_ref.shape[0], 0 : srows_ref.shape[1]] = srows_ref[...].astype(jnp.float32)
    ctab[0, 0 : ocols_ref.shape[0], 0 : ocols_ref.shape[1]] = ocols_ref[...]
    pl.semaphore_wait(barrier, len(link_to))
    for name in (("r", 0), ("l", 1), ("r", 1), ("l", 0)):
        a_send(name)
    loads[0].wait()

    for i in range(rows):
        for a in range(2):
            tile = jnp.where(agg_ref[0, i] == a, p_ref[i, 0], p_ref[i, 1])
            ordered[i, :, a * T : (a + 1) * T] = tile
            flat = tile.T
            for g in range(4):
                right_t[i, g * 64 + a * 32 : g * 64 + a * 32 + 32, :] = flat[g * 32 : (g + 1) * 32]
        mine[i * 64 : (i + 1) * 64, :] = right_t[i, pl.ds(pl.multiple_of(x * 64, 64), 64), :]
    mine[4 * T :, :] = stage[...].astype(mine.dtype)

    plan = flood_plan()
    names = sorted(plan, key=str)
    index = {name: i for i, name in enumerate(names)}

    def block(offset, rows_at):
        dz, dy = offset
        return gath.at[core, lax.rem(z + (NZ - dz), NZ), lax.rem(y + (NY - dy), NY), pl.ds(*rows_at)]

    def f_copy(name, sending):
        link, there, here, part, _ = plan[name]
        at = PARTS[part]
        dst = block(there if sending else here, at)
        src = mine.at[pl.ds(*at)] if sending and there == (0, 0) else dst
        i = index[name]
        return remote(src, dst, ssem.at[i], rsem.at[i], link_to[link])

    started = set()

    rank = flood_rank(plan)

    def start_ready(have):
        for name in sorted(plan, key=rank.get):
            if name not in started and all(a in have for a in plan[name][4]):
                started.add(name)
                copy = f_copy(name, True)
                copy.start()
                sends.append(copy)

    def s_copy(key, sending):
        kind, dz, dy = key
        i = len(names) + SHARES.index(key)
        at = pl.ds(*PARTS[kind])
        plane = gath.at[core if sending else 1 - core, lax.rem(z + (NZ - dz), NZ)]
        ref = plane.at[:, at] if dy is None else plane.at[lax.rem(y + (NY - dy), NY), at]
        return remote(ref, ref, ssem.at[i], rsem.at[i], link_to["core"])

    need = {}
    for kind, dz, dy in SHARES:
        zs = [] if dz == 0 else ([("Z", dz)] if dz != 4 else [("Z", 4, 1), ("Z", 4, -1)])
        parts = {}
        if kind == "z":
            parts = {0: zs, **{d: [("ZY", dz, d)] for d in (1, -1, 2)}}
        elif dz == 0:
            parts = {0: [], 1: [("Y", 1)], -1: [("Y", -1)], 2: [("Y", 2, 1), ("Y", 2, -1)]}
        else:
            parts = {d: [("YZ", dz, d)] for d in (0, 1, -1, 2)}
        need[kind, dz, dy] = sum(parts.values(), []) if dy is None else parts[dy]

    def share(have):
        for key in list(need):
            if all(a in have for a in need[key]):
                copy = s_copy(key, True)
                copy.start()
                sends.append(copy)
                del need[key]

    have = set()
    start_ready(have)
    for d in (1, 2, 3):
        copy = c_copy(d)
        copy.start()
        sends.append(copy)
    keep = pltpu.make_async_copy(mine, gath.at[core, z, y], lsem.at[0])
    keep.start()

    per = ao_hbm.shape[1]

    def transposed_left(tile, i):
        return lax.dot_general(
            tile, ordered[i], (((0,), (0,)), ((), ())), preferred_element_type=jnp.float32
        ).astype(jnp.bfloat16)

    def diag_rows(lo, hi):
        def row(i, _):
            for k in range(per):
                dacc[...] += jnp.dot(
                    right_t[dcols_ref[k, i]],
                    transposed_left(ad_ref[i, k], i),
                    preferred_element_type=jnp.float32,
                )
            return 0

        lax.fori_loop(lo, hi, row, 0)

    def left_rows(slot, part):
        def row(i, _):
            for k in range(per):
                left[slot, i, k] = transposed_left(a_all[slot, i, k], i)
            return 0

        lax.fori_loop(part * half, part * half + half, row, 0)

    def share_of(quarter):
        return pl.ds(pl.multiple_of(quarter * 64, 64), 64)

    def d_copy(d):
        return remote(
            dacc.at[share_of(xat[d])], drecv.at[d - 1], xs_sem.at[8 + d], xr_sem.at[8 + d], link_to[d]
        )

    def send_diag():
        for d in (1, 2, 3):
            copy = d_copy(d)
            copy.start()
            sends.append(copy)

    def a_take(name, then=None):
        a_copy(name, False).wait_recv()
        if then:
            a_send(then)

    def begin():
        dacc[...] = jnp.zeros_like(dacc)
        loads[1].wait()
        loads[2].wait()

    events = [(t, 1, name) for name, t in flood_order(plan).items()]
    steps = [
        (0.0, begin),
        (0.5, lambda: diag_rows(0, 1)),
        (1.4, lambda: diag_rows(1, 2)),
        (2.3, lambda: diag_rows(2, 3)),
        (3.2, lambda: diag_rows(3, 4)),
        (4.1, lambda: diag_rows(4, 5)),
        (5.0, lambda: diag_rows(5, 6)),
        (5.9, lambda: diag_rows(6, 7)),
        (6.8, lambda: diag_rows(7, 8)),
        (7.6, send_diag),
        (11.5, lambda: a_take(("r", 0), ("r", 2))), (11.6, lambda: a_take(("l", 1), ("l", 2))),
        (10.5, lambda: left_rows(0, 0)), (12.0, lambda: left_rows(0, 1)),
        (13.5, lambda: left_rows(1, 0)), (15.0, lambda: left_rows(3, 1)),
        (18.0, lambda: (a_take(("r", 1)), left_rows(1, 1))),
        (19.5, lambda: (a_take(("l", 0)), left_rows(3, 0))),
    ]
    events += [(t, 0, step) for t, step in steps]
    kept = False
    for _, kind, item in sorted(events, key=lambda e: (e[0], e[1], str(e[2]) if e[1] else "")):
        if kind == 0:
            item()
            continue
        f_copy(item, False).wait_recv()
        have.add(item)
        start_ready(have)
        if not kept:
            kept = True
            keep.wait()
        share(have)
    for name, part in ((("r", 2), 0), (("l", 2), 1)):
        a_take(name)
        left_rows(2, part)

    total = dacc[share_of(x), :]
    for d in (1, 2, 3):
        d_copy(d).wait_recv()
        total = total + drecv[d - 1]
        c_copy(d).wait_recv()
    own_ref[...] = total
    cols_ref[...] = ctab[...]

    for key in SHARES:
        s_copy(key, False).wait_recv()
    tail = gath[:, :, :, 4 * T :, :].reshape(2 * NZ * NY * 16, T)
    pick = (lax.broadcasted_iota(jnp.int32, (T, T), 0) == me).astype(jnp.bfloat16)
    spread = jnp.dot(tail, pick, preferred_element_type=jnp.float32).reshape(2 * NZ * NY, 16, T)
    line = lax.broadcasted_iota(jnp.int32, spread.shape, 1) == lax.broadcasted_iota(
        jnp.int32, spread.shape, 2
    )
    tbl_ref[...] = jnp.sum(jnp.where(line, spread, 0.0), axis=1).astype(jnp.int32)

    for copy in sends:
        copy.wait_send()


def gather_all(a_diag, diag_cols, a_offd, offd_cols, prolong, aggregate, send_rows):
    rows, per, _, _ = a_offd.shape
    vmem = pl.BlockSpec(memory_space=pltpu.VMEM)
    smem = pl.BlockSpec(memory_space=pltpu.SMEM)
    hbm = pl.BlockSpec(memory_space=pltpu.HBM)
    copies = len(flood_plan()) + len(SHARES)
    bf16, f32 = jnp.bfloat16, jnp.float32
    return pl.pallas_call(
        gather_kernel,
        in_specs=[smem, smem, vmem, vmem, hbm, hbm, hbm],
        out_specs=[vmem, vmem, vmem, vmem, vmem],
        out_shape=[
            jax.ShapeDtypeStruct((2, NZ, NY, ROWS, T), bf16),
            jax.ShapeDtypeStruct((4, rows, per, T, 2 * T), bf16),
            jax.ShapeDtypeStruct((64, 2 * T), f32),
            jax.ShapeDtypeStruct((2 * NZ * NY, T), jnp.int32),
            jax.ShapeDtypeStruct((4, 8, T), jnp.int32),
        ],
        scratch_shapes=[
            pltpu.VMEM((rows, 2, T, T), bf16),
            pltpu.VMEM((rows, per, T, T), bf16),
            pltpu.VMEM((ROWS, T), bf16),
            pltpu.VMEM((16, T), f32),
            pltpu.VMEM((rows, T, 2 * T), bf16),
            pltpu.VMEM((rows, 2 * T, T), bf16),
            pltpu.VMEM((4, rows, per, T, T), bf16),
            pltpu.VMEM((2 * T, 2 * T), f32),
            pltpu.VMEM((3, 64, 2 * T), f32),
            pltpu.VMEM((4, 8, T), jnp.int32),
            pltpu.SemaphoreType.DMA((copies,)),
            pltpu.SemaphoreType.DMA((copies,)),
            pltpu.SemaphoreType.DMA((12,)),
            pltpu.SemaphoreType.DMA((12,)),
            pltpu.SemaphoreType.DMA((4,)),
        ],
        compiler_params=pltpu.CompilerParams(
            collective_id=0, has_side_effects=True, vmem_limit_bytes=32 << 20
        ),
        name="gather_all",
    )(
        *(
            pltpu.with_memory_space_constraint(item, pltpu.HBM)
            for item in (aggregate.T, diag_cols.T, offd_cols.T, send_rows[0].T, prolong, a_diag, a_offd)
        )
    )


def slot_of(node):
    return lax.rem(node, 2) * (NZ * NY) + node // 2


def offd_kernel(me_ref, tbl_ref, cols_ref, l_ref, gath_ref, d_ref, acc):
    groups, rows, per, _, _ = l_ref.shape
    acc[...] = jnp.zeros_like(acc)

    def row(i, _):
        for t in range(groups * per):
            g, k = t // per, t % per
            col = cols_ref[g, k, i]
            slot = slot_of(col // 4)
            at = pl.multiple_of(tbl_ref[slot, lax.rem(col, 4)] * 64, 64)
            acc[slot] += jnp.dot(
                gath_ref[slot, pl.ds(at, 64), :], l_ref[g, i, k], preferred_element_type=jnp.float32
            )
        return 0

    lax.fori_loop(0, rows, row, 0, unroll=4)
    acc[slot_of(me_ref[0])] = d_ref[...]


def offd_terms(me, table, cols, left, gathered, own):
    vmem = pl.BlockSpec(memory_space=pltpu.VMEM)
    smem = pl.BlockSpec(memory_space=pltpu.SMEM)
    return pl.pallas_call(
        offd_kernel,
        in_specs=[smem, smem, smem, vmem, vmem, vmem],
        out_specs=vmem,
        out_shape=jax.ShapeDtypeStruct((gathered.shape[0], 64, 2 * T), jnp.float32),
        compiler_params=pltpu.CompilerParams(vmem_limit_bytes=32 << 20),
        name="offd_terms",
    )(me, table, cols, left, gathered, own)


def swap_kernel(map_ref, acc, out, src, ssem, rsem, lsem):
    me = lax.axis_index("rows")
    x = lax.axis_index("grp")
    at = [lax.rem(x + d, 4) for d in range(4)]
    barrier = pltpu.get_barrier_semaphore()
    for d in (2, 1, 3):
        pl.semaphore_signal(barrier, inc=1, device_id=(me, at[d]), device_id_type=MESH)
    pairs, quarter = src.shape[1], src.shape[2]
    cuts = [0, 2, 7, 21, 35, pairs]
    chunks = len(cuts) - 1

    def pack(p):
        items = []
        for a in range(CR1):
            for j in range(2):
                gid = map_ref[2 * p + j]
                both = acc[slot_of(gid // CR1), :, a * T : (a + 1) * T]
                items.append(jnp.where(lax.rem(gid, CR1) == 0, both[:32], both[32:]))
        both = jnp.concatenate(items, axis=0).T.astype(src.dtype)
        for g in range(src.shape[0]):
            src[g, p] = both[g * quarter : (g + 1) * quarter]

    def remote(d, c, a, b):
        piece = pl.ds(cuts[c], cuts[c + 1] - cuts[c])
        return pltpu.make_async_remote_copy(
            src_ref=a.at[piece], dst_ref=b.at[piece],
            send_sem=ssem.at[d - 1, c], recv_sem=rsem.at[d - 1, c],
            device_id=(me, at[d]), device_id_type=MESH,
        )

    for c in range(chunks):
        for p in range(cuts[c], cuts[c + 1]):
            pack(p)
        if c == 0:
            pl.semaphore_wait(barrier, 3)
        for d in (2, 1, 3):
            remote(d, c, src.at[at[d]], out.at[x]).start()
    stay = pltpu.make_async_copy(src.at[x], out.at[x], lsem)
    stay.start()
    for c in range(chunks):
        for d in (1, 3, 2):
            came = out.at[at[4 - d]]
            remote(d, c, came, came).wait_recv()
    stay.wait()
    for c in range(chunks):
        for d in (1, 3, 2):
            remote(d, c, src.at[at[d]], out.at[x]).wait_send()


def swap_slices(col_map, sums):
    vmem = pl.BlockSpec(memory_space=pltpu.VMEM)
    shape = (4, col_map.shape[0] // 2, T // 4, T)
    chunks = 5
    return pl.pallas_call(
        swap_kernel,
        in_specs=[pl.BlockSpec(memory_space=pltpu.SMEM), vmem],
        out_specs=vmem,
        out_shape=jax.ShapeDtypeStruct(shape, jnp.bfloat16),
        scratch_shapes=[
            pltpu.VMEM(shape, jnp.bfloat16),
            pltpu.SemaphoreType.DMA((3, chunks)),
            pltpu.SemaphoreType.DMA((3, chunks)),
            pltpu.SemaphoreType.DMA,
        ],
        compiler_params=pltpu.CompilerParams(
            collective_id=1, has_side_effects=True, vmem_limit_bytes=16 << 20
        ),
        name="swap_slices",
    )(col_map, sums)


def place_kernel(x_ref, out_hbm, buf, sem):
    pairs, quarter = x_ref.shape[1], x_ref.shape[2]
    chunks = sem.shape[1]
    step = pairs // chunks

    def copies(n):
        at = pl.ds(2 * step * n, 2 * step)
        return [pltpu.make_async_copy(buf.at[r, at], out_hbm.at[r, at], sem.at[r, n]) for r in range(CR1)]

    row = lax.broadcasted_iota(jnp.int32, (4 * T, 4 * T), 0)
    col = lax.broadcasted_iota(jnp.int32, (4 * T, 4 * T), 1)
    move = (row % 32 == col % 32) & ((row // 32) % 4 == col // T) & (row // T == (col // 32) % 4)
    move = jnp.where(move, 1.0, 0.0).astype(jnp.bfloat16)
    for n in range(chunks):
        at = pl.ds(n * step, step)
        x = jnp.concatenate([x_ref[s, at].reshape(step * quarter, T) for s in range(4)], axis=1)
        o = jnp.dot(x, move, preferred_element_type=jnp.float32).astype(buf.dtype)
        for r in range(CR1):
            for j in range(2):
                piece = o[:, (r * 2 + j) * T : (r * 2 + j + 1) * T].reshape(step, quarter, T)
                for p in range(step):
                    buf[r, 2 * (n * step + p) + j] = piece[p]
        for copy in copies(n):
            copy.start()
    for n in range(chunks):
        for copy in copies(n):
            copy.wait()


def place_slots(arrived):
    groups, pairs, quarter, _ = arrived.shape
    shape = (CR1, 2 * pairs, quarter, T)
    return pl.pallas_call(
        place_kernel,
        in_specs=[pl.BlockSpec(memory_space=pltpu.VMEM)],
        out_specs=pl.BlockSpec(memory_space=pltpu.HBM),
        out_shape=jax.ShapeDtypeStruct(shape, jnp.bfloat16),
        scratch_shapes=[pltpu.VMEM(shape, jnp.bfloat16), pltpu.SemaphoreType.DMA((CR1, 7))],
        compiler_params=pltpu.CompilerParams(vmem_limit_bytes=16 << 20),
        name="place_slots",
    )(arrived)


def per_device(
    a_diag, diag_cols, a_offd, offd_cols, prolong, aggregate, send_rows, ghost_agg, coarse_map
):
    me = lax.axis_index("rows").reshape(1)
    gathered, left, own, table, cols = gather_all(
        a_diag, diag_cols, a_offd, offd_cols, prolong, aggregate, send_rows
    )
    gathered = gathered.reshape(2 * NZ * NY, ROWS, T)
    sums = offd_terms(me, table, cols, left, gathered, own)
    return place_slots(swap_slices(coarse_map[0], sums))


def solution(mesh):
    in_specs = (
        P("rows", "grp", None, None),
        P("rows", "grp"),
        P("rows", "grp", None, None),
        P("rows", "grp"),
        P("rows", None, None, None),
        P("rows", None),
        P("rows", None, None),
        P("rows", None, None, None),
        P("rows", None),
    )
    out_specs = P("rows", None, "grp", None)
    return jax.shard_map(
        per_device, mesh=mesh, in_specs=in_specs, out_specs=out_specs, check_vma=False
    )
```

```python
import functools

import jax
import jax.numpy as jnp
from jax import lax
from jax.experimental import pallas as pl
from jax.experimental.pallas import tpu as pltpu
from jax.sharding import PartitionSpec as P

CR1 = 2
T = 128


ROWS = 528
ZR = 288
NZ, NY = 8, 4
MESH = pl.DeviceIdType.MESH
PARTS = {"z": (0, ZR), "za": (0, ZR // 2), "zb": (ZR // 2, ZR // 2),
         "y": (ZR, ROWS - ZR), "ya": (ZR, 112), "yb": (ZR + 112, ROWS - ZR - 112)}
DZ = (0, 1, -1, 2, -2, 3, -3, 4)
LATE_UP = (0, 1, 2, 3)
SHARES = [
    (kind, dz, dy)
    for dz in DZ
    for kind in ("z", "y")
    for dy in ((None,) if abs(dz) < 3 else (0, 1, -1, 2))
]


def flood_plan():
    plan = {}

    def add(name, link, there, here, part, after):
        plan[name] = (link, there, here, part, tuple(after))

    for sign, link in ((1, "z+"), (-1, "z-")):
        for d in range(1, 5):
            part = "z" if d < 4 else ("za" if sign == 1 else "zb")
            after = [] if d == 1 else [("Z", sign * (d - 1))]
            here = sign * d if d < 4 else 4
            name = ("Z", here) if d < 4 else ("Z", 4, sign)
            add(name, link, (sign * (d - 1), 0), (here, 0), part, after)
    for e in DZ:
        have = [] if e == 0 else ([("Z", e)] if e != 4 else [("Z", 4, 1), ("Z", 4, -1)])
        for sign, link in ((1, "y+"), (-1, "y-")):
            add(("ZY", e, sign), link, (e, 0), (e, sign), "z", have)
        sign = 1 if e in LATE_UP else -1
        add(("ZY", e, 2), "y+" if sign == 1 else "y-", (e, sign), (e, 2), "z", [("ZY", e, sign)])
    for sign, link in ((1, "y+"), (-1, "y-")):
        add(("Y", sign), link, (0, 0), (0, sign), "y", [])
        add(("Y", 2, sign), link, (0, sign), (0, 2), "ya" if sign == 1 else "yb", [("Y", sign)])
    for sign, link in ((1, "z+"), (-1, "z-")):
        for d in range(1, 5):
            for dy in (0, 1, -1, 2):
                if d == 4 and (dy in (0, 1)) != (sign == 1):
                    continue
                if d > 1:
                    after = [("YZ", sign * (d - 1), dy)]
                elif dy == 0:
                    after = []
                else:
                    after = [("Y", dy)] if dy != 2 else [("Y", 2, 1), ("Y", 2, -1)]
                here = sign * d if d < 4 else 4
                add(("YZ", here, dy), link, (sign * (d - 1), dy), (here, dy), "y", after)
    return plan


def flood_rank(plan):
    kids = {}
    for name, item in plan.items():
        for a in item[4]:
            kids.setdefault(a, []).append(name)
    memo = {}

    def depth(name):
        if name not in memo:
            memo[name] = 1 + max([depth(k) for k in kids.get(name, [])], default=0)
        return memo[name]

    kind = {"Y": 0, "Z": 1, "YZ": 2, "ZY": 3}
    return {n: (-depth(n), kind[n[0]], abs(n[1]), str(n)) for n in plan}


def flood_order(plan, latency=2.5, rate=49e3):
    rank = flood_rank(plan)
    free = {}
    arrive, waiting = {}, dict(plan)
    while waiting:
        best = None
        for name, (link, _, _, part, after) in waiting.items():
            if any(a not in arrive for a in after):
                continue
            start = max([arrive[a] for a in after] + [free.get(link, 0.0)])
            key = (start,) + rank[name]
            if best is None or key < best[0]:
                best = (key, name, start, link, PARTS[part][1] * 256 / rate)
        _, name, start, link, took = best
        free[link] = start + took
        arrive[name] = start + took + latency
        del waiting[name]
    return arrive


def gather_kernel(
    agg_ref, dcols_ref, ocols_ref, srows_ref, p_hbm, ad_hbm, ao_hbm,
    gath, left, own_ref, tbl_ref, cols_ref,
    p_ref, ad_ref, mine, stage, ordered, right_t, a_all, dacc, drecv, ctab,
    ssem, rsem, xs_sem, xr_sem, lsem,
):
    me = lax.axis_index("rows")
    x = lax.axis_index("grp")
    core = lax.rem(me, 2)
    y = lax.rem(me // 2, NY)
    z = me // (2 * NY)

    def row_of(zz, yy, cc):
        return (zz * NY + yy) * 2 + cc

    up_z, dn_z = lax.rem(z + 1, NZ), lax.rem(z + NZ - 1, NZ)
    up_y, dn_y = lax.rem(y + 1, NY), lax.rem(y + NY - 1, NY)
    xat = [lax.rem(x + d, 4) for d in range(4)]
    link_to = {
        "z+": (row_of(up_z, y, core), x),
        "z-": (row_of(dn_z, y, core), x),
        "y+": (row_of(z, up_y, core), x),
        "y-": (row_of(z, dn_y, core), x),
        "core": (row_of(z, y, 1 - core), x),
        1: (me, xat[1]),
        2: (me, xat[2]),
        3: (me, xat[3]),
    }
    barrier = pltpu.get_barrier_semaphore()
    for device in link_to.values():
        pl.semaphore_signal(barrier, inc=1, device_id=device, device_id_type=MESH)

    loads = [
        pltpu.make_async_copy(p_hbm, p_ref, lsem.at[1]),
        pltpu.make_async_copy(ao_hbm, a_all.at[0], lsem.at[2]),
        pltpu.make_async_copy(ad_hbm, ad_ref, lsem.at[3]),
    ]
    for load in loads:
        load.start()

    sends = []

    def remote(src, dst, s, r, device):
        return pltpu.make_async_remote_copy(
            src_ref=src, dst_ref=dst, send_sem=s, recv_sem=r, device_id=device, device_id_type=MESH
        )

    half = ao_hbm.shape[0] // 2
    first, second = pl.ds(0, half), pl.ds(half, half)
    a_plan = {
        ("r", 0): (0, 1, first, 1), ("r", 1): (0, 1, second, 1), ("r", 2): (1, 2, first, 1),
        ("l", 1): (0, 3, second, 3), ("l", 0): (0, 3, first, 3), ("l", 2): (3, 2, second, 3),
    }
    a_index = {name: i for i, name in enumerate(a_plan)}

    def a_copy(name, sending):
        src_slot, dst_slot, part, to = a_plan[name]
        dst = a_all.at[dst_slot, part]
        src = (ao_hbm if src_slot == 0 else a_all.at[src_slot]).at[part] if sending else dst
        i = a_index[name]
        return remote(src, dst, xs_sem.at[i], xr_sem.at[i], link_to[to])

    def a_send(name):
        copy = a_copy(name, True)
        copy.start()
        sends.append(copy)

    def c_copy(d):
        return remote(ctab.at[0], ctab.at[d], xs_sem.at[5 + d], xr_sem.at[5 + d], link_to[d])

    rows = p_hbm.shape[0]
    stage[...] = jnp.zeros_like(stage)
    stage[0 : srows_ref.shape[0], 0 : srows_ref.shape[1]] = srows_ref[...].astype(jnp.float32)
    ctab[0, 0 : ocols_ref.shape[0], 0 : ocols_ref.shape[1]] = ocols_ref[...]
    pl.semaphore_wait(barrier, len(link_to))
    for name in (("r", 0), ("l", 1), ("r", 1), ("l", 0)):
        a_send(name)
    loads[0].wait()

    for i in range(rows):
        for a in range(2):
            tile = jnp.where(agg_ref[0, i] == a, p_ref[i, 0], p_ref[i, 1])
            ordered[i, :, a * T : (a + 1) * T] = tile
            flat = tile.T
            for g in range(4):
                right_t[i, g * 64 + a * 32 : g * 64 + a * 32 + 32, :] = flat[g * 32 : (g + 1) * 32]
        mine[i * 64 : (i + 1) * 64, :] = right_t[i, pl.ds(pl.multiple_of(x * 64, 64), 64), :]
    mine[4 * T :, :] = stage[...].astype(mine.dtype)

    plan = flood_plan()
    names = sorted(plan, key=str)
    index = {name: i for i, name in enumerate(names)}

    def block(offset, rows_at):
        dz, dy = offset
        return gath.at[core, lax.rem(z + (NZ - dz), NZ), lax.rem(y + (NY - dy), NY), pl.ds(*rows_at)]

    def f_copy(name, sending):
        link, there, here, part, _ = plan[name]
        at = PARTS[part]
        dst = block(there if sending else here, at)
        src = mine.at[pl.ds(*at)] if sending and there == (0, 0) else dst
        i = index[name]
        return remote(src, dst, ssem.at[i], rsem.at[i], link_to[link])

    started = set()

    rank = flood_rank(plan)

    def start_ready(have):
        for name in sorted(plan, key=rank.get):
            if name not in started and all(a in have for a in plan[name][4]):
                started.add(name)
                copy = f_copy(name, True)
                copy.start()
                sends.append(copy)

    def s_copy(key, sending):
        kind, dz, dy = key
        i = len(names) + SHARES.index(key)
        at = pl.ds(*PARTS[kind])
        plane = gath.at[core if sending else 1 - core, lax.rem(z + (NZ - dz), NZ)]
        ref = plane.at[:, at] if dy is None else plane.at[lax.rem(y + (NY - dy), NY), at]
        return remote(ref, ref, ssem.at[i], rsem.at[i], link_to["core"])

    need = {}
    for kind, dz, dy in SHARES:
        zs = [] if dz == 0 else ([("Z", dz)] if dz != 4 else [("Z", 4, 1), ("Z", 4, -1)])
        parts = {}
        if kind == "z":
            parts = {0: zs, **{d: [("ZY", dz, d)] for d in (1, -1, 2)}}
        elif dz == 0:
            parts = {0: [], 1: [("Y", 1)], -1: [("Y", -1)], 2: [("Y", 2, 1), ("Y", 2, -1)]}
        else:
            parts = {d: [("YZ", dz, d)] for d in (0, 1, -1, 2)}
        need[kind, dz, dy] = sum(parts.values(), []) if dy is None else parts[dy]

    def share(have):
        for key in list(need):
            if all(a in have for a in need[key]):
                copy = s_copy(key, True)
                copy.start()
                sends.append(copy)
                del need[key]

    have = set()
    start_ready(have)
    for d in (1, 2, 3):
        copy = c_copy(d)
        copy.start()
        sends.append(copy)
    keep = pltpu.make_async_copy(mine, gath.at[core, z, y], lsem.at[0])
    keep.start()

    per = ao_hbm.shape[1]

    def transposed_left(tile, i):
        return lax.dot_general(
            tile, ordered[i], (((0,), (0,)), ((), ())), preferred_element_type=jnp.float32
        ).astype(jnp.bfloat16)

    def diag_rows(lo, hi):
        def row(i, _):
            for k in range(per):
                dacc[...] += jnp.dot(
                    right_t[dcols_ref[k, i]],
                    transposed_left(ad_ref[i, k], i),
                    preferred_element_type=jnp.float32,
                )
            return 0

        lax.fori_loop(lo, hi, row, 0)

    def left_rows(slot, part):
        def row(i, _):
            for k in range(per):
                left[slot, i, k] = transposed_left(a_all[slot, i, k], i)
            return 0

        lax.fori_loop(part * half, part * half + half, row, 0)

    def share_of(quarter):
        return pl.ds(pl.multiple_of(quarter * 64, 64), 64)

    def d_copy(d):
        return remote(
            dacc.at[share_of(xat[d])], drecv.at[d - 1], xs_sem.at[8 + d], xr_sem.at[8 + d], link_to[d]
        )

    def send_diag():
        for d in (1, 2, 3):
            copy = d_copy(d)
            copy.start()
            sends.append(copy)

    def a_take(name, then=None):
        a_copy(name, False).wait_recv()
        if then:
            a_send(then)

    def begin():
        dacc[...] = jnp.zeros_like(dacc)
        loads[1].wait()
        loads[2].wait()

    events = [(t, 1, name) for name, t in flood_order(plan).items()]
    steps = [
        (0.0, begin),
        (0.5, lambda: diag_rows(0, 1)),
        (1.4, lambda: diag_rows(1, 2)),
        (2.3, lambda: diag_rows(2, 3)),
        (3.2, lambda: diag_rows(3, 4)),
        (4.1, lambda: diag_rows(4, 5)),
        (5.0, lambda: diag_rows(5, 6)),
        (5.9, lambda: diag_rows(6, 7)),
        (6.8, lambda: diag_rows(7, 8)),
        (7.6, send_diag),
        (11.5, lambda: a_take(("r", 0), ("r", 2))), (11.6, lambda: a_take(("l", 1), ("l", 2))),
        (10.5, lambda: left_rows(0, 0)), (12.0, lambda: left_rows(0, 1)),
        (13.5, lambda: left_rows(1, 0)), (15.0, lambda: left_rows(3, 1)),
        (18.0, lambda: (a_take(("r", 1)), left_rows(1, 1))),
        (19.5, lambda: (a_take(("l", 0)), left_rows(3, 0))),
    ]
    events += [(t, 0, step) for t, step in steps]
    kept = False
    for _, kind, item in sorted(events, key=lambda e: (e[0], e[1], str(e[2]) if e[1] else "")):
        if kind == 0:
            item()
            continue
        f_copy(item, False).wait_recv()
        have.add(item)
        start_ready(have)
        if not kept:
            kept = True
            keep.wait()
        share(have)
    for name, part in ((("r", 2), 0), (("l", 2), 1)):
        a_take(name)
        left_rows(2, part)

    total = dacc[share_of(x), :]
    for d in (1, 2, 3):
        d_copy(d).wait_recv()
        total = total + drecv[d - 1]
        c_copy(d).wait_recv()
    own_ref[...] = total
    cols_ref[...] = ctab[...]

    for key in SHARES:
        s_copy(key, False).wait_recv()
    tail = gath[:, :, :, 4 * T :, :].reshape(2 * NZ * NY * 16, T)
    pick = (lax.broadcasted_iota(jnp.int32, (T, T), 0) == me).astype(jnp.bfloat16)
    spread = jnp.dot(tail, pick, preferred_element_type=jnp.float32).reshape(2 * NZ * NY, 16, T)
    line = lax.broadcasted_iota(jnp.int32, spread.shape, 1) == lax.broadcasted_iota(
        jnp.int32, spread.shape, 2
    )
    tbl_ref[...] = jnp.sum(jnp.where(line, spread, 0.0), axis=1).astype(jnp.int32)

    for copy in sends:
        copy.wait_send()


def gather_all(a_diag, diag_cols, a_offd, offd_cols, prolong, aggregate, send_rows):
    rows, per, _, _ = a_offd.shape
    vmem = pl.BlockSpec(memory_space=pltpu.VMEM)
    smem = pl.BlockSpec(memory_space=pltpu.SMEM)
    hbm = pl.BlockSpec(memory_space=pltpu.HBM)
    copies = len(flood_plan()) + len(SHARES)
    bf16, f32 = jnp.bfloat16, jnp.float32
    return pl.pallas_call(
        gather_kernel,
        in_specs=[smem, smem, vmem, vmem, hbm, hbm, hbm],
        out_specs=[vmem, vmem, vmem, vmem, vmem],
        out_shape=[
            jax.ShapeDtypeStruct((2, NZ, NY, ROWS, T), bf16),
            jax.ShapeDtypeStruct((4, rows, per, T, 2 * T), bf16),
            jax.ShapeDtypeStruct((64, 2 * T), f32),
            jax.ShapeDtypeStruct((2 * NZ * NY, T), jnp.int32),
            jax.ShapeDtypeStruct((4, 8, T), jnp.int32),
        ],
        scratch_shapes=[
            pltpu.VMEM((rows, 2, T, T), bf16),
            pltpu.VMEM((rows, per, T, T), bf16),
            pltpu.VMEM((ROWS, T), bf16),
            pltpu.VMEM((16, T), f32),
            pltpu.VMEM((rows, T, 2 * T), bf16),
            pltpu.VMEM((rows, 2 * T, T), bf16),
            pltpu.VMEM((4, rows, per, T, T), bf16),
            pltpu.VMEM((2 * T, 2 * T), f32),
            pltpu.VMEM((3, 64, 2 * T), f32),
            pltpu.VMEM((4, 8, T), jnp.int32),
            pltpu.SemaphoreType.DMA((copies,)),
            pltpu.SemaphoreType.DMA((copies,)),
            pltpu.SemaphoreType.DMA((12,)),
            pltpu.SemaphoreType.DMA((12,)),
            pltpu.SemaphoreType.DMA((4,)),
        ],
        compiler_params=pltpu.CompilerParams(
            collective_id=0, has_side_effects=True, vmem_limit_bytes=32 << 20
        ),
        name="gather_all",
    )(
        *(
            pltpu.with_memory_space_constraint(item, pltpu.HBM)
            for item in (aggregate.T, diag_cols.T, offd_cols.T, send_rows[0].T, prolong, a_diag, a_offd)
        )
    )


def slot_of(node):
    return lax.rem(node, 2) * (NZ * NY) + node // 2


def offd_kernel(me_ref, tbl_ref, cols_ref, l_ref, gath_ref, d_ref, acc):
    groups, rows, per, _, _ = l_ref.shape
    acc[...] = jnp.zeros_like(acc)

    def row(i, _):
        for t in range(groups * per):
            g, k = t // per, t % per
            col = cols_ref[g, k, i]
            slot = slot_of(col // 4)
            at = pl.multiple_of(tbl_ref[slot, lax.rem(col, 4)] * 64, 64)
            acc[slot] += jnp.dot(
                gath_ref[slot, pl.ds(at, 64), :], l_ref[g, i, k], preferred_element_type=jnp.float32
            )
        return 0

    lax.fori_loop(0, rows, row, 0, unroll=8)
    acc[slot_of(me_ref[0])] = d_ref[...]


def offd_terms(me, table, cols, left, gathered, own):
    vmem = pl.BlockSpec(memory_space=pltpu.VMEM)
    smem = pl.BlockSpec(memory_space=pltpu.SMEM)
    return pl.pallas_call(
        offd_kernel,
        in_specs=[smem, smem, smem, vmem, vmem, vmem],
        out_specs=vmem,
        out_shape=jax.ShapeDtypeStruct((gathered.shape[0], 64, 2 * T), jnp.float32),
        compiler_params=pltpu.CompilerParams(vmem_limit_bytes=32 << 20),
        name="offd_terms",
    )(me, table, cols, left, gathered, own)


def swap_kernel(map_ref, acc, out, src, ssem, rsem, lsem):
    me = lax.axis_index("rows")
    x = lax.axis_index("grp")
    at = [lax.rem(x + d, 4) for d in range(4)]
    barrier = pltpu.get_barrier_semaphore()
    for d in (2, 1, 3):
        pl.semaphore_signal(barrier, inc=1, device_id=(me, at[d]), device_id_type=MESH)
    pairs, quarter = src.shape[1], src.shape[2]
    cuts = [0, 2, 7, 21, 35, pairs]
    chunks = len(cuts) - 1

    def pack(p):
        items = []
        for a in range(CR1):
            for j in range(2):
                gid = map_ref[2 * p + j]
                both = acc[slot_of(gid // CR1), :, a * T : (a + 1) * T]
                items.append(jnp.where(lax.rem(gid, CR1) == 0, both[:32], both[32:]))
        both = jnp.concatenate(items, axis=0).T.astype(src.dtype)
        for g in range(src.shape[0]):
            src[g, p] = both[g * quarter : (g + 1) * quarter]

    def remote(d, c, a, b):
        piece = pl.ds(cuts[c], cuts[c + 1] - cuts[c])
        return pltpu.make_async_remote_copy(
            src_ref=a.at[piece], dst_ref=b.at[piece],
            send_sem=ssem.at[d - 1, c], recv_sem=rsem.at[d - 1, c],
            device_id=(me, at[d]), device_id_type=MESH,
        )

    for c in range(chunks):
        for p in range(cuts[c], cuts[c + 1]):
            pack(p)
        if c == 0:
            pl.semaphore_wait(barrier, 3)
        for d in (2, 1, 3):
            remote(d, c, src.at[at[d]], out.at[x]).start()
    stay = pltpu.make_async_copy(src.at[x], out.at[x], lsem)
    stay.start()
    for c in range(chunks):
        for d in (1, 3, 2):
            came = out.at[at[4 - d]]
            remote(d, c, came, came).wait_recv()
    stay.wait()
    for c in range(chunks):
        for d in (1, 3, 2):
            remote(d, c, src.at[at[d]], out.at[x]).wait_send()


def swap_slices(col_map, sums):
    vmem = pl.BlockSpec(memory_space=pltpu.VMEM)
    shape = (4, col_map.shape[0] // 2, T // 4, T)
    chunks = 5
    return pl.pallas_call(
        swap_kernel,
        in_specs=[pl.BlockSpec(memory_space=pltpu.SMEM), vmem],
        out_specs=vmem,
        out_shape=jax.ShapeDtypeStruct(shape, jnp.bfloat16),
        scratch_shapes=[
            pltpu.VMEM(shape, jnp.bfloat16),
            pltpu.SemaphoreType.DMA((3, chunks)),
            pltpu.SemaphoreType.DMA((3, chunks)),
            pltpu.SemaphoreType.DMA,
        ],
        compiler_params=pltpu.CompilerParams(
            collective_id=1, has_side_effects=True, vmem_limit_bytes=16 << 20
        ),
        name="swap_slices",
    )(col_map, sums)


def place_kernel(x_ref, out_hbm, buf, sem):
    pairs, quarter = x_ref.shape[1], x_ref.shape[2]
    chunks = sem.shape[1]
    step = pairs // chunks

    def copies(n):
        at = pl.ds(2 * step * n, 2 * step)
        return [pltpu.make_async_copy(buf.at[r, at], out_hbm.at[r, at], sem.at[r, n]) for r in range(CR1)]

    row = lax.broadcasted_iota(jnp.int32, (4 * T, 4 * T), 0)
    col = lax.broadcasted_iota(jnp.int32, (4 * T, 4 * T), 1)
    move = (row % 32 == col % 32) & ((row // 32) % 4 == col // T) & (row // T == (col // 32) % 4)
    move = jnp.where(move, 1.0, 0.0).astype(jnp.bfloat16)
    for n in range(chunks):
        at = pl.ds(n * step, step)
        x = jnp.concatenate([x_ref[s, at].reshape(step * quarter, T) for s in range(4)], axis=1)
        o = jnp.dot(x, move, preferred_element_type=jnp.float32).astype(buf.dtype)
        for r in range(CR1):
            for j in range(2):
                piece = o[:, (r * 2 + j) * T : (r * 2 + j + 1) * T].reshape(step, quarter, T)
                for p in range(step):
                    buf[r, 2 * (n * step + p) + j] = piece[p]
        for copy in copies(n):
            copy.start()
    for n in range(chunks):
        for copy in copies(n):
            copy.wait()


def place_slots(arrived):
    groups, pairs, quarter, _ = arrived.shape
    shape = (CR1, 2 * pairs, quarter, T)
    return pl.pallas_call(
        place_kernel,
        in_specs=[pl.BlockSpec(memory_space=pltpu.VMEM)],
        out_specs=pl.BlockSpec(memory_space=pltpu.HBM),
        out_shape=jax.ShapeDtypeStruct(shape, jnp.bfloat16),
        scratch_shapes=[pltpu.VMEM(shape, jnp.bfloat16), pltpu.SemaphoreType.DMA((CR1, 7))],
        compiler_params=pltpu.CompilerParams(vmem_limit_bytes=16 << 20),
        name="place_slots",
    )(arrived)


def per_device(
    a_diag, diag_cols, a_offd, offd_cols, prolong, aggregate, send_rows, ghost_agg, coarse_map
):
    me = lax.axis_index("rows").reshape(1)
    gathered, left, own, table, cols = gather_all(
        a_diag, diag_cols, a_offd, offd_cols, prolong, aggregate, send_rows
    )
    gathered = gathered.reshape(2 * NZ * NY, ROWS, T)
    sums = offd_terms(me, table, cols, left, gathered, own)
    return place_slots(swap_slices(coarse_map[0], sums))


def solution(mesh):
    in_specs = (
        P("rows", "grp", None, None),
        P("rows", "grp"),
        P("rows", "grp", None, None),
        P("rows", "grp"),
        P("rows", None, None, None),
        P("rows", None),
        P("rows", None, None),
        P("rows", None, None, None),
        P("rows", None),
    )
    out_specs = P("rows", None, "grp", None)
    return jax.shard_map(
        per_device, mesh=mesh, in_specs=in_specs, out_specs=out_specs, check_vma=False
    )
```
